256 devices in a mesh: row: 2 (over core), span: 32 (over z_lo, y, x), pitch: 4 (over z_hi).
Axes of the slice: x: 4, y: 4, z: 8 (z_hi: 4, z_lo: 2; z = z_hi * 2 + z_lo), core: 2. Of those that a mesh axis runs over, the one named last changes fastest.
Arguments:
- adjoint: float32 [2, 6, 128, 32, 128], P('row', None, 'span', 'pitch'), may hold values from -6 to 6
- source: float32 [2, 6, 128, 32, 128], P('row', None, 'span', 'pitch'), may hold values from -6 to 6
- pseudo_step: float32 [2, 128, 32, 128], P('row', 'span', 'pitch'), may hold values from 0.05 to 0.12
- jac_blocks: bfloat16 [2, 7, 6, 6, 128, 32, 128], P('row', None, None, None, 'span', 'pitch'), as said below
- band_map: int32 [2, 128], replicated, may hold values from 0 to 31, never falling along the last dimension, each value on 1 to 8 neighbouring positions
- face_cell: int32 [2, 32, 4, 128], P('row', 'span', 'pitch'), may hold values from 0 to 4095
- face_owner: int32 [2, 32, 4, 128], P('row', 'span', 'pitch'), may hold values from 0 to 16383
- face_weight: float32 [2, 32, 4, 18, 128], P('row', 'span', 'pitch'), may hold values from -6 to 6
Outputs:
- adjoint_out: float32 [2, 6, 128, 32, 128], P('row', None, 'span', 'pitch')
- sensitivity: float32 [2, 3, 16384], P('row', None, ('span', 'pitch'))
The draws below stay inside these ranges and needn't reach their ends.
Inputs may be any that keep to these rules, and one draw needn't show every extreme that they name: `band_map`: in each row the span bands never fall with span and every band 0 to 31 holds 1 to 8 span cells. `jac_blocks`: the centre block of each cell is diagonally dominant.
All inputs are finite; a program needn't handle non-finite values.
Results may differ from the reference program's by a relative error of at most 0.0003.
Values sent between devices are 32-bit elements; how exact they have to be, the bound alone decides.
No kernel may reach another device: no remote copies, remote signals or barrier semaphores. Data moves between devices by JAX's collectives and lax.ppermute only.
A program may use at most 64 MiB of HBM per device.

```python
import math
import jax
import jax.numpy as jnp
import numpy as np
from jax import lax

CS = 4
CP = 8
NA = 128
NVAR = 6
ITERS = 2
F_DEV = 128
NS = 128
NP = 32
NB = 32
NODES = 16384
N_SPAN = 32
N_PITCH = 4


def draw_jac_blocks(key, part):
    shape = (2, 7, NVAR, NVAR, NS, NP, NA)
    base = jax.random.uniform(key, shape, jnp.float32, -0.12, 0.12)
    stencil = lax.broadcasted_iota(jnp.int32, shape, 1)
    output_var = lax.broadcasted_iota(jnp.int32, shape, 2)
    input_var = lax.broadcasted_iota(jnp.int32, shape, 3)
    centre = (stencil == 0) & (output_var == input_var)
    return jnp.where(centre, base * 4.0 + 6.0, base).astype(jnp.bfloat16)


def touch_ends(array, rng, smallest, high):
    longest = array.shape.index(max(array.shape))
    spots = []
    for shift in (0, 1):
        where = [jax.random.randint(jax.random.fold_in(rng, axis), (), 0, length) for axis, length in enumerate(array.shape)]
        where[longest] = (where[longest] + shift) % array.shape[longest]
        spots.append(tuple(where))
    return array.at[spots[0]].set(smallest).at[spots[1]].set(high)


def steps_of(rng, dims, shards, smallest, high):
    factor_of, own = 1.0, jax.random.fold_in(rng, 6)
    for position, shards_of in shards:
        heights = jnp.exp(jax.random.uniform(jax.random.fold_in(own, position), (shards_of,), jnp.float32, smallest / len(shards), high / len(shards)))
        factor_of = factor_of * jnp.repeat(heights, dims[position] // shards_of).reshape([-1 if axis == position else 1 for axis in range(len(dims))])
    return factor_of


def rank_table(count, lean):
    weights = [(1 << 20) // math.isqrt(standing ** lean) + 1 for standing in range(1, count + 1)]
    scale = 1 + sum(weights) // (1 << 30)
    return np.cumsum(np.array([max(1, weight // scale) for weight in weights]))


def ranked_ids(own_key, dims, number_of, slope):
    table = rank_table(number_of, slope)
    lot = jax.random.randint(jax.random.fold_in(own_key, 1), dims, 0, int(table[number_of - 1]))
    standing = jnp.searchsorted(jnp.asarray(table, jnp.int32), lot, side="right")
    return jax.random.permutation(jax.random.fold_in(own_key, 2), number_of)[standing].astype(jnp.int32)


def length_profile(amount, total, most, skew):
    portions = [(1 << 20) // math.isqrt(standing ** skew) + 1 for standing in range(2, amount + 1)]
    spare, given = total - most - (amount - 1), [1] * (amount - 1)
    while spare > 0:
        movable = [i for i in range(amount - 1) if given[i] < most]
        mass, left = sum([portions[i] for i in movable]), spare
        for i in movable:
            addition = min(most - given[i], max(1, left * portions[i] // mass), spare)
            given[i] = given[i] + addition
            spare = spare - addition
    return np.array([most] + given)


def ragged_sizes(stream_key, amount, total, limit, slope):
    if amount == 2:
        one = jax.random.randint(stream_key, (), max(1, total - limit), min(limit, total - 1) + 1)
        return jnp.stack([one, total - one])
    sizes = jnp.asarray(length_profile(amount, total, limit, slope), jnp.int32)
    twos = (amount - 1) // 2
    source_of, receiver = sizes[1:1 + 2 * twos:2], sizes[2:2 + 2 * twos:2]
    slack = jnp.minimum(source_of - 1, limit - receiver)
    passed = jax.random.randint(jax.random.fold_in(stream_key, 1), (twos,), 0, 1 << 20) % (slack + 1)
    sizes = sizes.at[1:1 + 2 * twos:2].set(source_of - passed).at[2:2 + 2 * twos:2].set(receiver + passed)
    return sizes[jax.random.permutation(jax.random.fold_in(stream_key, 2), amount)]


def gaussian(stream_key, extent, deviation, most, pieces=(), held_as=jnp.bfloat16):
    drawn = jax.random.normal(stream_key, extent, jnp.float32) * deviation
    if len(pieces) > 0:
        drawn = steps_of(stream_key, extent, pieces, -0.22, 0.18) * drawn
    return jnp.clip(drawn, min=-most, max=most).astype(held_as)


def setup_inputs(seed: int = 0) -> dict:
    splits = jax.random.split(jax.random.key(seed), 9)
    return {
        "adjoint": gaussian(splits[0], (2, NVAR, NS, NP, NA), 1.0, 6.0, ((0, 2), (2, 32), (3, 4)), jnp.float32),
        "source": gaussian(splits[1], (2, NVAR, NS, NP, NA), 1.0, 6.0, ((0, 2), (2, 32), (3, 4)), jnp.float32),
        "pseudo_step": jnp.clip(jnp.exp(math.log(0.12) - 0.8754687 * jax.random.uniform(splits[2], (2, NS, NP, NA), jnp.float32) ** steps_of(splits[2], (2, NS, NP, NA), ((0, 2), (1, 32), (2, 4)), -0.2, 0.2)), 0.05, 0.12),
        "jac_blocks": draw_jac_blocks(jax.random.fold_in(splits[8], 71), 0),
        "band_map": jax.vmap(lambda own: jnp.searchsorted(jnp.cumsum(ragged_sizes(own, NB, NS, 8, 1)), jnp.arange(NS), side="right"))(jax.random.split(splits[4], 2)).reshape((2, NS)).astype(jnp.int32),
        "face_cell": touch_ends(jax.random.randint(splits[5], (2, N_SPAN, N_PITCH, F_DEV), 0, CS * CP * NA), jax.random.fold_in(splits[5], 1), 0, (CS * CP * NA) - 1).astype(jnp.int32),
        "face_owner": touch_ends(ranked_ids(splits[6], (2, N_SPAN, N_PITCH, F_DEV), NODES, 2), jax.random.fold_in(splits[6], 3), 0, NODES - 1).astype(jnp.int32),
        "face_weight": gaussian(splits[7], (2, N_SPAN, N_PITCH, 3 * NVAR, F_DEV), 1.0, 6.0, ((0, 2), (1, 32), (2, 4)), jnp.float32),
    }


def stencil_fields(field, ghost_lower, ghost_upper):
    zeros_span = jnp.zeros_like(field[:, :1])
    return [field,
            jnp.concatenate([zeros_span, field[:, :-1]], axis=1),
            jnp.concatenate([field[:, 1:], zeros_span], axis=1),
            jnp.roll(field, 1, axis=2),
            jnp.roll(field, -1, axis=2),
            jnp.concatenate([ghost_lower[..., None], field[..., :-1]], axis=3),
            jnp.concatenate([field[..., 1:], ghost_upper[..., None]], axis=3)]


def apply_blocks(blocks, fields):
    summed = jnp.zeros_like(fields[0])
    for stencil in range(7):
        summed = summed + jnp.einsum("cdjpa,djpa->cjpa", blocks[stencil].astype(jnp.float32), fields[stencil], precision=lax.Precision.HIGHEST)
    return summed


def reference(adjoint, source, pseudo_step, jac_blocks, band_map, face_cell, face_owner, face_weight):
    band_count = band_map.shape[1] // 4
    band_ids = jnp.arange(band_count, dtype=jnp.int32)
    members = [(band_map[side][:, None] == band_ids[None, :]).astype(jnp.float32) for side in range(2)]
    counts = [jnp.sum(members[side], axis=0) * adjoint.shape[3] for side in range(2)]
    fields = [adjoint[0], adjoint[1]]
    for sweep in range(ITERS):
        outlet = [fields[0][..., -1], fields[1][..., 0]]
        totals = [jnp.einsum("cjp,jb->cb", outlet[side], members[side], precision=lax.Precision.HIGHEST) for side in range(2)]
        cycles = []
        for side in range(2):
            band_means = totals[1 - side] / counts[1 - side][None, :]
            cycle_values = jnp.dot(band_means, members[side].T, precision=lax.Precision.HIGHEST)
            cycles.append(jnp.broadcast_to(cycle_values[:, :, None], outlet[side].shape))
        zero_cycle = jnp.zeros_like(outlet[0])
        lowers = [zero_cycle, cycles[1]]
        uppers = [cycles[0], zero_cycle]
        updated = []
        for side in range(2):
            image = apply_blocks(jac_blocks[side], stencil_fields(fields[side], lowers[side], uppers[side]))
            updated.append(fields[side] + pseudo_step[side][None] * (source[side] - image))
        fields = updated
    adjoint_out = jnp.stack(fields, axis=0)
    results = []
    for side in range(2):
        block_view = fields[side].reshape(NVAR, N_SPAN, CS, N_PITCH, CP, NA).transpose(1, 3, 0, 2, 4, 5).reshape(N_SPAN, N_PITCH, NVAR, CS * CP * NA)
        face_values = jnp.take_along_axis(block_view, face_cell[side][:, :, None, :], axis=3)
        weights = face_weight[side].reshape(N_SPAN, N_PITCH, 3, NVAR, F_DEV)
        face_terms = jnp.sum(weights * face_values[:, :, None], axis=3)
        flat_terms = face_terms.transpose(2, 0, 1, 3).reshape(3, N_SPAN * N_PITCH * F_DEV)
        owners = face_owner[side].reshape(N_SPAN * N_PITCH * F_DEV)
        results.append(jnp.stack([jax.ops.segment_sum(flat_terms[coord], owners, num_segments=NODES) for coord in range(3)], axis=0))
    return adjoint_out, jnp.stack(results, axis=0)
```

```python
import jax
import jax.numpy as jnp
from jax import lax
from jax.sharding import PartitionSpec as P

ITERS = 2
NODE_DEV = 128


def padded(value, sides, width, wrap):
    for axis, dim in sides:
        devices, length = (lax.axis_size(axis), value.shape[dim])
        up = [(i, (i + 1) % devices) for i in range(devices if wrap else devices - 1)]
        down = [(j, i) for i, j in up]
        last = lax.slice_in_dim(value, length - width, length, axis=dim)
        first = lax.slice_in_dim(value, 0, width, axis=dim)
        before = lax.ppermute(last, axis, up)
        after = lax.ppermute(first, axis, down)
        value = jnp.concatenate([before, value, after], axis=dim)
    return value


def shifted(value, axis, by):
    devices = lax.axis_size(axis)
    return lax.ppermute(value, axis, [(i, (i + by) % devices) for i in range(devices)])


def neighbours(field, cycle_lower, cycle_upper):
    span_padded = padded(field, (("span", 1),), 1, False)
    pitch_padded = padded(field, (("pitch", 2),), 1, True)
    axial_lower = jnp.concatenate([cycle_lower[..., None], field[..., :-1]], axis=3)
    axial_upper = jnp.concatenate([field[..., 1:], cycle_upper[..., None]], axis=3)
    return [
        field,
        span_padded[:, :-2],
        span_padded[:, 2:],
        pitch_padded[:, :, :-2],
        pitch_padded[:, :, 2:],
        axial_lower,
        axial_upper,
    ]


def apply_blocks(blocks, fields):
    summed = jnp.zeros_like(fields[0])
    for stencil in range(7):
        summed = summed + jnp.einsum(
            "cdjpa,djpa->cjpa",
            blocks[stencil].astype(jnp.float32),
            fields[stencil],
            precision=lax.Precision.HIGHEST,
        )
    return summed


def summed_over_row(value):
    devices = lax.axis_size("span") * lax.axis_size("pitch")
    copies = jnp.broadcast_to(value.reshape(1, 1, -1), (devices, 1, value.size))
    received = lax.all_to_all(copies, ("span", "pitch"), 0, 0)
    return jnp.sum(received, axis=(0, 1)).reshape(value.shape)


def mixing_cycles(fields, row_ids, own_locals, other_locals, other_counts):
    outlet = jnp.stack([jnp.where(row_ids[0] == 0, fields[0][..., -1], fields[0][..., 0])], axis=0)
    received = shifted(outlet, "row", 1)[::-1]
    partial_totals = jnp.stack(
        [jnp.einsum("cjp,jb->cb", received[0], other_locals[0], precision=lax.Precision.HIGHEST)],
        axis=0,
    )
    other_list = summed_over_row(partial_totals[0])
    band_means = other_list / other_counts[0][None, :]
    cycle_values = jnp.dot(band_means, own_locals[0].T, precision=lax.Precision.HIGHEST)
    cycle_full = jnp.broadcast_to(cycle_values[:, :, None], outlet[0].shape)
    zero_cycle = jnp.zeros_like(cycle_full)
    cycles = [
        (
            jnp.where(row_ids[0] == 1, cycle_full, zero_cycle),
            jnp.where(row_ids[0] == 0, cycle_full, zero_cycle),
        )
    ]
    return cycles


def on_device(
    adjoint, source, pseudo_step, jac_blocks, band_map, face_cell, face_owner, face_weight
):
    local_rows = adjoint.shape[0]
    first_row = lax.axis_index("row") * local_rows
    row_ids = [first_row + 0]
    span_cells = adjoint.shape[2]
    pitch_cells = adjoint.shape[3]
    band_count = band_map.shape[1] // 4
    band_ids = jnp.arange(band_count, dtype=jnp.int32)
    span_start = lax.axis_index("span") * span_cells
    k = 0
    own_map = lax.dynamic_index_in_dim(band_map, row_ids[k], 0, keepdims=False)
    other_map = lax.dynamic_index_in_dim(band_map, 1 - row_ids[k], 0, keepdims=False)
    own_members = (own_map[:, None] == band_ids[None, :]).astype(jnp.float32)
    other_members = (other_map[:, None] == band_ids[None, :]).astype(jnp.float32)
    own_locals = [lax.dynamic_slice_in_dim(own_members, span_start, span_cells, 0)]
    other_locals = [lax.dynamic_slice_in_dim(other_members, span_start, span_cells, 0)]
    other_counts = [jnp.sum(other_members, axis=0) * (pitch_cells * lax.axis_size("pitch"))]
    fields = [adjoint[0]]
    for sweep in range(ITERS):
        cycles = mixing_cycles(fields, row_ids, own_locals, other_locals, other_counts)
        k = 0
        image = apply_blocks(jac_blocks[k], neighbours(fields[k], cycles[k][0], cycles[k][1]))
        updated = [fields[k] + pseudo_step[k][None] * (source[k] - image)]
        fields = updated
    k = 0
    flat_field = fields[k].reshape(fields[k].shape[0], -1)
    cells = face_cell[k, 0, 0]
    face_values = jnp.take(flat_field, cells, axis=1)
    weights = face_weight[k, 0, 0].reshape(3, fields[k].shape[0], cells.shape[0])
    face_list = jnp.sum(weights * face_values[None], axis=1)
    owner_list = face_owner[k, 0, 0]
    devices = lax.axis_size("span") * lax.axis_size("pitch")
    dense_terms = (
        jnp.zeros((devices, 3, NODE_DEV), jnp.float32)
        .at[owner_list // NODE_DEV, :, owner_list % NODE_DEV]
        .add(face_list.T)
    )
    received = lax.all_to_all(dense_terms, ("span", "pitch"), 0, 0)
    node_values = jnp.sum(received, axis=0)[None]
    return (jnp.stack(fields, axis=0), node_values)


def solution(mesh):
    in_specs = (
        P("row", None, "span", "pitch", None),
        P("row", None, "span", "pitch", None),
        P("row", "span", "pitch", None),
        P("row", None, None, None, "span", "pitch", None),
        P(),
        P("row", "span", "pitch", None),
        P("row", "span", "pitch", None),
        P("row", "span", "pitch", None, None),
    )
    out_specs = (P("row", None, "span", "pitch", None), P("row", None, ("span", "pitch")))
    return jax.shard_map(
        on_device, mesh=mesh, in_specs=in_specs, out_specs=out_specs, check_vma=False
    )
```

```python
import jax
import jax.numpy as jnp
from jax import lax
from jax.experimental import pallas as pl
from jax.experimental.pallas import tpu as pltpu
from jax.sharding import PartitionSpec as P

NVAR = 6
CS = 4
CP = 8
LANES = 128
F32 = jnp.float32
BF16 = jnp.bfloat16
FIRST_AT = 8
WEIGHT_AT = 16
COUNT_AT = 6


def lane_ids(shape):
    return lax.broadcasted_iota(jnp.int32, shape, len(shape) - 1)


def row_ids(shape):
    return lax.broadcasted_iota(jnp.int32, shape, len(shape) - 2)


def split3(x):
    hi = x.astype(BF16)
    rest = x - hi.astype(F32)
    mid = rest.astype(BF16)
    low = (rest - mid.astype(F32)).astype(BF16)
    return hi, mid, low


def dot3(x, onehot, dims):
    parts = [
        lax.dot_general(part, onehot, (dims, ((), ())), preferred_element_type=F32)
        for part in split3(x)
    ]
    return parts[0] + (parts[1] + parts[2])


def fill_stencil(vs, field, up, down, left, right, lower, upper):
    tile = (CP, LANES)
    lane, sub = lane_ids(tile), row_ids(tile)
    for d in range(NVAR):
        for j in range(CS):
            x = field(d, j)
            vs[d, j] = x
            vs[6 + d, j] = field(d, j - 1) if j > 0 else up(d)
            vs[12 + d, j] = field(d, j + 1) if j < CS - 1 else down(d)
            vs[18 + d, j] = jnp.where(
                sub == 0, jnp.broadcast_to(left(d, j), tile), pltpu.roll(x, 1, 0)
            )
            vs[24 + d, j] = jnp.where(
                sub == CP - 1, jnp.broadcast_to(right(d, j), tile), pltpu.roll(x, CP - 1, 0)
            )
            vs[30 + d, j] = jnp.where(lane == 0, lower(d, j), pltpu.roll(x, 1, 1))
            vs[36 + d, j] = jnp.where(lane == LANES - 1, upper(d, j), pltpu.roll(x, LANES - 1, 1))


def image_of(jac_ref, vs, c):
    acc = jnp.zeros((CS, CP, LANES), F32)
    for s in range(7):
        for d in range(NVAR):
            acc = acc + jac_ref[0, s, c, d].astype(F32) * vs[6 * s + d]
    return acc


def first_kernel(
    adj_ref, src_ref, tau_ref, jac_ref, up_ref, down_ref, left_ref, right_ref,
    f1_ref, msg_ref, to_up_ref, to_down_ref, to_left_ref, to_right_ref, vs, rec,
):
    row = lax.axis_index("row")
    outlet = (1 - row) * (LANES - 1)
    ghost = 6 - row
    tile = (CP, LANES)
    zero = jnp.zeros(tile, F32)
    fill_stencil(
        vs,
        lambda d, j: adj_ref[0, d, j],
        lambda d: up_ref[d],
        lambda d: down_ref[d],
        lambda d, j: left_ref[d, j : j + 1],
        lambda d, j: right_ref[d, j : j + 1],
        lambda d, j: zero,
        lambda d, j: zero,
    )
    lane = lane_ids(tile)

    def body(c, carry):
        weights, sums = carry
        f0 = adj_ref[0, c]
        new = f0 + tau_ref[0] * (src_ref[0, c] - image_of(jac_ref, vs, c))
        f1_ref[c] = new
        weights, sums = list(weights), list(sums)
        for j in range(CS):
            for d in range(NVAR):
                at = WEIGHT_AT + 8 * d + c
                moved = pltpu.roll(jac_ref[0, ghost, c, d, j].astype(F32), at + 1 - row, 1)
                weights[j] = jnp.where(lane == at, moved, weights[j])
            sums[j] = jnp.where(lane == c, pltpu.roll(f0[j], c + 1 - row, 1), sums[j])
            at = FIRST_AT + c
            sums[j] = jnp.where(lane == at, pltpu.roll(new[j], at + 1 - row, 1), sums[j])
        return tuple(weights), tuple(sums)

    ones = jnp.where(lane == COUNT_AT, 1.0, 0.0).astype(F32)
    weights, sums = lax.fori_loop(0, NVAR, body, ((zero,) * CS, (ones,) * CS))
    rows = []
    for j in range(CS):
        tau_out = jnp.sum(jnp.where(lane == outlet, tau_ref[0, j], 0.0), axis=1, keepdims=True)
        record = sums[j] + weights[j] * tau_out
        rec[j] = record
        rows.append(jnp.sum(record, axis=0, keepdims=True))
    halves = [
        jnp.broadcast_to(rows[2 * h] + pltpu.roll(rows[2 * h + 1], 64, 1), tile) for h in range(2)
    ]
    packed = jnp.where(row_ids(tile) % 2 == 0, halves[0], halves[1])
    for i in range(msg_ref.shape[0] // CP):
        msg_ref[CP * i : CP * (i + 1)] = packed
    to_up_ref[0:NVAR] = f1_ref[:, 0]
    to_up_ref[NVAR] = rec[0]
    to_down_ref[0:NVAR] = f1_ref[:, CS - 1]
    to_down_ref[NVAR] = rec[CS - 1]
    for c in range(NVAR):
        to_left_ref[c] = f1_ref[c, :, 0, :]
        to_right_ref[c] = f1_ref[c, :, CP - 1, :]
    to_left_ref[NVAR] = rec[:, 0, :]
    to_right_ref[NVAR] = rec[:, CP - 1, :]


def weight_sum(x):
    for by in (32, 16, 8):
        x = x + pltpu.roll(x, LANES - by, 1)
    return x


def spread(values):
    lane = lane_ids(values.shape)
    out = jnp.zeros(values.shape, F32)
    for d in range(NVAR):
        out = jnp.where(
            lane // 8 == d + WEIGHT_AT // 8,
            jnp.broadcast_to(values[:, d : d + 1], values.shape),
            out,
        )
    return out


def second_kernel(
    bands_ref, f1_ref, src_ref, tau_ref, jac_ref, all_ref, ids_ref, up_ref, down_ref, left_ref,
    right_ref, cell_ref, owner_ref, weight_ref, out_ref, dense_ref, vs, field, cycle, edge, side,
):
    row = lax.axis_index("row")
    span = lax.axis_index("span")
    outlet = (1 - row) * (LANES - 1)
    ghost = 6 - row
    tile = (CP, LANES)
    lane = lane_ids(tile)
    last_cell = bands_ref.shape[1] - 1
    wanted = [
        bands_ref[row, jnp.clip(span * CS - 1 + t, 0, last_cell)] for t in range(CS + 2)
    ]
    half = all_ref.shape[0] // 2
    zero = jnp.zeros(tile, F32)

    def gather_bands(base):
        def body(i, sums):
            at = pl.multiple_of(base + i * CP, CP)
            ids, values = ids_ref[pl.ds(at, CP), :], all_ref[pl.ds(at, CP), :]
            return tuple(
                total + jnp.where(ids == band, values, 0.0) for total, band in zip(sums, wanted)
            )

        sums = lax.fori_loop(0, half // CP, body, (zero,) * (CS + 2), unroll=4)
        rows = [jnp.sum(x, axis=0, keepdims=True) for x in sums]
        rows = rows + [rows[-1]] * (CP - len(rows))
        folded = jnp.concatenate(rows, axis=0)
        folded = folded + pltpu.roll(folded, 64, 1)
        return folded, jnp.broadcast_to(folded[:, COUNT_AT : COUNT_AT + 1], tile)

    other, other_count = gather_bands(pl.multiple_of((1 - row) * half, CP))
    mine, my_count = gather_bands(pl.multiple_of(row * half, CP))
    cycle0 = other / other_count
    spread0 = spread(cycle0)
    lost = weight_sum(other * spread(mine / my_count))
    cycle1 = (other - pltpu.roll(lost, LANES - (WEIGHT_AT - FIRST_AT), 1)) / other_count
    at_outlet = lane == outlet

    for j in range(CS):
        for d in range(NVAR):
            cycle[d, j] = jnp.broadcast_to(cycle0[j + 1 : j + 2, d : d + 1], tile)

    def correct(c, carry):
        acc = jnp.zeros((CS, CP, LANES), F32)
        for d in range(NVAR):
            acc = acc + jac_ref[0, ghost, c, d].astype(F32) * cycle[d]
        field[c] = f1_ref[c] - jnp.where(at_outlet[None], tau_ref[0] * acc, 0.0)
        return carry

    lax.fori_loop(0, NVAR, correct, 0)
    for n, (ref, at) in enumerate(((up_ref, 0), (down_ref, CS + 1))):
        moved = weight_sum(ref[NVAR] * spread0[at : at + 1])
        for c in range(NVAR):
            part = jnp.broadcast_to(moved[:, WEIGHT_AT + c : WEIGHT_AT + c + 1], tile)
            edge[n, c] = ref[c] - jnp.where(at_outlet, part, 0.0)
    low = (CS, LANES)
    low_outlet = lane_ids(low) == outlet
    for n, ref in enumerate((left_ref, right_ref)):
        moved = weight_sum(ref[NVAR] * spread0[1 : 1 + CS])
        for c in range(NVAR):
            part = jnp.broadcast_to(moved[:, WEIGHT_AT + c : WEIGHT_AT + c + 1], low)
            side[n, c] = ref[c] - jnp.where(low_outlet, part, 0.0)
    is_upper = jnp.where(row == 0, 1.0, 0.0).astype(F32)

    def cycled(d, j):
        at = FIRST_AT + d
        return jnp.broadcast_to(cycle1[j + 1 : j + 2, at : at + 1], tile)

    fill_stencil(
        vs,
        lambda d, j: field[d, j],
        lambda d: edge[0, d],
        lambda d: edge[1, d],
        lambda d, j: side[0, d, j : j + 1],
        lambda d, j: side[1, d, j : j + 1],
        lambda d, j: cycled(d, j) * (1.0 - is_upper),
        lambda d, j: cycled(d, j) * is_upper,
    )

    def advance(c, carry):
        new = field[c] + tau_ref[0] * (src_ref[0, c] - image_of(jac_ref, vs, c))
        out_ref[0, c] = new
        return carry

    lax.fori_loop(0, NVAR, advance, 0)

    cells = cell_ref[0, 0]
    square = (LANES, LANES)
    axial_pick = (row_ids(square) == cells % LANES).astype(F32).astype(BF16)
    flat = out_ref[0].reshape(NVAR * CS * CP, LANES)
    picked = dot3(flat, axial_pick, ((1,), (0,)))
    here = row_ids((CS * CP, LANES)) == cells // LANES
    terms = [jnp.zeros((1, LANES), F32)] * 3
    for c in range(NVAR):
        block = picked[c * CS * CP : (c + 1) * CS * CP]
        value = jnp.sum(jnp.where(here, block, 0.0), axis=0, keepdims=True)
        for k in range(3):
            at = NVAR * k + c
            terms[k] = terms[k] + weight_ref[0, 0, 0, at : at + 1] * value
    owners = owner_ref[0, 0]
    shape = dense_ref.shape
    line = row_ids(shape)
    device = (line * 43691) >> 17
    coord = line - 3 * device
    value = jnp.where(
        coord == 0,
        jnp.broadcast_to(terms[0], shape),
        jnp.where(coord == 1, jnp.broadcast_to(terms[1], shape), jnp.broadcast_to(terms[2], shape)),
    )
    placed = jnp.where(device == owners // LANES, value, 0.0)
    node_pick = (row_ids(square) == owners % LANES).astype(F32).astype(BF16)
    dense_ref[...] = dot3(placed, node_pick, ((1,), (1,)))


def third_kernel(parts_ref, out_ref):
    folded = jnp.sum(parts_ref[...].reshape(-1, 24, LANES), axis=0)
    coord = row_ids(folded.shape) % 3
    for k in range(3):
        out_ref[0, k : k + 1] = jnp.sum(jnp.where(coord == k, folded, 0.0), axis=0, keepdims=True)


VM = pl.BlockSpec(memory_space=pltpu.VMEM)
SM = pl.BlockSpec(memory_space=pltpu.SMEM)
PARAMS = pltpu.CompilerParams(vmem_limit_bytes=32 * 1024 * 1024)


def exchange(to_up, to_down, to_left, to_right):
    spans, pitches = lax.axis_size("span"), lax.axis_size("pitch")
    rising = [(i, i + 1) for i in range(spans - 1)]
    falling = [(i + 1, i) for i in range(spans - 1)]
    onward = [(i, (i + 1) % pitches) for i in range(pitches)]
    back = [((i + 1) % pitches, i) for i in range(pitches)]
    return (
        lax.ppermute(to_down, "span", rising),
        lax.ppermute(to_up, "span", falling),
        lax.ppermute(to_right, "pitch", onward),
        lax.ppermute(to_left, "pitch", back),
    )


def on_device(
    adjoint, source, pseudo_step, jac_blocks, band_map, face_cell, face_owner, face_weight
):
    rows, spans, pitches = (lax.axis_size(name) for name in ("row", "span", "pitch"))
    devices = rows * spans * pitches
    peers = spans * pitches
    halo = exchange(adjoint[0, :, 0], adjoint[0, :, CS - 1], adjoint[0, :, :, 0], adjoint[0, :, :, CP - 1])
    edge_shape = jax.ShapeDtypeStruct((NVAR + 1, CP, LANES), F32)
    side_shape = jax.ShapeDtypeStruct((NVAR + 1, CS, LANES), F32)
    block = (NVAR, CS, CP, LANES)
    first, record, *sends = pl.pallas_call(
        first_kernel,
        out_shape=(
            jax.ShapeDtypeStruct(block, F32),
            jax.ShapeDtypeStruct((2 * devices, LANES), F32),
            edge_shape, edge_shape, side_shape, side_shape,
        ),
        in_specs=[VM] * 8,
        out_specs=(VM,) * 6,
        scratch_shapes=[
            pltpu.VMEM((7 * NVAR, CS, CP, LANES), F32),
            pltpu.VMEM((CS, CP, LANES), F32),
        ],
        compiler_params=PARAMS,
        name="first_iteration",
    )(adjoint, source, pseudo_step, jac_blocks, *halo)
    records = lax.all_to_all(
        record.reshape(devices, 1, 2 * LANES), ("row", "span", "pitch"), 0, 0
    ).reshape(2 * devices, LANES)
    halo = exchange(*sends)
    ids = jnp.broadcast_to(
        band_map.reshape(rows, spans, 1, CS // 2, 2, 1),
        (rows, spans, pitches, CS // 2, 2, LANES // 2),
    ).reshape(2 * devices, LANES)
    field, dense = pl.pallas_call(
        second_kernel,
        out_shape=(
            jax.ShapeDtypeStruct((1,) + block, F32),
            jax.ShapeDtypeStruct((3 * peers, LANES), F32),
        ),
        in_specs=[SM] + [VM] * 13,
        out_specs=(VM,) * 2,
        scratch_shapes=[
            pltpu.VMEM((7 * NVAR, CS, CP, LANES), F32),
            pltpu.VMEM(block, F32),
            pltpu.VMEM(block, F32),
            pltpu.VMEM((2, NVAR, CP, LANES), F32),
            pltpu.VMEM((2, NVAR, CS, LANES), F32),
        ],
        compiler_params=PARAMS,
        name="second_iteration",
    )(
        band_map, first, source, pseudo_step, jac_blocks, records, ids, *halo,
        face_cell, face_owner, face_weight,
    )
    parts = lax.all_to_all(dense.reshape(peers, 1, 3 * LANES), ("span", "pitch"), 0, 0)
    nodes = pl.pallas_call(
        third_kernel,
        out_shape=jax.ShapeDtypeStruct((1, 3, LANES), F32),
        in_specs=[VM],
        out_specs=VM,
        compiler_params=PARAMS,
        name="node_sums",
    )(parts.reshape(3 * peers, LANES))
    return field, nodes


def solution(mesh):
    in_specs = (
        P("row", None, "span", "pitch", None),
        P("row", None, "span", "pitch", None),
        P("row", "span", "pitch", None),
        P("row", None, None, None, "span", "pitch", None),
        P(),
        P("row", "span", "pitch", None),
        P("row", "span", "pitch", None),
        P("row", "span", "pitch", None, None),
    )
    out_specs = (P("row", None, "span", "pitch", None), P("row", None, ("span", "pitch")))
    return jax.shard_map(
        on_device, mesh=mesh, in_specs=in_specs, out_specs=out_specs, check_vma=False
    )
```

```python
import jax
import jax.numpy as jnp
from jax import lax
from jax.experimental import pallas as pl
from jax.experimental.pallas import tpu as pltpu
from jax.sharding import PartitionSpec as P

NVAR = 6
CS = 4
CP = 8
LANES = 128
F32 = jnp.float32
BF16 = jnp.bfloat16
FIRST_AT = 8
WEIGHT_AT = 16
COUNT_AT = 6


def lane_ids(shape):
    return lax.broadcasted_iota(jnp.int32, shape, len(shape) - 1)


def row_ids(shape):
    return lax.broadcasted_iota(jnp.int32, shape, len(shape) - 2)


def split3(x):
    hi = x.astype(BF16)
    rest = x - hi.astype(F32)
    mid = rest.astype(BF16)
    low = (rest - mid.astype(F32)).astype(BF16)
    return hi, mid, low


def dot3(x, onehot, dims):
    parts = [
        lax.dot_general(part, onehot, (dims, ((), ())), preferred_element_type=F32)
        for part in split3(x)
    ]
    return parts[0] + (parts[1] + parts[2])


def fill_stencil(vs, field, up, down, left, right, lower, upper):
    tile = (CP, LANES)
    lane, sub = lane_ids(tile), row_ids(tile)
    for d in range(NVAR):
        for j in range(CS):
            x = field(d, j)
            vs[d, j] = x
            vs[6 + d, j] = field(d, j - 1) if j > 0 else up(d)
            vs[12 + d, j] = field(d, j + 1) if j < CS - 1 else down(d)
            vs[18 + d, j] = jnp.where(
                sub == 0, jnp.broadcast_to(left(d, j), tile), pltpu.roll(x, 1, 0)
            )
            vs[24 + d, j] = jnp.where(
                sub == CP - 1, jnp.broadcast_to(right(d, j), tile), pltpu.roll(x, CP - 1, 0)
            )
            vs[30 + d, j] = jnp.where(lane == 0, lower(d, j), pltpu.roll(x, 1, 1))
            vs[36 + d, j] = jnp.where(lane == LANES - 1, upper(d, j), pltpu.roll(x, LANES - 1, 1))


def image_of(jac_ref, vs, c):
    acc = jnp.zeros((CS, CP, LANES), F32)
    for s in range(7):
        for d in range(NVAR):
            acc = acc + jac_ref[s, c, d].astype(F32) * vs[6 * s + d]
    return acc


def edges_kernel(adj_ref, up_ref, down_ref, left_ref, right_ref, sems):
    adj = adj_ref.at[0]
    copies = [
        pltpu.make_async_copy(adj.at[:, 0], up_ref, sems.at[0]),
        pltpu.make_async_copy(adj.at[:, CS - 1], down_ref, sems.at[1]),
        pltpu.make_async_copy(adj.at[:, :, 0], left_ref, sems.at[2]),
        pltpu.make_async_copy(adj.at[:, :, CP - 1], right_ref, sems.at[3]),
    ]
    for copy in copies:
        copy.start()
    for copy in copies:
        copy.wait()


def interior_kernel(
    adj_hbm, src_hbm, tau_hbm, jac_hbm, part_ref, rec_ref, jac_ref, src_ref, tau_ref, adj_ref, vs,
    image, sems,
):
    row = lax.axis_index("row")
    outlet = (1 - row) * (LANES - 1)
    ghost = 6 - row
    tile = (CP, LANES)
    zero = jnp.zeros(tile, F32)
    lane = lane_ids(tile)
    load_adj = pltpu.make_async_copy(adj_hbm.at[0], adj_ref, sems.at[0])
    load_jac = [
        pltpu.make_async_copy(jac_hbm.at[0, s], jac_ref.at[s], sems.at[1 + s]) for s in range(7)
    ]
    load_tau = pltpu.make_async_copy(tau_hbm.at[0], tau_ref, sems.at[8])
    load_src = pltpu.make_async_copy(src_hbm.at[0], src_ref, sems.at[9])
    for copy in [load_adj] + load_jac + [load_tau, load_src]:
        copy.start()
    load_adj.wait()
    fill_stencil(
        vs,
        lambda d, j: adj_ref[d, j],
        lambda d: zero,
        lambda d: zero,
        lambda d, j: zero,
        lambda d, j: zero,
        lambda d, j: zero,
        lambda d, j: zero,
    )
    for s in range(7):
        load_jac[s].wait()

        def apply(c, carry):
            acc = jnp.zeros((CS, CP, LANES), F32) if s == 0 else image[c]
            for d in range(NVAR):
                acc = acc + jac_ref[s, c, d].astype(F32) * vs[6 * s + d]
            image[c] = acc
            return carry

        lax.fori_loop(0, NVAR, apply, 0)
    load_tau.wait()
    load_src.wait()

    def finish(c, carry):
        weights, sums = (list(x) for x in carry)
        f0 = adj_ref[c]
        part_ref[c] = f0 + tau_ref[...] * (src_ref[c] - image[c])
        for j in range(CS):
            for d in range(NVAR):
                at = WEIGHT_AT + 8 * d + c
                moved = pltpu.roll(jac_ref[ghost, c, d, j].astype(F32), at + 1 - row, 1)
                weights[j] = jnp.where(lane == at, moved, weights[j])
            sums[j] = jnp.where(lane == c, pltpu.roll(f0[j], c + 1 - row, 1), sums[j])
        return tuple(weights), tuple(sums)

    ones = jnp.where(lane == COUNT_AT, 1.0, 0.0).astype(F32)
    weights, sums = lax.fori_loop(0, NVAR, finish, ((zero,) * CS, (ones,) * CS))
    for j in range(CS):
        tau_out = jnp.sum(jnp.where(lane == outlet, tau_ref[j], 0.0), axis=1, keepdims=True)
        rec_ref[j] = sums[j] + weights[j] * tau_out


def edge_kernel(
    part_ref, rec_in, jac_ref, tau_ref, up_ref, down_ref, left_ref, right_ref,
    f1_ref, msg_ref, to_up_ref, to_down_ref, to_left_ref, to_right_ref, sides, rec,
):
    row = lax.axis_index("row")
    tile = (CP, LANES)
    lane, sub = lane_ids(tile), row_ids(tile)
    for d in range(NVAR):
        for j in range(CS):
            sides[d, j] = jnp.where(
                sub == 0, jnp.broadcast_to(left_ref[d, j : j + 1], tile), 0.0
            )
            sides[NVAR + d, j] = jnp.where(
                sub == CP - 1, jnp.broadcast_to(right_ref[d, j : j + 1], tile), 0.0
            )

    def body(c, sums):
        sums = list(sums)
        acc = jnp.zeros((CS, CP, LANES), F32)
        first = jnp.zeros(tile, F32)
        last = jnp.zeros(tile, F32)
        for d in range(NVAR):
            acc = acc + jac_ref[3, c, d].astype(F32) * sides[d]
            acc = acc + jac_ref[4, c, d].astype(F32) * sides[NVAR + d]
            first = first + jac_ref[1, c, d, 0].astype(F32) * up_ref[d]
            last = last + jac_ref[2, c, d, CS - 1].astype(F32) * down_ref[d]
        at = FIRST_AT + c
        for j in range(CS):
            lost = acc[j]
            if j == 0:
                lost = lost + first
            if j == CS - 1:
                lost = lost + last
            new = part_ref[c, j] - tau_ref[j] * lost
            f1_ref[c, j] = new
            sums[j] = jnp.where(lane == at, pltpu.roll(new, at + 1 - row, 1), sums[j])
        return tuple(sums)

    sums = lax.fori_loop(0, NVAR, body, tuple(rec_in[j] for j in range(CS)))
    rows = []
    for j in range(CS):
        rec[j] = sums[j]
        rows.append(jnp.sum(sums[j], axis=0, keepdims=True))
    halves = [
        jnp.broadcast_to(rows[2 * h] + pltpu.roll(rows[2 * h + 1], 64, 1), tile) for h in range(2)
    ]
    packed = jnp.where(sub % 2 == 0, halves[0], halves[1])
    for i in range(msg_ref.shape[0] // CP):
        msg_ref[CP * i : CP * (i + 1)] = packed
    to_up_ref[0:NVAR] = f1_ref[:, 0]
    to_up_ref[NVAR] = rec[0]
    to_down_ref[0:NVAR] = f1_ref[:, CS - 1]
    to_down_ref[NVAR] = rec[CS - 1]
    for c in range(NVAR):
        to_left_ref[c] = f1_ref[c, :, 0, :]
        to_right_ref[c] = f1_ref[c, :, CP - 1, :]
    to_left_ref[NVAR] = rec[:, 0, :]
    to_right_ref[NVAR] = rec[:, CP - 1, :]


def weight_sum(x):
    for by in (32, 16, 8):
        x = x + pltpu.roll(x, LANES - by, 1)
    return x


def spread(values):
    lane = lane_ids(values.shape)
    out = jnp.zeros(values.shape, F32)
    for d in range(NVAR):
        out = jnp.where(
            lane // 8 == d + WEIGHT_AT // 8,
            jnp.broadcast_to(values[:, d : d + 1], values.shape),
            out,
        )
    return out


def second_kernel(
    bands_ref, f1_ref, src_ref, tau_ref, jac_ref, all_ref, up_ref, down_ref, left_ref, right_ref,
    cell_ref, owner_ref, weight_ref, out_ref, dense_ref, vs, field, cycle, edge, side,
):
    row = lax.axis_index("row")
    span = lax.axis_index("span")
    outlet = (1 - row) * (LANES - 1)
    ghost = 6 - row
    tile = (CP, LANES)
    lane = lane_ids(tile)
    last_cell = bands_ref.shape[1] - 1
    wanted = [
        bands_ref[row, jnp.clip(span * CS - 1 + t, 0, last_cell)] for t in range(CS + 2)
    ]
    half = all_ref.shape[0] // 2
    zero = jnp.zeros(tile, F32)

    second_half = lane >= LANES // 2
    odd = row_ids(tile) % 2 == 1

    def gather_bands(of_row):
        base = of_row * half

        def body(i, sums):
            values = all_ref[pl.ds(pl.multiple_of(base + i * CP, CP), CP), :]
            cells = [bands_ref[of_row, i * CS + j] for j in range(CS)]
            ids = jnp.where(
                odd,
                jnp.where(second_half, cells[3], cells[2]),
                jnp.where(second_half, cells[1], cells[0]),
            )
            return tuple(
                total + jnp.where(ids == band, values, 0.0) for total, band in zip(sums, wanted)
            )

        sums = lax.fori_loop(0, half // CP, body, (zero,) * (CS + 2), unroll=4)
        rows = [jnp.sum(x, axis=0, keepdims=True) for x in sums]
        rows = rows + [rows[-1]] * (CP - len(rows))
        folded = jnp.concatenate(rows, axis=0)
        folded = folded + pltpu.roll(folded, 64, 1)
        return folded, jnp.broadcast_to(folded[:, COUNT_AT : COUNT_AT + 1], tile)

    other, other_count = gather_bands(1 - row)
    mine, my_count = gather_bands(row)
    cycle0 = other / other_count
    spread0 = spread(cycle0)
    lost = weight_sum(other * spread(mine / my_count))
    cycle1 = (other - pltpu.roll(lost, LANES - (WEIGHT_AT - FIRST_AT), 1)) / other_count
    at_outlet = lane == outlet

    for j in range(CS):
        for d in range(NVAR):
            cycle[d, j] = jnp.broadcast_to(cycle0[j + 1 : j + 2, d : d + 1], tile)

    def correct(c, carry):
        acc = jnp.zeros((CS, CP, LANES), F32)
        for d in range(NVAR):
            acc = acc + jac_ref[ghost, c, d].astype(F32) * cycle[d]
        field[c] = f1_ref[c] - jnp.where(at_outlet[None], tau_ref[...] * acc, 0.0)
        return carry

    lax.fori_loop(0, NVAR, correct, 0)
    for n, (ref, at) in enumerate(((up_ref, 0), (down_ref, CS + 1))):
        moved = weight_sum(ref[NVAR] * spread0[at : at + 1])
        for c in range(NVAR):
            part = jnp.broadcast_to(moved[:, WEIGHT_AT + c : WEIGHT_AT + c + 1], tile)
            edge[n, c] = ref[c] - jnp.where(at_outlet, part, 0.0)
    low = (CS, LANES)
    low_outlet = lane_ids(low) == outlet
    for n, ref in enumerate((left_ref, right_ref)):
        moved = weight_sum(ref[NVAR] * spread0[1 : 1 + CS])
        for c in range(NVAR):
            part = jnp.broadcast_to(moved[:, WEIGHT_AT + c : WEIGHT_AT + c + 1], low)
            side[n, c] = ref[c] - jnp.where(low_outlet, part, 0.0)
    is_upper = jnp.where(row == 0, 1.0, 0.0).astype(F32)

    def cycled(d, j):
        at = FIRST_AT + d
        return jnp.broadcast_to(cycle1[j + 1 : j + 2, at : at + 1], tile)

    fill_stencil(
        vs,
        lambda d, j: field[d, j],
        lambda d: edge[0, d],
        lambda d: edge[1, d],
        lambda d, j: side[0, d, j : j + 1],
        lambda d, j: side[1, d, j : j + 1],
        lambda d, j: cycled(d, j) * (1.0 - is_upper),
        lambda d, j: cycled(d, j) * is_upper,
    )

    def advance(c, carry):
        new = field[c] + tau_ref[...] * (src_ref[c] - image_of(jac_ref, vs, c))
        out_ref[0, c] = new
        return carry

    lax.fori_loop(0, NVAR, advance, 0)

    cells = cell_ref[0, 0]
    square = (LANES, LANES)
    axial_pick = (row_ids(square) == cells % LANES).astype(F32).astype(BF16)
    flat = out_ref[0].reshape(NVAR * CS * CP, LANES)
    picked = dot3(flat, axial_pick, ((1,), (0,)))
    here = row_ids((CS * CP, LANES)) == cells // LANES
    terms = [jnp.zeros((1, LANES), F32)] * 3
    for c in range(NVAR):
        block = picked[c * CS * CP : (c + 1) * CS * CP]
        value = jnp.sum(jnp.where(here, block, 0.0), axis=0, keepdims=True)
        for k in range(3):
            at = NVAR * k + c
            terms[k] = terms[k] + weight_ref[0, 0, 0, at : at + 1] * value
    owners = owner_ref[0, 0]
    shape = dense_ref.shape
    line = row_ids(shape)
    device = (line * 43691) >> 17
    coord = line - 3 * device
    value = jnp.where(
        coord == 0,
        jnp.broadcast_to(terms[0], shape),
        jnp.where(coord == 1, jnp.broadcast_to(terms[1], shape), jnp.broadcast_to(terms[2], shape)),
    )
    placed = jnp.where(device == owners // LANES, value, 0.0)
    node_pick = (row_ids(square) == owners % LANES).astype(F32).astype(BF16)
    dense_ref[...] = dot3(placed, node_pick, ((1,), (1,)))


def third_kernel(parts_ref, out_ref):
    folded = jnp.sum(parts_ref[...].reshape(-1, 24, LANES), axis=0)
    coord = row_ids(folded.shape) % 3
    for k in range(3):
        out_ref[k] = jnp.sum(jnp.where(coord == k, folded, 0.0), axis=0, keepdims=True)


VM = pl.BlockSpec(memory_space=pltpu.VMEM)
SM = pl.BlockSpec(memory_space=pltpu.SMEM)
PARAMS = pltpu.CompilerParams(vmem_limit_bytes=32 * 1024 * 1024)


HBM = pl.BlockSpec(memory_space=pltpu.HBM)


def call(kernel, name, outs, in_specs, scratch=(), cost=None):
    outs = [out if isinstance(out[0], tuple) else (out, F32) for out in outs]
    return pl.pallas_call(
        kernel,
        out_shape=tuple(jax.ShapeDtypeStruct(shape, dtype) for shape, dtype in outs),
        in_specs=in_specs,
        out_specs=(VM,) * len(outs),
        scratch_shapes=list(scratch),
        compiler_params=PARAMS,
        cost_estimate=cost,
        name=name,
    )


def exchange(to_up, to_down, to_left, to_right):
    spans, pitches = lax.axis_size("span"), lax.axis_size("pitch")
    rising = [(i, i + 1) for i in range(spans - 1)]
    falling = [(i + 1, i) for i in range(spans - 1)]
    onward = [(i, (i + 1) % pitches) for i in range(pitches)]
    back = [((i + 1) % pitches, i) for i in range(pitches)]
    return (
        lax.ppermute(to_down, "span", rising),
        lax.ppermute(to_up, "span", falling),
        lax.ppermute(to_right, "pitch", onward),
        lax.ppermute(to_left, "pitch", back),
    )


def on_device(
    adjoint, source, pseudo_step, jac_blocks, band_map, face_cell, face_owner, face_weight
):
    rows, spans, pitches = (lax.axis_size(name) for name in ("row", "span", "pitch"))
    devices = rows * spans * pitches
    peers = spans * pitches
    block = (NVAR, CS, CP, LANES)
    edge = (NVAR, CP, LANES)
    side = (NVAR, CS, LANES)
    edges = call(
        edges_kernel,
        "edges",
        [edge, edge, side, side],
        in_specs=[HBM],
        scratch=[pltpu.SemaphoreType.DMA((4,))],
    )(adjoint)
    halo = exchange(*edges)
    part, record, jac, src, tau = call(
        interior_kernel,
        "interior",
        [block, (CS, CP, LANES), ((7, NVAR) + block, BF16), block, (CS, CP, LANES)],
        in_specs=[HBM] * 4,
        scratch=[
            pltpu.VMEM(block, F32),
            pltpu.VMEM((7 * NVAR, CS, CP, LANES), F32),
            pltpu.VMEM(block, F32),
            pltpu.SemaphoreType.DMA((10,)),
        ],
        cost=pl.CostEstimate(flops=9_000_000, bytes_accessed=3_000_000, transcendentals=0),
    )(adjoint, source, pseudo_step, jac_blocks)
    edge = (NVAR + 1, CP, LANES)
    side = (NVAR + 1, CS, LANES)
    first, message, *sends = call(
        edge_kernel,
        "edge_update",
        [block, (2 * devices, LANES), edge, edge, side, side],
        in_specs=[VM] * 8,
        scratch=[
            pltpu.VMEM((2 * NVAR, CS, CP, LANES), F32),
            pltpu.VMEM((CS, CP, LANES), F32),
        ],
    )(part, record, jac, tau, *halo)
    records = lax.all_to_all(
        message.reshape(devices, 1, 2 * LANES), ("row", "span", "pitch"), 0, 0
    ).reshape(2 * devices, LANES)
    halo = exchange(*sends)
    field, dense = call(
        second_kernel,
        "second_iteration",
        [(1,) + block, (3 * peers, LANES)],
        in_specs=[SM] + [VM] * 12,
        scratch=[
            pltpu.VMEM((7 * NVAR, CS, CP, LANES), F32),
            pltpu.VMEM(block, F32),
            pltpu.VMEM(block, F32),
            pltpu.VMEM((2, NVAR, CP, LANES), F32),
            pltpu.VMEM((2, NVAR, CS, LANES), F32),
        ],
    )(
        band_map, first, src, tau, jac, records, *halo, face_cell, face_owner, face_weight,
    )
    parts = lax.all_to_all(dense.reshape(peers, 1, 3 * LANES), ("span", "pitch"), 0, 0)
    (nodes,) = call(third_kernel, "node_sums", [(3, 1, LANES)], in_specs=[VM])(
        parts.reshape(3 * peers, LANES)
    )
    return field, nodes.transpose(1, 0, 2)


def solution(mesh):
    in_specs = (
        P("row", None, "span", "pitch", None),
        P("row", None, "span", "pitch", None),
        P("row", "span", "pitch", None),
        P("row", None, None, None, "span", "pitch", None),
        P(),
        P("row", "span", "pitch", None),
        P("row", "span", "pitch", None),
        P("row", "span", "pitch", None, None),
    )
    out_specs = (P("row", None, "span", "pitch", None), P("row", None, ("span", "pitch")))
    return jax.shard_map(
        on_device, mesh=mesh, in_specs=in_specs, out_specs=out_specs, check_vma=False
    )
```

```python
import jax
import jax.numpy as jnp
from jax import lax
from jax.experimental import pallas as pl
from jax.experimental.pallas import tpu as pltpu
from jax.sharding import PartitionSpec as P

NVAR = 6
CS = 4
CP = 8
LANES = 128
F32 = jnp.float32
BF16 = jnp.bfloat16
FIRST_AT = 8
WEIGHT_AT = 16
COUNT_AT = 6


def lane_ids(shape):
    return lax.broadcasted_iota(jnp.int32, shape, len(shape) - 1)


def row_ids(shape):
    return lax.broadcasted_iota(jnp.int32, shape, len(shape) - 2)


def split3(x):
    hi = x.astype(BF16)
    rest = x - hi.astype(F32)
    mid = rest.astype(BF16)
    low = (rest - mid.astype(F32)).astype(BF16)
    return hi, mid, low


def dot3(x, onehot, dims):
    parts = [
        lax.dot_general(part, onehot, (dims, ((), ())), preferred_element_type=F32)
        for part in split3(x)
    ]
    return parts[0] + (parts[1] + parts[2])


def fill_stencil(vs, field, up, down, left, right, lower, upper):
    tile = (CP, LANES)
    lane, sub = lane_ids(tile), row_ids(tile)
    for d in range(NVAR):
        for j in range(CS):
            x = field(d, j)
            vs[d, j] = x
            vs[6 + d, j] = field(d, j - 1) if j > 0 else up(d)
            vs[12 + d, j] = field(d, j + 1) if j < CS - 1 else down(d)
            vs[18 + d, j] = jnp.where(
                sub == 0, jnp.broadcast_to(left(d, j), tile), pltpu.roll(x, 1, 0)
            )
            vs[24 + d, j] = jnp.where(
                sub == CP - 1, jnp.broadcast_to(right(d, j), tile), pltpu.roll(x, CP - 1, 0)
            )
            vs[30 + d, j] = jnp.where(lane == 0, lower(d, j), pltpu.roll(x, 1, 1))
            vs[36 + d, j] = jnp.where(lane == LANES - 1, upper(d, j), pltpu.roll(x, LANES - 1, 1))


def image_of(jac_ref, vs, c):
    acc = jnp.zeros((CS, CP, LANES), F32)
    for s in range(7):
        for d in range(NVAR):
            acc = acc + jac_ref[s, c, d].astype(F32) * vs[6 * s + d]
    return acc


def edges_kernel(adj_ref, up_ref, down_ref, left_ref, right_ref, sems):
    adj = adj_ref.at[0]
    copies = [
        pltpu.make_async_copy(adj.at[:, 0], up_ref, sems.at[0]),
        pltpu.make_async_copy(adj.at[:, CS - 1], down_ref, sems.at[1]),
        pltpu.make_async_copy(adj.at[:, :, 0], left_ref, sems.at[2]),
        pltpu.make_async_copy(adj.at[:, :, CP - 1], right_ref, sems.at[3]),
    ]
    for copy in copies:
        copy.start()
    for copy in copies:
        copy.wait()


def interior_kernel(
    adj_hbm, src_hbm, tau_hbm, jac_hbm, part_ref, rec_ref, jac_ref, src_ref, tau_ref, adj_ref, vs,
    image, sems,
):
    row = lax.axis_index("row")
    outlet = (1 - row) * (LANES - 1)
    ghost = 6 - row
    tile = (CP, LANES)
    zero = jnp.zeros(tile, F32)
    lane = lane_ids(tile)
    load_adj = pltpu.make_async_copy(adj_hbm.at[0], adj_ref, sems.at[0])
    load_jac = [
        pltpu.make_async_copy(jac_hbm.at[0, s], jac_ref.at[s], sems.at[1 + s]) for s in range(7)
    ]
    load_tau = pltpu.make_async_copy(tau_hbm.at[0], tau_ref, sems.at[8])
    load_src = pltpu.make_async_copy(src_hbm.at[0], src_ref, sems.at[9])
    for copy in [load_adj] + load_jac + [load_tau, load_src]:
        copy.start()
    load_adj.wait()
    fill_stencil(
        vs,
        lambda d, j: adj_ref[d, j],
        lambda d: zero,
        lambda d: zero,
        lambda d, j: zero,
        lambda d, j: zero,
        lambda d, j: zero,
        lambda d, j: zero,
    )
    for s in range(7):
        load_jac[s].wait()

        def apply(c, carry):
            acc = jnp.zeros((CS, CP, LANES), F32) if s == 0 else image[c]
            for d in range(NVAR):
                acc = acc + jac_ref[s, c, d].astype(F32) * vs[6 * s + d]
            image[c] = acc
            return carry

        lax.fori_loop(0, NVAR, apply, 0)
    load_tau.wait()
    load_src.wait()

    def finish(c, carry):
        weights, sums = (list(x) for x in carry)
        f0 = adj_ref[c]
        part_ref[c] = f0 + tau_ref[...] * (src_ref[c] - image[c])
        for j in range(CS):
            for d in range(NVAR):
                at = WEIGHT_AT + 8 * d + c
                moved = pltpu.roll(jac_ref[ghost, c, d, j].astype(F32), at + 1 - row, 1)
                weights[j] = jnp.where(lane == at, moved, weights[j])
            sums[j] = jnp.where(lane == c, pltpu.roll(f0[j], c + 1 - row, 1), sums[j])
        return tuple(weights), tuple(sums)

    ones = jnp.where(lane == COUNT_AT, 1.0, 0.0).astype(F32)
    weights, sums = lax.fori_loop(0, NVAR, finish, ((zero,) * CS, (ones,) * CS))
    for j in range(CS):
        tau_out = jnp.sum(jnp.where(lane == outlet, tau_ref[j], 0.0), axis=1, keepdims=True)
        rec_ref[j] = sums[j] + weights[j] * tau_out


def inner_sides():
    span = lax.axis_index("span")
    return (
        jnp.where(span > 0, 1.0, 0.0).astype(F32),
        jnp.where(span < lax.axis_size("span") - 1, 1.0, 0.0).astype(F32),
    )


def edge_kernel(
    part_ref, rec_in, jac_ref, tau_ref, up_ref, down_ref, left_ref, right_ref,
    f1_ref, msg_ref, to_up_ref, to_down_ref, to_left_ref, to_right_ref, sides, rec,
):
    row = lax.axis_index("row")
    keep = inner_sides()
    tile = (CP, LANES)
    lane, sub = lane_ids(tile), row_ids(tile)
    for d in range(NVAR):
        for j in range(CS):
            sides[d, j] = jnp.where(
                sub == 0, jnp.broadcast_to(left_ref[d, j : j + 1], tile), 0.0
            )
            sides[NVAR + d, j] = jnp.where(
                sub == CP - 1, jnp.broadcast_to(right_ref[d, j : j + 1], tile), 0.0
            )

    def body(c, sums):
        sums = list(sums)
        acc = jnp.zeros((CS, CP, LANES), F32)
        first = jnp.zeros(tile, F32)
        last = jnp.zeros(tile, F32)
        for d in range(NVAR):
            acc = acc + jac_ref[3, c, d].astype(F32) * sides[d]
            acc = acc + jac_ref[4, c, d].astype(F32) * sides[NVAR + d]
            first = first + jac_ref[1, c, d, 0].astype(F32) * up_ref[d]
            last = last + jac_ref[2, c, d, CS - 1].astype(F32) * down_ref[d]
        at = FIRST_AT + c
        for j in range(CS):
            lost = acc[j]
            if j == 0:
                lost = lost + first * keep[0]
            if j == CS - 1:
                lost = lost + last * keep[1]
            new = part_ref[c, j] - tau_ref[j] * lost
            f1_ref[c, j] = new
            sums[j] = jnp.where(lane == at, pltpu.roll(new, at + 1 - row, 1), sums[j])
        return tuple(sums)

    sums = lax.fori_loop(0, NVAR, body, tuple(rec_in[j] for j in range(CS)))
    rows = []
    for j in range(CS):
        rec[j] = sums[j]
        rows.append(jnp.sum(sums[j], axis=0, keepdims=True))
    halves = [
        jnp.broadcast_to(rows[2 * h] + pltpu.roll(rows[2 * h + 1], 64, 1), tile) for h in range(2)
    ]
    packed = jnp.where(sub % 2 == 0, halves[0], halves[1])
    for i in range(msg_ref.shape[0] // CP):
        msg_ref[CP * i : CP * (i + 1)] = packed
    to_up_ref[0:NVAR] = f1_ref[:, 0]
    to_up_ref[NVAR] = rec[0]
    to_down_ref[0:NVAR] = f1_ref[:, CS - 1]
    to_down_ref[NVAR] = rec[CS - 1]
    for c in range(NVAR):
        to_left_ref[c] = f1_ref[c, :, 0, :]
        to_right_ref[c] = f1_ref[c, :, CP - 1, :]
    to_left_ref[NVAR] = rec[:, 0, :]
    to_right_ref[NVAR] = rec[:, CP - 1, :]


def weight_sum(x):
    for by in (32, 16, 8):
        x = x + pltpu.roll(x, LANES - by, 1)
    return x


def spread(values):
    lane = lane_ids(values.shape)
    out = jnp.zeros(values.shape, F32)
    for d in range(NVAR):
        out = jnp.where(
            lane // 8 == d + WEIGHT_AT // 8,
            jnp.broadcast_to(values[:, d : d + 1], values.shape),
            out,
        )
    return out


def second_kernel(
    bands_ref, f1_ref, src_ref, tau_ref, jac_ref, all_ref, up_ref, down_ref, left_ref, right_ref,
    cell_ref, owner_ref, weight_ref, out_ref, dense_ref, vs, field, cycle, edge, side,
):
    row = lax.axis_index("row")
    span = lax.axis_index("span")
    outlet = (1 - row) * (LANES - 1)
    ghost = 6 - row
    tile = (CP, LANES)
    lane = lane_ids(tile)
    last_cell = bands_ref.shape[1] - 1
    wanted = [
        bands_ref[row, jnp.clip(span * CS - 1 + t, 0, last_cell)] for t in range(CS + 2)
    ]
    half = all_ref.shape[0] // 2
    zero = jnp.zeros(tile, F32)

    second_half = lane >= LANES // 2
    odd = row_ids(tile) % 2 == 1

    def gather_bands(of_row):
        base = of_row * half

        def body(i, sums):
            values = all_ref[pl.ds(pl.multiple_of(base + i * CP, CP), CP), :]
            cells = [bands_ref[of_row, i * CS + j] for j in range(CS)]
            ids = jnp.where(
                odd,
                jnp.where(second_half, cells[3], cells[2]),
                jnp.where(second_half, cells[1], cells[0]),
            )
            return tuple(
                total + jnp.where(ids == band, values, 0.0) for total, band in zip(sums, wanted)
            )

        sums = lax.fori_loop(0, half // CP, body, (zero,) * (CS + 2), unroll=4)
        rows = [jnp.sum(x, axis=0, keepdims=True) for x in sums]
        rows = rows + [rows[-1]] * (CP - len(rows))
        folded = jnp.concatenate(rows, axis=0)
        folded = folded + pltpu.roll(folded, 64, 1)
        return folded, jnp.broadcast_to(folded[:, COUNT_AT : COUNT_AT + 1], tile)

    other, other_count = gather_bands(1 - row)
    mine, my_count = gather_bands(row)
    cycle0 = other / other_count
    spread0 = spread(cycle0)
    lost = weight_sum(other * spread(mine / my_count))
    cycle1 = (other - pltpu.roll(lost, LANES - (WEIGHT_AT - FIRST_AT), 1)) / other_count
    at_outlet = lane == outlet

    for j in range(CS):
        for d in range(NVAR):
            cycle[d, j] = jnp.broadcast_to(cycle0[j + 1 : j + 2, d : d + 1], tile)

    def correct(c, carry):
        acc = jnp.zeros((CS, CP, LANES), F32)
        for d in range(NVAR):
            acc = acc + jac_ref[ghost, c, d].astype(F32) * cycle[d]
        field[c] = f1_ref[c] - jnp.where(at_outlet[None], tau_ref[...] * acc, 0.0)
        return carry

    lax.fori_loop(0, NVAR, correct, 0)
    keep = inner_sides()
    for n, (ref, at) in enumerate(((up_ref, 0), (down_ref, CS + 1))):
        moved = weight_sum(ref[NVAR] * spread0[at : at + 1])
        for c in range(NVAR):
            part = jnp.broadcast_to(moved[:, WEIGHT_AT + c : WEIGHT_AT + c + 1], tile)
            edge[n, c] = (ref[c] - jnp.where(at_outlet, part, 0.0)) * keep[n]
    low = (CS, LANES)
    low_outlet = lane_ids(low) == outlet
    for n, ref in enumerate((left_ref, right_ref)):
        moved = weight_sum(ref[NVAR] * spread0[1 : 1 + CS])
        for c in range(NVAR):
            part = jnp.broadcast_to(moved[:, WEIGHT_AT + c : WEIGHT_AT + c + 1], low)
            side[n, c] = ref[c] - jnp.where(low_outlet, part, 0.0)
    is_upper = jnp.where(row == 0, 1.0, 0.0).astype(F32)

    def cycled(d, j):
        at = FIRST_AT + d
        return jnp.broadcast_to(cycle1[j + 1 : j + 2, at : at + 1], tile)

    fill_stencil(
        vs,
        lambda d, j: field[d, j],
        lambda d: edge[0, d],
        lambda d: edge[1, d],
        lambda d, j: side[0, d, j : j + 1],
        lambda d, j: side[1, d, j : j + 1],
        lambda d, j: cycled(d, j) * (1.0 - is_upper),
        lambda d, j: cycled(d, j) * is_upper,
    )

    def advance(c, carry):
        new = field[c] + tau_ref[...] * (src_ref[c] - image_of(jac_ref, vs, c))
        out_ref[0, c] = new
        return carry

    lax.fori_loop(0, NVAR, advance, 0)

    cells = cell_ref[0, 0]
    square = (LANES, LANES)
    axial_pick = (row_ids(square) == cells % LANES).astype(F32).astype(BF16)
    flat = out_ref[0].reshape(NVAR * CS * CP, LANES)
    picked = dot3(flat, axial_pick, ((1,), (0,)))
    here = row_ids((CS * CP, LANES)) == cells // LANES
    terms = [jnp.zeros((1, LANES), F32)] * 3
    for c in range(NVAR):
        block = picked[c * CS * CP : (c + 1) * CS * CP]
        value = jnp.sum(jnp.where(here, block, 0.0), axis=0, keepdims=True)
        for k in range(3):
            at = NVAR * k + c
            terms[k] = terms[k] + weight_ref[0, 0, 0, at : at + 1] * value
    owners = owner_ref[0, 0]
    shape = dense_ref.shape
    line = row_ids(shape)
    device = (line * 43691) >> 17
    coord = line - 3 * device
    value = jnp.where(
        coord == 0,
        jnp.broadcast_to(terms[0], shape),
        jnp.where(coord == 1, jnp.broadcast_to(terms[1], shape), jnp.broadcast_to(terms[2], shape)),
    )
    placed = jnp.where(device == owners // LANES, value, 0.0)
    node_pick = (row_ids(square) == owners % LANES).astype(F32).astype(BF16)
    dense_ref[...] = dot3(placed, node_pick, ((1,), (1,)))


def third_kernel(parts_ref, out_ref):
    folded = jnp.sum(parts_ref[...].reshape(-1, 24, LANES), axis=0)
    coord = row_ids(folded.shape) % 3
    for k in range(3):
        out_ref[k] = jnp.sum(jnp.where(coord == k, folded, 0.0), axis=0, keepdims=True)


VM = pl.BlockSpec(memory_space=pltpu.VMEM)
SM = pl.BlockSpec(memory_space=pltpu.SMEM)
PARAMS = pltpu.CompilerParams(vmem_limit_bytes=32 * 1024 * 1024)


HBM = pl.BlockSpec(memory_space=pltpu.HBM)


def in_hbm(x):
    return pltpu.with_memory_space_constraint(x, pltpu.HBM)


def call(kernel, name, outs, in_specs, scratch=(), cost=None):
    outs = [out if isinstance(out[0], tuple) else (out, F32) for out in outs]
    return pl.pallas_call(
        kernel,
        out_shape=tuple(jax.ShapeDtypeStruct(shape, dtype) for shape, dtype in outs),
        in_specs=in_specs,
        out_specs=(VM,) * len(outs),
        scratch_shapes=list(scratch),
        compiler_params=PARAMS,
        cost_estimate=cost,
        name=name,
    )


def exchange(to_up, to_down, to_left, to_right):
    spans, pitches = lax.axis_size("span"), lax.axis_size("pitch")
    rising = [(i, (i + 1) % spans) for i in range(spans)]
    falling = [((i + 1) % spans, i) for i in range(spans)]
    onward = [(i, (i + 1) % pitches) for i in range(pitches)]
    back = [((i + 1) % pitches, i) for i in range(pitches)]
    return (
        lax.ppermute(to_down, "span", rising),
        lax.ppermute(to_up, "span", falling),
        lax.ppermute(to_right, "pitch", onward),
        lax.ppermute(to_left, "pitch", back),
    )


def on_device(
    adjoint, source, pseudo_step, jac_blocks, band_map, face_cell, face_owner, face_weight
):
    rows, spans, pitches = (lax.axis_size(name) for name in ("row", "span", "pitch"))
    devices = rows * spans * pitches
    peers = spans * pitches
    block = (NVAR, CS, CP, LANES)
    edge = (NVAR, CP, LANES)
    side = (NVAR, CS, LANES)
    edges = call(
        edges_kernel,
        "edges",
        [edge, edge, side, side],
        in_specs=[HBM],
        scratch=[pltpu.SemaphoreType.DMA((4,))],
    )(in_hbm(adjoint))
    halo = exchange(*edges)
    part, record, jac, src, tau = call(
        interior_kernel,
        "interior",
        [block, (CS, CP, LANES), ((7, NVAR) + block, BF16), block, (CS, CP, LANES)],
        in_specs=[HBM] * 4,
        scratch=[
            pltpu.VMEM(block, F32),
            pltpu.VMEM((7 * NVAR, CS, CP, LANES), F32),
            pltpu.VMEM(block, F32),
            pltpu.SemaphoreType.DMA((10,)),
        ],
        cost=pl.CostEstimate(flops=9_000_000, bytes_accessed=3_000_000, transcendentals=0),
    )(*(in_hbm(x) for x in (adjoint, source, pseudo_step, jac_blocks)))
    edge = (NVAR + 1, CP, LANES)
    side = (NVAR + 1, CS, LANES)
    first, message, *sends = call(
        edge_kernel,
        "edge_update",
        [block, (2 * devices, LANES), edge, edge, side, side],
        in_specs=[VM] * 8,
        scratch=[
            pltpu.VMEM((2 * NVAR, CS, CP, LANES), F32),
            pltpu.VMEM((CS, CP, LANES), F32),
        ],
    )(part, record, jac, tau, *halo)
    records = lax.all_to_all(
        message.reshape(devices, 1, 2 * LANES), ("row", "span", "pitch"), 0, 0
    ).reshape(2 * devices, LANES)
    halo = exchange(*sends)
    field, dense = call(
        second_kernel,
        "second_iteration",
        [(1,) + block, (3 * peers, LANES)],
        in_specs=[SM] + [VM] * 12,
        scratch=[
            pltpu.VMEM((7 * NVAR, CS, CP, LANES), F32),
            pltpu.VMEM(block, F32),
            pltpu.VMEM(block, F32),
            pltpu.VMEM((2, NVAR, CP, LANES), F32),
            pltpu.VMEM((2, NVAR, CS, LANES), F32),
        ],
    )(
        band_map, first, src, tau, jac, records, *halo, face_cell, face_owner, face_weight,
    )
    parts = lax.all_to_all(dense.reshape(peers, 1, 3 * LANES), ("span", "pitch"), 0, 0)
    (nodes,) = call(third_kernel, "node_sums", [(3, 1, LANES)], in_specs=[VM])(
        parts.reshape(3 * peers, LANES)
    )
    return field, nodes.transpose(1, 0, 2)


def solution(mesh):
    in_specs = (
        P("row", None, "span", "pitch", None),
        P("row", None, "span", "pitch", None),
        P("row", "span", "pitch", None),
        P("row", None, None, None, "span", "pitch", None),
        P(),
        P("row", "span", "pitch", None),
        P("row", "span", "pitch", None),
        P("row", "span", "pitch", None, None),
    )
    out_specs = (P("row", None, "span", "pitch", None), P("row", None, ("span", "pitch")))
    return jax.shard_map(
        on_device, mesh=mesh, in_specs=in_specs, out_specs=out_specs, check_vma=False
    )
```

```python
import jax
import jax.numpy as jnp
from jax import lax
from jax.experimental import pallas as pl
from jax.experimental.pallas import tpu as pltpu
from jax.sharding import PartitionSpec as P

NVAR = 6
CS = 4
CP = 8
LANES = 128
F32 = jnp.float32
BF16 = jnp.bfloat16
FIRST_AT = 8
WEIGHT_AT = 16
COUNT_AT = 6
OWN_AT = 22
OWN_COUNT_AT = 14


def lane_ids(shape):
    return lax.broadcasted_iota(jnp.int32, shape, len(shape) - 1)


def row_ids(shape):
    return lax.broadcasted_iota(jnp.int32, shape, len(shape) - 2)


def split3(x):
    hi = x.astype(BF16)
    rest = x - hi.astype(F32)
    mid = rest.astype(BF16)
    low = (rest - mid.astype(F32)).astype(BF16)
    return hi, mid, low


def dot3(x, onehot, dims):
    parts = [
        lax.dot_general(part, onehot, (dims, ((), ())), preferred_element_type=F32)
        for part in split3(x)
    ]
    return parts[0] + (parts[1] + parts[2])


def fill_stencil(vs, field, up, down, left, right, lower, upper):
    tile = (CP, LANES)
    lane, sub = lane_ids(tile), row_ids(tile)
    for d in range(NVAR):
        for j in range(CS):
            x = field(d, j)
            vs[d, j] = x
            vs[6 + d, j] = field(d, j - 1) if j > 0 else up(d)
            vs[12 + d, j] = field(d, j + 1) if j < CS - 1 else down(d)
            vs[18 + d, j] = jnp.where(
                sub == 0, jnp.broadcast_to(left(d, j), tile), pltpu.roll(x, 1, 0)
            )
            vs[24 + d, j] = jnp.where(
                sub == CP - 1, jnp.broadcast_to(right(d, j), tile), pltpu.roll(x, CP - 1, 0)
            )
            vs[30 + d, j] = jnp.where(lane == 0, lower(d, j), pltpu.roll(x, 1, 1))
            vs[36 + d, j] = jnp.where(lane == LANES - 1, upper(d, j), pltpu.roll(x, LANES - 1, 1))


def image_of(jac_ref, vs, c):
    acc = jnp.zeros((CS, CP, LANES), F32)
    for s in range(7):
        for d in range(NVAR):
            acc = acc + jac_ref[s, c, d].astype(F32) * vs[6 * s + d]
    return acc


def edges_kernel(adj_ref, up_ref, down_ref, left_ref, right_ref, sems):
    adj = adj_ref.at[0]
    copies = [
        pltpu.make_async_copy(adj.at[:, 0], up_ref, sems.at[0]),
        pltpu.make_async_copy(adj.at[:, CS - 1], down_ref, sems.at[1]),
        pltpu.make_async_copy(adj.at[:, :, 0], left_ref, sems.at[2]),
        pltpu.make_async_copy(adj.at[:, :, CP - 1], right_ref, sems.at[3]),
    ]
    for copy in copies:
        copy.start()
    for copy in copies:
        copy.wait()


def interior_kernel(
    adj_hbm, src_hbm, tau_hbm, jac_hbm, part_ref, rec_ref, jac_ref, src_ref, tau_ref, adj_ref, vs,
    image, sems,
):
    row = lax.axis_index("row")
    outlet = (1 - row) * (LANES - 1)
    ghost = 6 - row
    tile = (CP, LANES)
    zero = jnp.zeros(tile, F32)
    lane = lane_ids(tile)
    load_adj = pltpu.make_async_copy(adj_hbm.at[0], adj_ref, sems.at[0])
    load_jac = [
        pltpu.make_async_copy(jac_hbm.at[0, s], jac_ref.at[s], sems.at[1 + s]) for s in range(7)
    ]
    load_tau = pltpu.make_async_copy(tau_hbm.at[0], tau_ref, sems.at[8])
    load_src = pltpu.make_async_copy(src_hbm.at[0], src_ref, sems.at[9])
    for copy in [load_adj] + load_jac + [load_tau, load_src]:
        copy.start()
    load_adj.wait()
    fill_stencil(
        vs,
        lambda d, j: adj_ref[d, j],
        lambda d: zero,
        lambda d: zero,
        lambda d, j: zero,
        lambda d, j: zero,
        lambda d, j: zero,
        lambda d, j: zero,
    )
    for s in range(7):
        load_jac[s].wait()

        def apply(c, carry):
            acc = jnp.zeros((CS, CP, LANES), F32) if s == 0 else image[c]
            for d in range(NVAR):
                acc = acc + jac_ref[s, c, d].astype(F32) * vs[6 * s + d]
            image[c] = acc
            return carry

        lax.fori_loop(0, NVAR, apply, 0)
    load_tau.wait()
    load_src.wait()

    def finish(c, carry):
        weights, sums = (list(x) for x in carry)
        f0 = adj_ref[c]
        part_ref[c] = f0 + tau_ref[...] * (src_ref[c] - image[c])
        for j in range(CS):
            for d in range(NVAR):
                at = WEIGHT_AT + 8 * d + c
                moved = pltpu.roll(jac_ref[ghost, c, d, j].astype(F32), at + 1 - row, 1)
                weights[j] = jnp.where(lane == at, moved, weights[j])
            sums[j] = jnp.where(lane == c, pltpu.roll(f0[j], c + 1 - row, 1), sums[j])
        return tuple(weights), tuple(sums)

    ones = jnp.where(lane == COUNT_AT, 1.0, 0.0).astype(F32)
    weights, sums = lax.fori_loop(0, NVAR, finish, ((zero,) * CS, (ones,) * CS))
    for j in range(CS):
        tau_out = jnp.sum(jnp.where(lane == outlet, tau_ref[j], 0.0), axis=1, keepdims=True)
        rec_ref[j] = sums[j] + weights[j] * tau_out


def inner_sides():
    span = lax.axis_index("span")
    return (
        jnp.where(span > 0, 1.0, 0.0).astype(F32),
        jnp.where(span < lax.axis_size("span") - 1, 1.0, 0.0).astype(F32),
    )


def edge_kernel(
    part_ref, rec_in, jac_ref, tau_ref, up_ref, down_ref, left_ref, right_ref,
    f1_ref, swap_ref, own_ref, to_up_ref, to_down_ref, to_left_ref, to_right_ref, sides, rec,
):
    row = lax.axis_index("row")
    keep = inner_sides()
    tile = (CP, LANES)
    lane, sub = lane_ids(tile), row_ids(tile)
    for d in range(NVAR):
        for j in range(CS):
            sides[d, j] = jnp.where(
                sub == 0, jnp.broadcast_to(left_ref[d, j : j + 1], tile), 0.0
            )
            sides[NVAR + d, j] = jnp.where(
                sub == CP - 1, jnp.broadcast_to(right_ref[d, j : j + 1], tile), 0.0
            )

    def body(c, sums):
        sums = list(sums)
        acc = jnp.zeros((CS, CP, LANES), F32)
        first = jnp.zeros(tile, F32)
        last = jnp.zeros(tile, F32)
        for d in range(NVAR):
            acc = acc + jac_ref[3, c, d].astype(F32) * sides[d]
            acc = acc + jac_ref[4, c, d].astype(F32) * sides[NVAR + d]
            first = first + jac_ref[1, c, d, 0].astype(F32) * up_ref[d]
            last = last + jac_ref[2, c, d, CS - 1].astype(F32) * down_ref[d]
        at = FIRST_AT + c
        for j in range(CS):
            lost = acc[j]
            if j == 0:
                lost = lost + first * keep[0]
            if j == CS - 1:
                lost = lost + last * keep[1]
            new = part_ref[c, j] - tau_ref[j] * lost
            f1_ref[c, j] = new
            sums[j] = jnp.where(lane == at, pltpu.roll(new, at + 1 - row, 1), sums[j])
        return tuple(sums)

    sums = lax.fori_loop(0, NVAR, body, tuple(rec_in[j] for j in range(CS)))
    rows, own_rows = [], []
    for j in range(CS):
        rec[j] = sums[j]
        rows.append(jnp.sum(sums[j], axis=0, keepdims=True))
        own = jnp.where(
            lane[:1] == OWN_COUNT_AT, pltpu.roll(rows[j], OWN_COUNT_AT - COUNT_AT, 1), 0.0
        )
        for c in range(NVAR):
            at = OWN_AT + 8 * c
            own = jnp.where(lane[:1] == at, pltpu.roll(rows[j], at - c, 1), own)
        own_rows.append(own)
    for ref, lines in ((swap_ref, rows), (own_ref, own_rows)):
        for h in range(2):
            ref[h : h + 1] = lines[2 * h] + pltpu.roll(lines[2 * h + 1], 64, 1)
    to_up_ref[0:NVAR] = f1_ref[:, 0]
    to_up_ref[NVAR] = rec[0]
    to_down_ref[0:NVAR] = f1_ref[:, CS - 1]
    to_down_ref[NVAR] = rec[CS - 1]
    for c in range(NVAR):
        to_left_ref[c] = f1_ref[c, :, 0, :]
        to_right_ref[c] = f1_ref[c, :, CP - 1, :]
    to_left_ref[NVAR] = rec[:, 0, :]
    to_right_ref[NVAR] = rec[:, CP - 1, :]


def weight_sum(x):
    for by in (32, 16, 8):
        x = x + pltpu.roll(x, LANES - by, 1)
    return x


def spread(values, first, step):
    lane = lane_ids(values.shape)
    out = jnp.zeros(values.shape, F32)
    for d in range(NVAR):
        at = first + step * d
        out = jnp.where(
            lane // 8 == d + WEIGHT_AT // 8,
            jnp.broadcast_to(values[:, at : at + 1], values.shape),
            out,
        )
    return out


def second_kernel(
    bands_ref, f1_ref, src_ref, tau_ref, jac_ref, all_ref, up_ref, down_ref, left_ref, right_ref,
    cell_ref, owner_ref, weight_ref, out_ref, dense_ref, vs, field, cycle, edge, side,
):
    row = lax.axis_index("row")
    span = lax.axis_index("span")
    outlet = (1 - row) * (LANES - 1)
    ghost = 6 - row
    tile = (CP, LANES)
    lane = lane_ids(tile)
    last_cell = bands_ref.shape[1] - 1
    wanted = [
        bands_ref[row, jnp.clip(span * CS - 1 + t, 0, last_cell)] for t in range(CS + 2)
    ]
    lines = all_ref.shape[0]
    zero = jnp.zeros(tile, F32)

    second_half = lane >= LANES // 2
    odd = row_ids(tile) % 2 == 1

    def gather_bands(of_row, count_at):
        def body(i, sums):
            values = all_ref[pl.ds(pl.multiple_of(i * CP, CP), CP), :]
            cells = [bands_ref[of_row, i * CS + j] for j in range(CS)]
            ids = jnp.where(
                odd,
                jnp.where(second_half, cells[3], cells[2]),
                jnp.where(second_half, cells[1], cells[0]),
            )
            return tuple(
                total + jnp.where(ids == band, values, 0.0) for total, band in zip(sums, wanted)
            )

        sums = lax.fori_loop(0, lines // CP, body, (zero,) * (CS + 2), unroll=4)
        rows = [jnp.sum(x, axis=0, keepdims=True) for x in sums]
        rows = rows + [rows[-1]] * (CP - len(rows))
        folded = jnp.concatenate(rows, axis=0)
        folded = folded + pltpu.roll(folded, 64, 1)
        return folded, jnp.broadcast_to(folded[:, count_at : count_at + 1], tile)

    other, other_count = gather_bands(1 - row, COUNT_AT)
    mine, my_count = gather_bands(row, OWN_COUNT_AT)
    cycle0 = other / other_count
    spread0 = spread(cycle0, 0, 1)
    lost = weight_sum(other * spread(mine / my_count, OWN_AT, 8))
    cycle1 = (other - pltpu.roll(lost, LANES - (WEIGHT_AT - FIRST_AT), 1)) / other_count
    at_outlet = lane == outlet

    for j in range(CS):
        for d in range(NVAR):
            cycle[d, j] = jnp.broadcast_to(cycle0[j + 1 : j + 2, d : d + 1], tile)

    def correct(c, carry):
        acc = jnp.zeros((CS, CP, LANES), F32)
        for d in range(NVAR):
            acc = acc + jac_ref[ghost, c, d].astype(F32) * cycle[d]
        field[c] = f1_ref[c] - jnp.where(at_outlet[None], tau_ref[...] * acc, 0.0)
        return carry

    lax.fori_loop(0, NVAR, correct, 0)
    keep = inner_sides()
    for n, (ref, at) in enumerate(((up_ref, 0), (down_ref, CS + 1))):
        moved = weight_sum(ref[NVAR] * spread0[at : at + 1])
        for c in range(NVAR):
            part = jnp.broadcast_to(moved[:, WEIGHT_AT + c : WEIGHT_AT + c + 1], tile)
            edge[n, c] = (ref[c] - jnp.where(at_outlet, part, 0.0)) * keep[n]
    low = (CS, LANES)
    low_outlet = lane_ids(low) == outlet
    for n, ref in enumerate((left_ref, right_ref)):
        moved = weight_sum(ref[NVAR] * spread0[1 : 1 + CS])
        for c in range(NVAR):
            part = jnp.broadcast_to(moved[:, WEIGHT_AT + c : WEIGHT_AT + c + 1], low)
            side[n, c] = ref[c] - jnp.where(low_outlet, part, 0.0)
    is_upper = jnp.where(row == 0, 1.0, 0.0).astype(F32)

    def cycled(d, j):
        at = FIRST_AT + d
        return jnp.broadcast_to(cycle1[j + 1 : j + 2, at : at + 1], tile)

    fill_stencil(
        vs,
        lambda d, j: field[d, j],
        lambda d: edge[0, d],
        lambda d: edge[1, d],
        lambda d, j: side[0, d, j : j + 1],
        lambda d, j: side[1, d, j : j + 1],
        lambda d, j: cycled(d, j) * (1.0 - is_upper),
        lambda d, j: cycled(d, j) * is_upper,
    )

    def advance(c, carry):
        new = field[c] + tau_ref[...] * (src_ref[c] - image_of(jac_ref, vs, c))
        out_ref[0, c] = new
        return carry

    lax.fori_loop(0, NVAR, advance, 0)

    cells = cell_ref[0, 0]
    square = (LANES, LANES)
    axial_pick = (row_ids(square) == cells % LANES).astype(F32).astype(BF16)
    flat = out_ref[0].reshape(NVAR * CS * CP, LANES)
    picked = dot3(flat, axial_pick, ((1,), (0,)))
    here = row_ids((CS * CP, LANES)) == cells // LANES
    terms = [jnp.zeros((1, LANES), F32)] * 3
    for c in range(NVAR):
        block = picked[c * CS * CP : (c + 1) * CS * CP]
        value = jnp.sum(jnp.where(here, block, 0.0), axis=0, keepdims=True)
        for k in range(3):
            at = NVAR * k + c
            terms[k] = terms[k] + weight_ref[0, 0, 0, at : at + 1] * value
    owners = owner_ref[0, 0]
    shape = dense_ref.shape
    line = row_ids(shape)
    device = (line * 43691) >> 17
    coord = line - 3 * device
    value = jnp.where(
        coord == 0,
        jnp.broadcast_to(terms[0], shape),
        jnp.where(coord == 1, jnp.broadcast_to(terms[1], shape), jnp.broadcast_to(terms[2], shape)),
    )
    placed = jnp.where(device == owners // LANES, value, 0.0)
    node_pick = (row_ids(square) == owners % LANES).astype(F32).astype(BF16)
    dense_ref[...] = dot3(placed, node_pick, ((1,), (1,)))


def third_kernel(parts_ref, out_ref):
    folded = jnp.sum(parts_ref[...].reshape(-1, 24, LANES), axis=0)
    coord = row_ids(folded.shape) % 3
    for k in range(3):
        out_ref[k] = jnp.sum(jnp.where(coord == k, folded, 0.0), axis=0, keepdims=True)


VM = pl.BlockSpec(memory_space=pltpu.VMEM)
SM = pl.BlockSpec(memory_space=pltpu.SMEM)
PARAMS = pltpu.CompilerParams(vmem_limit_bytes=32 * 1024 * 1024)


HBM = pl.BlockSpec(memory_space=pltpu.HBM)


def in_hbm(x):
    return pltpu.with_memory_space_constraint(x, pltpu.HBM)


def call(kernel, name, outs, in_specs, scratch=(), cost=None):
    outs = [out if isinstance(out[0], tuple) else (out, F32) for out in outs]
    return pl.pallas_call(
        kernel,
        out_shape=tuple(jax.ShapeDtypeStruct(shape, dtype) for shape, dtype in outs),
        in_specs=in_specs,
        out_specs=(VM,) * len(outs),
        scratch_shapes=list(scratch),
        compiler_params=PARAMS,
        cost_estimate=cost,
        name=name,
    )


def exchange(to_up, to_down, to_left, to_right):
    spans, pitches = lax.axis_size("span"), lax.axis_size("pitch")
    rising = [(i, (i + 1) % spans) for i in range(spans)]
    falling = [((i + 1) % spans, i) for i in range(spans)]
    onward = [(i, (i + 1) % pitches) for i in range(pitches)]
    back = [((i + 1) % pitches, i) for i in range(pitches)]
    return (
        lax.ppermute(to_down, "span", rising),
        lax.ppermute(to_up, "span", falling),
        lax.ppermute(to_right, "pitch", onward),
        lax.ppermute(to_left, "pitch", back),
    )


def on_device(
    adjoint, source, pseudo_step, jac_blocks, band_map, face_cell, face_owner, face_weight
):
    rows, spans, pitches = (lax.axis_size(name) for name in ("row", "span", "pitch"))
    peers = spans * pitches
    block = (NVAR, CS, CP, LANES)
    edge = (NVAR, CP, LANES)
    side = (NVAR, CS, LANES)
    edges = call(
        edges_kernel,
        "edges",
        [edge, edge, side, side],
        in_specs=[HBM],
        scratch=[pltpu.SemaphoreType.DMA((4,))],
    )(in_hbm(adjoint))
    halo = exchange(*edges)
    part, record, jac, src, tau = call(
        interior_kernel,
        "interior",
        [block, (CS, CP, LANES), ((7, NVAR) + block, BF16), block, (CS, CP, LANES)],
        in_specs=[HBM] * 4,
        scratch=[
            pltpu.VMEM(block, F32),
            pltpu.VMEM((7 * NVAR, CS, CP, LANES), F32),
            pltpu.VMEM(block, F32),
            pltpu.SemaphoreType.DMA((10,)),
        ],
        cost=pl.CostEstimate(flops=9_000_000, bytes_accessed=3_000_000, transcendentals=0),
    )(*(in_hbm(x) for x in (adjoint, source, pseudo_step, jac_blocks)))
    edge = (NVAR + 1, CP, LANES)
    side = (NVAR + 1, CS, LANES)
    first, swapped, own, *sends = call(
        edge_kernel,
        "edge_update",
        [block, (2, LANES), (2, LANES), edge, edge, side, side],
        in_specs=[VM] * 8,
        scratch=[
            pltpu.VMEM((2 * NVAR, CS, CP, LANES), F32),
            pltpu.VMEM((CS, CP, LANES), F32),
        ],
    )(part, record, jac, tau, *halo)
    message = lax.ppermute(swapped, "row", [(i, rows - 1 - i) for i in range(rows)]) + own
    records = lax.all_to_all(
        jnp.broadcast_to(message.reshape(1, 1, 2 * LANES), (peers, 1, 2 * LANES)),
        ("span", "pitch"), 0, 0,
    ).reshape(2 * peers, LANES)
    halo = exchange(*sends)
    field, dense = call(
        second_kernel,
        "second_iteration",
        [(1,) + block, (3 * peers, LANES)],
        in_specs=[SM] + [VM] * 12,
        scratch=[
            pltpu.VMEM((7 * NVAR, CS, CP, LANES), F32),
            pltpu.VMEM(block, F32),
            pltpu.VMEM(block, F32),
            pltpu.VMEM((2, NVAR, CP, LANES), F32),
            pltpu.VMEM((2, NVAR, CS, LANES), F32),
        ],
    )(
        band_map, first, src, tau, jac, records, *halo, face_cell, face_owner, face_weight,
    )
    parts = lax.all_to_all(dense.reshape(peers, 1, 3 * LANES), ("span", "pitch"), 0, 0)
    (nodes,) = call(third_kernel, "node_sums", [(3, 1, LANES)], in_specs=[VM])(
        parts.reshape(3 * peers, LANES)
    )
    return field, nodes.transpose(1, 0, 2)


def solution(mesh):
    in_specs = (
        P("row", None, "span", "pitch", None),
        P("row", None, "span", "pitch", None),
        P("row", "span", "pitch", None),
        P("row", None, None, None, "span", "pitch", None),
        P(),
        P("row", "span", "pitch", None),
        P("row", "span", "pitch", None),
        P("row", "span", "pitch", None, None),
    )
    out_specs = (P("row", None, "span", "pitch", None), P("row", None, ("span", "pitch")))
    return jax.shard_map(
        on_device, mesh=mesh, in_specs=in_specs, out_specs=out_specs, check_vma=False
    )
```

```python
import jax
import jax.numpy as jnp
from jax import lax
from jax.experimental import pallas as pl
from jax.experimental.pallas import tpu as pltpu
from jax.sharding import PartitionSpec as P

NVAR = 6
CS = 4
CP = 8
LANES = 128
F32 = jnp.float32
BF16 = jnp.bfloat16
FIRST_AT = 8
WEIGHT_AT = 16
COUNT_AT = 6


def lane_ids(shape):
    return lax.broadcasted_iota(jnp.int32, shape, len(shape) - 1)


def row_ids(shape):
    return lax.broadcasted_iota(jnp.int32, shape, len(shape) - 2)


def split3(x):
    hi = x.astype(BF16)
    rest = x - hi.astype(F32)
    mid = rest.astype(BF16)
    low = (rest - mid.astype(F32)).astype(BF16)
    return hi, mid, low


def dot3(x, onehot, dims):
    parts = [
        lax.dot_general(part, onehot, (dims, ((), ())), preferred_element_type=F32)
        for part in split3(x)
    ]
    return parts[0] + (parts[1] + parts[2])


def fill_stencil(vs, field, up, down, left, right, lower, upper):
    tile = (CP, LANES)
    lane, sub = lane_ids(tile), row_ids(tile)
    for d in range(NVAR):
        for j in range(CS):
            x = field(d, j)
            vs[d, j] = x
            vs[6 + d, j] = field(d, j - 1) if j > 0 else up(d)
            vs[12 + d, j] = field(d, j + 1) if j < CS - 1 else down(d)
            vs[18 + d, j] = jnp.where(
                sub == 0, jnp.broadcast_to(left(d, j), tile), pltpu.roll(x, 1, 0)
            )
            vs[24 + d, j] = jnp.where(
                sub == CP - 1, jnp.broadcast_to(right(d, j), tile), pltpu.roll(x, CP - 1, 0)
            )
            vs[30 + d, j] = jnp.where(lane == 0, lower(d, j), pltpu.roll(x, 1, 1))
            vs[36 + d, j] = jnp.where(lane == LANES - 1, upper(d, j), pltpu.roll(x, LANES - 1, 1))


def image_of(jac_ref, vs, c):
    acc = jnp.zeros((CS, CP, LANES), F32)
    for s in range(7):
        for d in range(NVAR):
            acc = acc + jac_ref[s, c, d].astype(F32) * vs[6 * s + d]
    return acc


def edges_kernel(adj_ref, up_ref, down_ref, left_ref, right_ref, sems):
    adj = adj_ref.at[0]
    copies = [
        pltpu.make_async_copy(adj.at[:, 0], up_ref, sems.at[0]),
        pltpu.make_async_copy(adj.at[:, CS - 1], down_ref, sems.at[1]),
        pltpu.make_async_copy(adj.at[:, :, 0], left_ref, sems.at[2]),
        pltpu.make_async_copy(adj.at[:, :, CP - 1], right_ref, sems.at[3]),
    ]
    for copy in copies:
        copy.start()
    for copy in copies:
        copy.wait()


def interior_kernel(
    adj_hbm, src_hbm, tau_hbm, jac_hbm, part_ref, rec_ref, jac_ref, src_ref, tau_ref, adj_ref, vs,
    image, sems,
):
    row = lax.axis_index("row")
    outlet = (1 - row) * (LANES - 1)
    ghost = 6 - row
    tile = (CP, LANES)
    zero = jnp.zeros(tile, F32)
    lane = lane_ids(tile)
    load_adj = pltpu.make_async_copy(adj_hbm.at[0], adj_ref, sems.at[0])
    load_jac = [
        pltpu.make_async_copy(jac_hbm.at[0, s], jac_ref.at[s], sems.at[1 + s]) for s in range(7)
    ]
    load_tau = pltpu.make_async_copy(tau_hbm.at[0], tau_ref, sems.at[8])
    load_src = pltpu.make_async_copy(src_hbm.at[0], src_ref, sems.at[9])
    for copy in [load_adj] + load_jac + [load_tau, load_src]:
        copy.start()
    load_adj.wait()
    fill_stencil(
        vs,
        lambda d, j: adj_ref[d, j],
        lambda d: zero,
        lambda d: zero,
        lambda d, j: zero,
        lambda d, j: zero,
        lambda d, j: zero,
        lambda d, j: zero,
    )
    for s in range(7):
        load_jac[s].wait()

        def apply(c, carry):
            acc = jnp.zeros((CS, CP, LANES), F32) if s == 0 else image[c]
            for d in range(NVAR):
                acc = acc + jac_ref[s, c, d].astype(F32) * vs[6 * s + d]
            image[c] = acc
            return carry

        lax.fori_loop(0, NVAR, apply, 0)
    load_tau.wait()
    load_src.wait()

    def finish(c, carry):
        weights, sums = (list(x) for x in carry)
        f0 = adj_ref[c]
        part_ref[c] = f0 + tau_ref[...] * (src_ref[c] - image[c])
        for j in range(CS):
            for d in range(NVAR):
                at = WEIGHT_AT + 8 * d + c
                moved = pltpu.roll(jac_ref[ghost, c, d, j].astype(F32), at + 1 - row, 1)
                weights[j] = jnp.where(lane == at, moved, weights[j])
            sums[j] = jnp.where(lane == c, pltpu.roll(f0[j], c + 1 - row, 1), sums[j])
        return tuple(weights), tuple(sums)

    ones = jnp.where(lane == COUNT_AT, 1.0, 0.0).astype(F32)
    weights, sums = lax.fori_loop(0, NVAR, finish, ((zero,) * CS, (ones,) * CS))
    for j in range(CS):
        tau_out = jnp.sum(jnp.where(lane == outlet, tau_ref[j], 0.0), axis=1, keepdims=True)
        rec_ref[j] = sums[j] + weights[j] * tau_out


def inner_sides():
    span = lax.axis_index("span")
    return (
        jnp.where(span > 0, 1.0, 0.0).astype(F32),
        jnp.where(span < lax.axis_size("span") - 1, 1.0, 0.0).astype(F32),
    )


def fill_sides(sides, left_ref, right_ref):
    tile = (CP, LANES)
    sub = row_ids(tile)
    for d in range(NVAR):
        for j in range(CS):
            sides[d, j] = jnp.where(
                sub == 0, jnp.broadcast_to(left_ref[d, j : j + 1], tile), 0.0
            )
            sides[NVAR + d, j] = jnp.where(
                sub == CP - 1, jnp.broadcast_to(right_ref[d, j : j + 1], tile), 0.0
            )


def edge_terms(jac_ref, sides, up_ref, down_ref, keep, c):
    acc = jnp.zeros((CS, CP, LANES), F32)
    first = jnp.zeros((CP, LANES), F32)
    last = jnp.zeros((CP, LANES), F32)
    for d in range(NVAR):
        acc = acc + jac_ref[3, c, d].astype(F32) * sides[d]
        acc = acc + jac_ref[4, c, d].astype(F32) * sides[NVAR + d]
        first = first + jac_ref[1, c, d, 0].astype(F32) * up_ref[d]
        last = last + jac_ref[2, c, d, CS - 1].astype(F32) * down_ref[d]
    lost = [acc[j] for j in range(CS)]
    lost[0] = lost[0] + first * keep[0]
    lost[CS - 1] = lost[CS - 1] + last * keep[1]
    return lost


def edge_kernel(
    part_ref, rec_in, jac_ref, tau_ref, up_ref, down_ref, left_ref, right_ref,
    f1_ref, msg_ref, rec, to_up_ref, to_down_ref, to_left_ref, to_right_ref, sides,
):
    row = lax.axis_index("row")
    keep = inner_sides()
    tile = (CP, LANES)
    lane, sub = lane_ids(tile), row_ids(tile)
    fill_sides(sides, left_ref, right_ref)

    def body(c, sums):
        sums = list(sums)
        lost = edge_terms(jac_ref, sides, up_ref, down_ref, keep, c)
        at = FIRST_AT + c
        for j in range(CS):
            new = part_ref[c, j] - tau_ref[j] * lost[j]
            f1_ref[c, j] = new
            sums[j] = jnp.where(lane == at, pltpu.roll(new, at + 1 - row, 1), sums[j])
        return tuple(sums)

    sums = lax.fori_loop(0, NVAR, body, tuple(rec_in[j] for j in range(CS)))
    rows = []
    for j in range(CS):
        rec[j] = sums[j]
        rows.append(jnp.sum(sums[j], axis=0, keepdims=True))
    halves = [
        jnp.broadcast_to(rows[2 * h] + pltpu.roll(rows[2 * h + 1], 64, 1), tile) for h in range(2)
    ]
    packed = jnp.where(sub % 2 == 0, halves[0], halves[1])
    for i in range(msg_ref.shape[0] // CP):
        msg_ref[CP * i : CP * (i + 1)] = packed
    to_up_ref[0:NVAR] = f1_ref[:, 0]
    to_up_ref[NVAR] = rec[0]
    to_down_ref[0:NVAR] = f1_ref[:, CS - 1]
    to_down_ref[NVAR] = rec[CS - 1]
    for c in range(NVAR):
        to_left_ref[c] = f1_ref[c, :, 0, :]
        to_right_ref[c] = f1_ref[c, :, CP - 1, :]
    to_left_ref[NVAR] = rec[:, 0, :]
    to_right_ref[NVAR] = rec[:, CP - 1, :]


def weight_sum(x):
    for by in (32, 16, 8):
        x = x + pltpu.roll(x, LANES - by, 1)
    return x


def spread(values, first):
    lane = lane_ids(values.shape)
    out = jnp.zeros(values.shape, F32)
    for d in range(NVAR):
        at = first + d
        out = jnp.where(
            lane // 8 == d + WEIGHT_AT // 8,
            jnp.broadcast_to(values[:, at : at + 1], values.shape),
            out,
        )
    return out


def outlet_lanes(row):
    return (1 - row) * (LANES - 1), (1 - row) * (LANES - 2) + row


def settle_kernel(
    bands_ref, f1_ref, src_ref, tau_ref, jac_ref, cell_ref, owner_ref,
    part_ref, pack_ref, ids_ref, seen_ref, node_ref, vs,
):
    row = lax.axis_index("row")
    outlet, inner = outlet_lanes(row)
    ghost = 6 - row
    tile = (CP, LANES)
    zero = jnp.zeros(tile, F32)
    lane = lane_ids(tile)
    fill_stencil(
        vs,
        lambda d, j: f1_ref[d, j],
        lambda d: zero,
        lambda d: zero,
        lambda d, j: zero,
        lambda d, j: zero,
        lambda d, j: zero,
        lambda d, j: zero,
    )
    for n in range(6):
        for j in range(CS):
            pack_ref[n, j] = zero

    def advance(c, carry):
        part_ref[c] = f1_ref[c] + tau_ref[...] * (src_ref[c] - image_of(jac_ref, vs, c))
        for n in range(6):
            point = n if n < 5 else ghost
            extra = 1 - row if n < 5 else 2 - 3 * row
            for j in range(CS):
                pack = pack_ref[n, j]
                for d in range(NVAR):
                    at = WEIGHT_AT + 8 * d + c
                    moved = pltpu.roll(jac_ref[point, c, d, j].astype(F32), at + extra, 1)
                    pack = jnp.where(lane == at, moved, pack)
                pack_ref[n, j] = pack
        return carry

    lax.fori_loop(0, NVAR, advance, 0)
    for j in range(CS):
        steps = [
            jnp.sum(jnp.where(lane == at, tau_ref[j], 0.0), axis=1, keepdims=True)
            for at in (outlet, inner)
        ]
        for n in range(6):
            pack_ref[n, j] = pack_ref[n, j] * steps[n // 5]
    second_half = lane >= LANES // 2
    odd = row_ids(tile) % 2 == 1
    spans = bands_ref.shape[1] // CS

    def label(i, carry):
        of_row = i // spans
        cells = [bands_ref[of_row, (i % spans) * CS + j] for j in range(CS)]
        ids_ref[pl.ds(pl.multiple_of(i * CP, CP), CP), :] = jnp.where(
            odd,
            jnp.where(second_half, cells[3], cells[2]),
            jnp.where(second_half, cells[1], cells[0]),
        )
        return carry

    lax.fori_loop(0, 2 * spans, label, 0)
    cells = cell_ref[0, 0]
    for j in range(CS):
        here = row_ids(tile) + CP * j == cells // LANES
        for n, at in enumerate((outlet, inner)):
            seen_ref[n, j] = jnp.where(here & (cells % LANES == at), 1.0, 0.0).astype(F32)
    square = (LANES, LANES)
    picked = (row_ids(square) == owner_ref[0, 0] % LANES).astype(F32).astype(BF16)
    for n in range(3):
        node_ref[:, LANES * n : LANES * (n + 1)] = picked


def settle_edges_kernel(
    part_ref, jac_ref, tau_ref, up_ref, down_ref, left_ref, right_ref, cell_ref,
    part2_ref, face_ref, sides,
):
    keep = inner_sides()
    tile = (CP, LANES)
    fill_sides(sides, left_ref, right_ref)

    def body(c, carry):
        lost = edge_terms(jac_ref, sides, up_ref, down_ref, keep, c)
        for j in range(CS):
            part2_ref[c, j] = part_ref[c, j] - tau_ref[j] * lost[j]
        return carry

    lax.fori_loop(0, NVAR, body, 0)
    cells = cell_ref[0, 0]
    square = (LANES, LANES)
    axial_pick = (row_ids(square) == cells % LANES).astype(F32).astype(BF16)
    picked = dot3(part2_ref[...].reshape(NVAR * CS * CP, LANES), axial_pick, ((1,), (0,)))
    here = row_ids((CS * CP, LANES)) == cells // LANES
    for c in range(NVAR):
        block = picked[c * CS * CP : (c + 1) * CS * CP]
        face_ref[c : c + 1] = jnp.sum(jnp.where(here, block, 0.0), axis=0, keepdims=True)


def cycle_kernel(
    bands_ref, part_ref, rec_ref, pack_ref, ids_ref, all_ref, up_ref, down_ref, left_ref, right_ref,
    seen_ref, node_ref, face_ref, owner_ref, weight_ref, out_ref, dense_ref,
):
    row = lax.axis_index("row")
    span = lax.axis_index("span")
    outlet, inner = outlet_lanes(row)
    keep = inner_sides()
    tile = (CP, LANES)
    lane, sub = lane_ids(tile), row_ids(tile)
    last_cell = bands_ref.shape[1] - 1
    wanted = [
        bands_ref[row, jnp.clip(span * CS - 1 + t, 0, last_cell)] for t in range(CS + 2)
    ]
    half = all_ref.shape[0] // 2
    zero = jnp.zeros(tile, F32)

    def body(i, sums):
        sums = list(sums)
        for n, of_row in enumerate((1 - row, row)):
            at = pl.multiple_of(of_row * half + i * CP, CP)
            ids, values = ids_ref[pl.ds(at, CP), :], all_ref[pl.ds(at, CP), :]
            for t, band in enumerate(wanted):
                k = (CS + 2) * n + t
                sums[k] = sums[k] + jnp.where(ids == band, values, 0.0)
        return tuple(sums)

    sums = lax.fori_loop(0, half // CP, body, (zero,) * (2 * CS + 4), unroll=2)

    def folded(parts):
        rows = [jnp.sum(x, axis=0, keepdims=True) for x in parts]
        whole = jnp.concatenate(rows + [rows[-1]] * (CP - len(rows)), axis=0)
        whole = whole + pltpu.roll(whole, 64, 1)
        return whole, jnp.broadcast_to(whole[:, COUNT_AT : COUNT_AT + 1], tile)

    other, other_count = folded(sums[: CS + 2])
    mine, my_count = folded(sums[CS + 2 :])
    spread0 = spread(other / other_count, 0)
    lost = weight_sum(other * spread(mine / my_count, 0))
    cycle1 = (other - pltpu.roll(lost, LANES - (WEIGHT_AT - FIRST_AT), 1)) / other_count
    spread1 = spread(cycle1, FIRST_AT)

    def shift_of(record, values):
        moved = weight_sum(record * values)
        return moved, spread(moved, WEIGHT_AT)

    own = [shift_of(rec_ref[j], spread0[j + 1 : j + 2]) for j in range(CS)]
    above = shift_of(up_ref[NVAR], spread0[:1])[1] * keep[0]
    below = shift_of(down_ref[NVAR], spread0[CS + 1 : CS + 2])[1] * keep[1]
    left = shift_of(left_ref[NVAR], spread0[1 : 1 + CS])[1]
    right = shift_of(right_ref[NVAR], spread0[1 : 1 + CS])[1]
    changes = []
    for j in range(CS):
        x = own[j][1]
        total = pack_ref[0, j] * x - rec_ref[j] * spread1[j + 1 : j + 2]
        total = total + pack_ref[1, j] * (own[j - 1][1] if j > 0 else above)
        total = total + pack_ref[2, j] * (own[j + 1][1] if j < CS - 1 else below)
        total = total + pack_ref[3, j] * jnp.where(
            sub == 0, jnp.broadcast_to(left[j : j + 1], tile), pltpu.roll(x, 1, 0)
        )
        total = total + pack_ref[4, j] * jnp.where(
            sub == CP - 1, jnp.broadcast_to(right[j : j + 1], tile), pltpu.roll(x, CP - 1, 0)
        )
        changes.append((weight_sum(total) - own[j][0], weight_sum(pack_ref[5, j] * x)))
    terms = [jnp.zeros((1, LANES), F32)] * 3
    for c in range(NVAR):
        at = WEIGHT_AT + c
        seen = zero
        for j in range(CS):
            first, second = (jnp.broadcast_to(x[:, at : at + 1], tile) for x in changes[j])
            moved = jnp.where(lane == outlet, first, jnp.where(lane == inner, second, 0.0))
            out_ref[0, c, j] = part_ref[c, j] + moved
            seen = seen + (seen_ref[0, j] * first + seen_ref[1, j] * second)
        value = face_ref[c : c + 1] + jnp.sum(seen, axis=0, keepdims=True)
        for k in range(3):
            at = NVAR * k + c
            terms[k] = terms[k] + weight_ref[0, 0, 0, at : at + 1] * value
    shape = dense_ref.shape
    line = row_ids(shape)
    device = (line * 43691) >> 17
    here = device == owner_ref[0, 0] // LANES
    cycle_rows = (24, LANES)
    coord = row_ids(cycle_rows) % 3
    pieces = []
    for parts in zip(*(split3(x) for x in terms)):
        wide = [jnp.broadcast_to(x.astype(F32), cycle_rows) for x in parts]
        pattern = jnp.where(coord == 0, wide[0], jnp.where(coord == 1, wide[1], wide[2]))
        pattern = jnp.concatenate([pattern] * (shape[0] // 24), axis=0)
        pieces.append(jnp.where(here, pattern, 0.0).astype(BF16))
    dense_ref[...] = lax.dot_general(
        jnp.concatenate(pieces, axis=1),
        node_ref[...],
        (((1,), (1,)), ((), ())),
        preferred_element_type=F32,
    )


def third_kernel(parts_ref, out_ref):
    folded = jnp.sum(parts_ref[...].reshape(-1, 24, LANES), axis=0)
    coord = row_ids(folded.shape) % 3
    for k in range(3):
        out_ref[k] = jnp.sum(jnp.where(coord == k, folded, 0.0), axis=0, keepdims=True)


VM = pl.BlockSpec(memory_space=pltpu.VMEM)
SM = pl.BlockSpec(memory_space=pltpu.SMEM)
PARAMS = pltpu.CompilerParams(vmem_limit_bytes=32 * 1024 * 1024)


HBM = pl.BlockSpec(memory_space=pltpu.HBM)


def in_hbm(x):
    return pltpu.with_memory_space_constraint(x, pltpu.HBM)


def call(kernel, name, outs, in_specs, scratch=(), cost=None):
    outs = [out if isinstance(out[0], tuple) else (out, F32) for out in outs]
    return pl.pallas_call(
        kernel,
        out_shape=tuple(jax.ShapeDtypeStruct(shape, dtype) for shape, dtype in outs),
        in_specs=in_specs,
        out_specs=(VM,) * len(outs),
        scratch_shapes=list(scratch),
        compiler_params=PARAMS,
        cost_estimate=cost,
        name=name,
    )


def exchange(to_up, to_down, to_left, to_right):
    spans, pitches = lax.axis_size("span"), lax.axis_size("pitch")
    rising = [(i, (i + 1) % spans) for i in range(spans)]
    falling = [((i + 1) % spans, i) for i in range(spans)]
    onward = [(i, (i + 1) % pitches) for i in range(pitches)]
    back = [((i + 1) % pitches, i) for i in range(pitches)]
    return (
        lax.ppermute(to_down, "span", rising),
        lax.ppermute(to_up, "span", falling),
        lax.ppermute(to_right, "pitch", onward),
        lax.ppermute(to_left, "pitch", back),
    )


def on_device(
    adjoint, source, pseudo_step, jac_blocks, band_map, face_cell, face_owner, face_weight
):
    rows, spans, pitches = (lax.axis_size(name) for name in ("row", "span", "pitch"))
    devices = rows * spans * pitches
    peers = spans * pitches
    block = (NVAR, CS, CP, LANES)
    edge = (NVAR, CP, LANES)
    side = (NVAR, CS, LANES)
    edges = call(
        edges_kernel,
        "edges",
        [edge, edge, side, side],
        in_specs=[HBM],
        scratch=[pltpu.SemaphoreType.DMA((4,))],
    )(in_hbm(adjoint))
    halo = exchange(*edges)
    part, record, jac, src, tau = call(
        interior_kernel,
        "interior",
        [block, (CS, CP, LANES), ((7, NVAR) + block, BF16), block, (CS, CP, LANES)],
        in_specs=[HBM] * 4,
        scratch=[
            pltpu.VMEM(block, F32),
            pltpu.VMEM((7 * NVAR, CS, CP, LANES), F32),
            pltpu.VMEM(block, F32),
            pltpu.SemaphoreType.DMA((10,)),
        ],
        cost=pl.CostEstimate(flops=9_000_000, bytes_accessed=3_000_000, transcendentals=0),
    )(*(in_hbm(x) for x in (adjoint, source, pseudo_step, jac_blocks)))
    edge = (NVAR + 1, CP, LANES)
    side = (NVAR + 1, CS, LANES)
    first, message, full_record, *sends = call(
        edge_kernel,
        "edge_update",
        [block, (2 * devices, LANES), (CS, CP, LANES), edge, edge, side, side],
        in_specs=[VM] * 8,
        scratch=[pltpu.VMEM((2 * NVAR, CS, CP, LANES), F32)],
    )(part, record, jac, tau, *halo)
    records = lax.all_to_all(
        message.reshape(devices, 1, 2 * LANES), ("row", "span", "pitch"), 0, 0
    ).reshape(2 * devices, LANES)
    halo = exchange(*sends)
    part, packs, ids, seen, picks = call(
        settle_kernel,
        "settle",
        [
            block, (6, CS, CP, LANES), ((2 * devices, LANES), jnp.int32), (2, CS, CP, LANES),
            ((LANES, 3 * LANES), BF16),
        ],
        in_specs=[SM] + [VM] * 6,
        scratch=[pltpu.VMEM((7 * NVAR, CS, CP, LANES), F32)],
        cost=pl.CostEstimate(flops=9_000_000, bytes_accessed=3_000_000, transcendentals=0),
    )(band_map, first, src, tau, jac, face_cell, face_owner)
    part, faces = call(
        settle_edges_kernel,
        "settle_edges",
        [block, (CP, LANES)],
        in_specs=[VM] * 8,
        scratch=[pltpu.VMEM((2 * NVAR, CS, CP, LANES), F32)],
        cost=pl.CostEstimate(flops=3_000_000, bytes_accessed=2_000_000, transcendentals=0),
    )(part, jac, tau, *halo, face_cell)
    field, dense = call(
        cycle_kernel,
        "cycle_update",
        [(1,) + block, (3 * peers, LANES)],
        in_specs=[SM] + [VM] * 14,
    )(
        band_map, part, full_record, packs, ids, records, *halo, seen, picks, faces, face_owner,
        face_weight,
    )
    parts = lax.all_to_all(dense.reshape(peers, 1, 3 * LANES), ("span", "pitch"), 0, 0)
    (nodes,) = call(third_kernel, "node_sums", [(3, 1, LANES)], in_specs=[VM])(
        parts.reshape(3 * peers, LANES)
    )
    return field, nodes.transpose(1, 0, 2)


def solution(mesh):
    in_specs = (
        P("row", None, "span", "pitch", None),
        P("row", None, "span", "pitch", None),
        P("row", "span", "pitch", None),
        P("row", None, None, None, "span", "pitch", None),
        P(),
        P("row", "span", "pitch", None),
        P("row", "span", "pitch", None),
        P("row", "span", "pitch", None, None),
    )
    out_specs = (P("row", None, "span", "pitch", None), P("row", None, ("span", "pitch")))
    return jax.shard_map(
        on_device, mesh=mesh, in_specs=in_specs, out_specs=out_specs, check_vma=False
    )
```

```python
import jax
import jax.numpy as jnp
from jax import lax
from jax.experimental import pallas as pl
from jax.experimental.pallas import tpu as pltpu
from jax.sharding import PartitionSpec as P

NVAR = 6
CS = 4
CP = 8
LANES = 128
F32 = jnp.float32
BF16 = jnp.bfloat16
FIRST_AT = 8
WEIGHT_AT = 16
COUNT_AT = 6


def lane_ids(shape):
    return lax.broadcasted_iota(jnp.int32, shape, len(shape) - 1)


def row_ids(shape):
    return lax.broadcasted_iota(jnp.int32, shape, len(shape) - 2)


def split3(x):
    hi = x.astype(BF16)
    rest = x - hi.astype(F32)
    mid = rest.astype(BF16)
    low = (rest - mid.astype(F32)).astype(BF16)
    return hi, mid, low


def dot3(x, onehot, dims):
    parts = [
        lax.dot_general(part, onehot, (dims, ((), ())), preferred_element_type=F32)
        for part in split3(x)
    ]
    return parts[0] + (parts[1] + parts[2])


def fill_stencil(vs, field, up, down, left, right, lower, upper):
    tile = (CP, LANES)
    lane, sub = lane_ids(tile), row_ids(tile)
    for d in range(NVAR):
        for j in range(CS):
            x = field(d, j)
            vs[d, j] = x
            vs[6 + d, j] = field(d, j - 1) if j > 0 else up(d)
            vs[12 + d, j] = field(d, j + 1) if j < CS - 1 else down(d)
            vs[18 + d, j] = jnp.where(
                sub == 0, jnp.broadcast_to(left(d, j), tile), pltpu.roll(x, 1, 0)
            )
            vs[24 + d, j] = jnp.where(
                sub == CP - 1, jnp.broadcast_to(right(d, j), tile), pltpu.roll(x, CP - 1, 0)
            )
            vs[30 + d, j] = jnp.where(lane == 0, lower(d, j), pltpu.roll(x, 1, 1))
            vs[36 + d, j] = jnp.where(lane == LANES - 1, upper(d, j), pltpu.roll(x, LANES - 1, 1))


def image_of(jac_ref, vs, c):
    acc = jnp.zeros((CS, CP, LANES), F32)
    for s in range(7):
        for d in range(NVAR):
            acc = acc + jac_ref[s, c, d].astype(F32) * vs[6 * s + d]
    return acc


def edges_kernel(adj_ref, up_ref, down_ref, left_ref, right_ref, sems):
    adj = adj_ref.at[0]
    copies = [
        pltpu.make_async_copy(adj.at[:, 0], up_ref, sems.at[0]),
        pltpu.make_async_copy(adj.at[:, CS - 1], down_ref, sems.at[1]),
        pltpu.make_async_copy(adj.at[:, :, 0], left_ref, sems.at[2]),
        pltpu.make_async_copy(adj.at[:, :, CP - 1], right_ref, sems.at[3]),
    ]
    for copy in copies:
        copy.start()
    for copy in copies:
        copy.wait()


def interior_kernel(
    adj_hbm, src_hbm, tau_hbm, jac_hbm, part_ref, rec_ref, jac_ref, src_ref, tau_ref, adj_ref, vs,
    image, sems,
):
    row = lax.axis_index("row")
    outlet = (1 - row) * (LANES - 1)
    ghost = 6 - row
    tile = (CP, LANES)
    zero = jnp.zeros(tile, F32)
    lane = lane_ids(tile)
    load_adj = pltpu.make_async_copy(adj_hbm.at[0], adj_ref, sems.at[0])
    load_jac = [
        pltpu.make_async_copy(jac_hbm.at[0, s], jac_ref.at[s], sems.at[1 + s]) for s in range(7)
    ]
    load_tau = pltpu.make_async_copy(tau_hbm.at[0], tau_ref, sems.at[8])
    load_src = pltpu.make_async_copy(src_hbm.at[0], src_ref, sems.at[9])
    for copy in [load_adj] + load_jac + [load_tau, load_src]:
        copy.start()
    load_adj.wait()
    fill_stencil(
        vs,
        lambda d, j: adj_ref[d, j],
        lambda d: zero,
        lambda d: zero,
        lambda d, j: zero,
        lambda d, j: zero,
        lambda d, j: zero,
        lambda d, j: zero,
    )
    for s in range(7):
        load_jac[s].wait()

        def apply(c, carry):
            acc = jnp.zeros((CS, CP, LANES), F32) if s == 0 else image[c]
            for d in range(NVAR):
                acc = acc + jac_ref[s, c, d].astype(F32) * vs[6 * s + d]
            image[c] = acc
            return carry

        lax.fori_loop(0, NVAR, apply, 0)
    load_tau.wait()
    load_src.wait()

    def finish(c, carry):
        weights, sums = (list(x) for x in carry)
        f0 = adj_ref[c]
        part_ref[c] = f0 + tau_ref[...] * (src_ref[c] - image[c])
        for j in range(CS):
            for d in range(NVAR):
                at = WEIGHT_AT + 8 * d + c
                moved = pltpu.roll(jac_ref[ghost, c, d, j].astype(F32), at + 1 - row, 1)
                weights[j] = jnp.where(lane == at, moved, weights[j])
            sums[j] = jnp.where(lane == c, pltpu.roll(f0[j], c + 1 - row, 1), sums[j])
        return tuple(weights), tuple(sums)

    ones = jnp.where(lane == COUNT_AT, 1.0, 0.0).astype(F32)
    weights, sums = lax.fori_loop(0, NVAR, finish, ((zero,) * CS, (ones,) * CS))
    for j in range(CS):
        tau_out = jnp.sum(jnp.where(lane == outlet, tau_ref[j], 0.0), axis=1, keepdims=True)
        rec_ref[j] = sums[j] + weights[j] * tau_out


def inner_sides():
    span = lax.axis_index("span")
    return (
        jnp.where(span > 0, 1.0, 0.0).astype(F32),
        jnp.where(span < lax.axis_size("span") - 1, 1.0, 0.0).astype(F32),
    )


def fill_sides(sides, left_ref, right_ref):
    tile = (CP, LANES)
    sub = row_ids(tile)
    for d in range(NVAR):
        for j in range(CS):
            sides[d, j] = jnp.where(
                sub == 0, jnp.broadcast_to(left_ref[d, j : j + 1], tile), 0.0
            )
            sides[NVAR + d, j] = jnp.where(
                sub == CP - 1, jnp.broadcast_to(right_ref[d, j : j + 1], tile), 0.0
            )


def edge_terms(jac_ref, sides, up_ref, down_ref, keep, c):
    acc = jnp.zeros((CS, CP, LANES), F32)
    first = jnp.zeros((CP, LANES), F32)
    last = jnp.zeros((CP, LANES), F32)
    for d in range(NVAR):
        acc = acc + jac_ref[3, c, d].astype(F32) * sides[d]
        acc = acc + jac_ref[4, c, d].astype(F32) * sides[NVAR + d]
        first = first + jac_ref[1, c, d, 0].astype(F32) * up_ref[d]
        last = last + jac_ref[2, c, d, CS - 1].astype(F32) * down_ref[d]
    lost = [acc[j] for j in range(CS)]
    lost[0] = lost[0] + first * keep[0]
    lost[CS - 1] = lost[CS - 1] + last * keep[1]
    return lost


def edge_kernel(
    part_ref, rec_in, jac_ref, tau_ref, up_ref, down_ref, left_ref, right_ref,
    f1_ref, msg_ref, rec, to_up_ref, to_down_ref, to_left_ref, to_right_ref, sides,
):
    row = lax.axis_index("row")
    keep = inner_sides()
    tile = (CP, LANES)
    lane, sub = lane_ids(tile), row_ids(tile)
    fill_sides(sides, left_ref, right_ref)

    def body(c, sums):
        sums = list(sums)
        lost = edge_terms(jac_ref, sides, up_ref, down_ref, keep, c)
        at = FIRST_AT + c
        for j in range(CS):
            new = part_ref[c, j] - tau_ref[j] * lost[j]
            f1_ref[c, j] = new
            sums[j] = jnp.where(lane == at, pltpu.roll(new, at + 1 - row, 1), sums[j])
        return tuple(sums)

    sums = lax.fori_loop(0, NVAR, body, tuple(rec_in[j] for j in range(CS)))
    rows = []
    for j in range(CS):
        rec[j] = sums[j]
        rows.append(jnp.sum(sums[j], axis=0, keepdims=True))
    halves = [
        jnp.broadcast_to(rows[2 * h] + pltpu.roll(rows[2 * h + 1], 64, 1), tile) for h in range(2)
    ]
    packed = jnp.where(sub % 2 == 0, halves[0], halves[1])
    for i in range(msg_ref.shape[0] // CP):
        msg_ref[CP * i : CP * (i + 1)] = packed
    to_up_ref[0:NVAR] = f1_ref[:, 0]
    to_up_ref[NVAR] = rec[0]
    to_down_ref[0:NVAR] = f1_ref[:, CS - 1]
    to_down_ref[NVAR] = rec[CS - 1]
    for c in range(NVAR):
        to_left_ref[c] = f1_ref[c, :, 0, :]
        to_right_ref[c] = f1_ref[c, :, CP - 1, :]
    to_left_ref[NVAR] = rec[:, 0, :]
    to_right_ref[NVAR] = rec[:, CP - 1, :]


def weight_sum(x):
    for by in (32, 16, 8):
        x = x + pltpu.roll(x, LANES - by, 1)
    return x


def spread(values, first):
    lane = lane_ids(values.shape)
    out = jnp.zeros(values.shape, F32)
    for d in range(NVAR):
        at = first + d
        out = jnp.where(
            lane // 8 == d + WEIGHT_AT // 8,
            jnp.broadcast_to(values[:, at : at + 1], values.shape),
            out,
        )
    return out


def outlet_lanes(row):
    return (1 - row) * (LANES - 1), (1 - row) * (LANES - 2) + row


def settle_kernel(
    bands_ref, f1_ref, src_ref, tau_ref, jac_ref, cell_ref, owner_ref,
    part_ref, pack_ref, ids_ref, seen_ref, node_ref, vs,
):
    row = lax.axis_index("row")
    outlet, inner = outlet_lanes(row)
    ghost = 6 - row
    tile = (CP, LANES)
    zero = jnp.zeros(tile, F32)
    lane = lane_ids(tile)
    fill_stencil(
        vs,
        lambda d, j: f1_ref[d, j],
        lambda d: zero,
        lambda d: zero,
        lambda d, j: zero,
        lambda d, j: zero,
        lambda d, j: zero,
        lambda d, j: zero,
    )
    for n in range(6):
        for j in range(CS):
            pack_ref[n, j] = zero

    def advance(c, carry):
        part_ref[c] = f1_ref[c] + tau_ref[...] * (src_ref[c] - image_of(jac_ref, vs, c))
        for n in range(6):
            point = n if n < 5 else ghost
            extra = 1 - row if n < 5 else 2 - 3 * row
            for j in range(CS):
                pack = pack_ref[n, j]
                for d in range(NVAR):
                    at = WEIGHT_AT + 8 * d + c
                    moved = pltpu.roll(jac_ref[point, c, d, j].astype(F32), at + extra, 1)
                    pack = jnp.where(lane == at, moved, pack)
                pack_ref[n, j] = pack
        return carry

    lax.fori_loop(0, NVAR, advance, 0)
    for j in range(CS):
        steps = [
            jnp.sum(jnp.where(lane == at, tau_ref[j], 0.0), axis=1, keepdims=True)
            for at in (outlet, inner)
        ]
        for n in range(6):
            pack_ref[n, j] = pack_ref[n, j] * steps[n // 5]
    square = (LANES, LANES)
    lines = ids_ref.shape[0] // 2
    even_cell = (lane_ids((lines, LANES)) == 2 * row_ids((lines, LANES))).astype(F32).astype(BF16)
    for of_row in range(2):
        bands = bands_ref[of_row : of_row + 1].astype(F32)
        pair = jnp.where(
            row_ids(square) < LANES // 2,
            jnp.broadcast_to(bands, square),
            jnp.broadcast_to(pltpu.roll(bands, LANES - 1, 1), square),
        )
        ids_ref[lines * of_row : lines * (of_row + 1)] = lax.dot_general(
            even_cell, pair.astype(BF16), (((1,), (1,)), ((), ())), preferred_element_type=F32
        )
    cells = cell_ref[0, 0]
    for j in range(CS):
        here = row_ids(tile) + CP * j == cells // LANES
        for n, at in enumerate((outlet, inner)):
            seen_ref[n, j] = jnp.where(here & (cells % LANES == at), 1.0, 0.0).astype(F32)
    picked = (row_ids(square) == owner_ref[0, 0] % LANES).astype(F32).astype(BF16)
    for n in range(3):
        node_ref[:, LANES * n : LANES * (n + 1)] = picked


def settle_edges_kernel(
    part_ref, jac_ref, tau_ref, up_ref, down_ref, left_ref, right_ref, cell_ref,
    part2_ref, face_ref, sides,
):
    keep = inner_sides()
    tile = (CP, LANES)
    fill_sides(sides, left_ref, right_ref)

    def body(c, carry):
        lost = edge_terms(jac_ref, sides, up_ref, down_ref, keep, c)
        for j in range(CS):
            part2_ref[c, j] = part_ref[c, j] - tau_ref[j] * lost[j]
        return carry

    lax.fori_loop(0, NVAR, body, 0)
    cells = cell_ref[0, 0]
    square = (LANES, LANES)
    axial_pick = (row_ids(square) == cells % LANES).astype(F32).astype(BF16)
    picked = dot3(part2_ref[...].reshape(NVAR * CS * CP, LANES), axial_pick, ((1,), (0,)))
    here = row_ids((CS * CP, LANES)) == cells // LANES
    for c in range(NVAR):
        block = picked[c * CS * CP : (c + 1) * CS * CP]
        face_ref[c : c + 1] = jnp.sum(jnp.where(here, block, 0.0), axis=0, keepdims=True)


def bands_kernel(
    bands_ref, ids_ref, all_ref, to_left_ref, to_right_ref, sum_ref, left_ref, right_ref
):
    row = lax.axis_index("row")
    span = lax.axis_index("span")
    tile = (CP, LANES)
    last_cell = bands_ref.shape[1] - 1
    wanted = [
        bands_ref[row, jnp.clip(span * CS - 1 + t, 0, last_cell)].astype(F32)
        for t in range(CS + 2)
    ]
    half = all_ref.shape[0] // 2

    def folded(of_row):
        sums = [jnp.zeros(tile, F32)] * (CS + 2)
        for i in range(half // CP):
            at = pl.multiple_of(of_row * half + i * CP, CP)
            ids, values = ids_ref[pl.ds(at, CP), :], all_ref[pl.ds(at, CP), :]
            sums = [x + jnp.where(ids == band, values, 0.0) for x, band in zip(sums, wanted)]
        rows = [jnp.sum(x, axis=0, keepdims=True) for x in sums]
        whole = jnp.concatenate(rows + [rows[-1]] * (CP - len(rows)), axis=0)
        return whole + pltpu.roll(whole, 64, 1)

    total = jnp.where(lane_ids(tile) < LANES // 2, folded(1 - row), folded(row))
    sum_ref[...] = total
    for out_ref, in_ref in ((left_ref, to_left_ref), (right_ref, to_right_ref)):
        out_ref[: NVAR + 1] = in_ref[...]
        out_ref[NVAR + 1] = total[:CS]
        out_ref[NVAR + 2] = total[CS:]


def cycle_kernel(
    part_ref, rec_ref, pack_ref, sum_ref, far_ref, up_ref, down_ref, left_ref, right_ref,
    seen_ref, node_ref, face_ref, owner_ref, weight_ref, out_hbm, dense_ref, field, sem,
):
    row = lax.axis_index("row")
    outlet, inner = outlet_lanes(row)
    keep = inner_sides()
    tile = (CP, LANES)
    lane, sub = lane_ids(tile), row_ids(tile)
    zero = jnp.zeros(tile, F32)
    sides = [
        jnp.concatenate([ref[NVAR + 1], ref[NVAR + 2]], axis=0) for ref in (left_ref, right_ref)
    ]
    other = (sum_ref[...] + far_ref[...]) + (sides[0] + sides[1])
    mine = pltpu.roll(other, LANES // 2, 1)
    other_count, my_count = (
        jnp.broadcast_to(x[:, COUNT_AT : COUNT_AT + 1], tile) for x in (other, mine)
    )
    spread0 = spread(other / other_count, 0)
    lost = weight_sum(other * spread(mine / my_count, 0))
    cycle1 = (other - pltpu.roll(lost, LANES - (WEIGHT_AT - FIRST_AT), 1)) / other_count
    spread1 = spread(cycle1, FIRST_AT)

    def shift_of(record, values):
        moved = weight_sum(record * values)
        return moved, spread(moved, WEIGHT_AT)

    own = [shift_of(rec_ref[j], spread0[j + 1 : j + 2]) for j in range(CS)]
    above = shift_of(up_ref[NVAR], spread0[:1])[1] * keep[0]
    below = shift_of(down_ref[NVAR], spread0[CS + 1 : CS + 2])[1] * keep[1]
    left = shift_of(left_ref[NVAR], spread0[1 : 1 + CS])[1]
    right = shift_of(right_ref[NVAR], spread0[1 : 1 + CS])[1]
    changes = []
    for j in range(CS):
        x = own[j][1]
        total = pack_ref[0, j] * x - rec_ref[j] * spread1[j + 1 : j + 2]
        total = total + pack_ref[1, j] * (own[j - 1][1] if j > 0 else above)
        total = total + pack_ref[2, j] * (own[j + 1][1] if j < CS - 1 else below)
        total = total + pack_ref[3, j] * jnp.where(
            sub == 0, jnp.broadcast_to(left[j : j + 1], tile), pltpu.roll(x, 1, 0)
        )
        total = total + pack_ref[4, j] * jnp.where(
            sub == CP - 1, jnp.broadcast_to(right[j : j + 1], tile), pltpu.roll(x, CP - 1, 0)
        )
        changes.append((weight_sum(total) - own[j][0], weight_sum(pack_ref[5, j] * x)))
    terms = [jnp.zeros((1, LANES), F32)] * 3
    for c in range(NVAR):
        at = WEIGHT_AT + c
        seen = zero
        for j in range(CS):
            first, second = (jnp.broadcast_to(x[:, at : at + 1], tile) for x in changes[j])
            moved = jnp.where(lane == outlet, first, jnp.where(lane == inner, second, 0.0))
            field[0, c, j] = part_ref[c, j] + moved
            seen = seen + (seen_ref[0, j] * first + seen_ref[1, j] * second)
        value = face_ref[c : c + 1] + jnp.sum(seen, axis=0, keepdims=True)
        for k in range(3):
            at = NVAR * k + c
            terms[k] = terms[k] + weight_ref[0, 0, 0, at : at + 1] * value
    write = pltpu.make_async_copy(field, out_hbm, sem)
    write.start()
    shape = dense_ref.shape
    line = row_ids(shape)
    device = (line * 43691) >> 17
    here = device == owner_ref[0, 0] // LANES
    cycle_rows = (24, LANES)
    coord = row_ids(cycle_rows) % 3
    pieces = []
    for parts in zip(*(split3(x) for x in terms)):
        wide = [jnp.broadcast_to(x.astype(F32), cycle_rows) for x in parts]
        pattern = jnp.where(coord == 0, wide[0], jnp.where(coord == 1, wide[1], wide[2]))
        pattern = jnp.concatenate([pattern] * (shape[0] // 24), axis=0)
        pieces.append(jnp.where(here, pattern, 0.0).astype(BF16))
    dense_ref[...] = lax.dot_general(
        jnp.concatenate(pieces, axis=1),
        node_ref[...],
        (((1,), (1,)), ((), ())),
        preferred_element_type=F32,
    )
    write.wait()


def third_kernel(parts_ref, out_ref):
    folded = jnp.sum(parts_ref[...].reshape(-1, 24, LANES), axis=0)
    coord = row_ids(folded.shape) % 3
    for k in range(3):
        out_ref[k] = jnp.sum(jnp.where(coord == k, folded, 0.0), axis=0, keepdims=True)


VM = pl.BlockSpec(memory_space=pltpu.VMEM)
SM = pl.BlockSpec(memory_space=pltpu.SMEM)
PARAMS = pltpu.CompilerParams(vmem_limit_bytes=32 * 1024 * 1024)


HBM = pl.BlockSpec(memory_space=pltpu.HBM)


def in_hbm(x):
    return pltpu.with_memory_space_constraint(x, pltpu.HBM)


def call(kernel, name, outs, in_specs, scratch=(), cost=None, out_specs=None):
    outs = [out if isinstance(out[0], tuple) else (out, F32) for out in outs]
    return pl.pallas_call(
        kernel,
        out_shape=tuple(jax.ShapeDtypeStruct(shape, dtype) for shape, dtype in outs),
        in_specs=in_specs,
        out_specs=out_specs or (VM,) * len(outs),
        scratch_shapes=list(scratch),
        compiler_params=PARAMS,
        cost_estimate=cost,
        name=name,
    )


def shifted(value, axis, by):
    devices = lax.axis_size(axis)
    return lax.ppermute(value, axis, [(i, (i + by) % devices) for i in range(devices)])


def over_span(to_up, to_down):
    return shifted(to_down, "span", 1), shifted(to_up, "span", -1)


def over_pitch(to_left, to_right):
    return shifted(to_right, "pitch", 1), shifted(to_left, "pitch", -1)


def on_device(
    adjoint, source, pseudo_step, jac_blocks, band_map, face_cell, face_owner, face_weight
):
    rows, spans, pitches = (lax.axis_size(name) for name in ("row", "span", "pitch"))
    groups = rows * spans
    peers = spans * pitches
    block = (NVAR, CS, CP, LANES)
    edge = (NVAR, CP, LANES)
    side = (NVAR, CS, LANES)
    edges = call(
        edges_kernel,
        "edges",
        [edge, edge, side, side],
        in_specs=[HBM],
        scratch=[pltpu.SemaphoreType.DMA((4,))],
    )(in_hbm(adjoint))
    halo = over_span(*edges[:2]) + over_pitch(*edges[2:])
    part, record, jac, src, tau = call(
        interior_kernel,
        "interior",
        [block, (CS, CP, LANES), ((7, NVAR) + block, BF16), block, (CS, CP, LANES)],
        in_specs=[HBM] * 4,
        scratch=[
            pltpu.VMEM(block, F32),
            pltpu.VMEM((7 * NVAR, CS, CP, LANES), F32),
            pltpu.VMEM(block, F32),
            pltpu.SemaphoreType.DMA((10,)),
        ],
        cost=pl.CostEstimate(flops=9_000_000, bytes_accessed=3_000_000, transcendentals=0),
    )(*(in_hbm(x) for x in (adjoint, source, pseudo_step, jac_blocks)))
    edge = (NVAR + 1, CP, LANES)
    side = (NVAR + 1, CS, LANES)
    first, message, full_record, *sends = call(
        edge_kernel,
        "edge_update",
        [block, (2 * groups, LANES), (CS, CP, LANES), edge, edge, side, side],
        in_specs=[VM] * 8,
        scratch=[pltpu.VMEM((2 * NVAR, CS, CP, LANES), F32)],
    )(part, record, jac, tau, *halo)
    records = lax.all_to_all(
        message.reshape(groups, 1, 2 * LANES), ("row", "span"), 0, 0
    ).reshape(2 * groups, LANES)
    halo = over_span(*sends[:2])
    part, packs, ids, seen, picks = call(
        settle_kernel,
        "settle",
        [
            block, (6, CS, CP, LANES), ((2 * groups, LANES), F32), (2, CS, CP, LANES),
            ((LANES, 3 * LANES), BF16),
        ],
        in_specs=[VM] * 7,
        scratch=[pltpu.VMEM((7 * NVAR, CS, CP, LANES), F32)],
        cost=pl.CostEstimate(flops=9_000_000, bytes_accessed=3_000_000, transcendentals=0),
    )(band_map, first, src, tau, jac, face_cell, face_owner)
    tail = (NVAR + 3, CS, LANES)
    sums, *sides = call(
        bands_kernel, "band_sums", [(CP, LANES), tail, tail], in_specs=[SM] + [VM] * 4
    )(band_map, ids, records, *sends[2:])
    halo = halo + over_pitch(*sides)
    far = shifted(sums, "pitch", 2)
    part, faces = call(
        settle_edges_kernel,
        "settle_edges",
        [block, (CP, LANES)],
        in_specs=[VM] * 8,
        scratch=[pltpu.VMEM((2 * NVAR, CS, CP, LANES), F32)],
        cost=pl.CostEstimate(flops=3_000_000, bytes_accessed=2_000_000, transcendentals=0),
    )(part, jac, tau, *halo, face_cell)
    field, dense = call(
        cycle_kernel,
        "cycle_update",
        [(1,) + block, (3 * peers, LANES)],
        in_specs=[VM] * 14,
        out_specs=(HBM, VM),
        scratch=[pltpu.VMEM((1,) + block, F32), pltpu.SemaphoreType.DMA],
    )(
        part, full_record, packs, sums, far, *halo, seen, picks, faces, face_owner, face_weight,
    )
    parts = lax.all_to_all(dense.reshape(peers, 1, 3 * LANES), ("span", "pitch"), 0, 0)
    (nodes,) = call(third_kernel, "node_sums", [(3, 1, LANES)], in_specs=[VM])(
        parts.reshape(3 * peers, LANES)
    )
    return field, nodes.transpose(1, 0, 2)


def solution(mesh):
    in_specs = (
        P("row", None, "span", "pitch", None),
        P("row", None, "span", "pitch", None),
        P("row", "span", "pitch", None),
        P("row", None, None, None, "span", "pitch", None),
        P(),
        P("row", "span", "pitch", None),
        P("row", "span", "pitch", None),
        P("row", "span", "pitch", None, None),
    )
    out_specs = (P("row", None, "span", "pitch", None), P("row", None, ("span", "pitch")))
    return jax.shard_map(
        on_device, mesh=mesh, in_specs=in_specs, out_specs=out_specs, check_vma=False
    )
```

```python
import jax
import jax.numpy as jnp
from jax import lax
from jax.experimental import pallas as pl
from jax.experimental.pallas import tpu as pltpu
from jax.sharding import PartitionSpec as P

NVAR = 6
CS = 4
CP = 8
LANES = 128
F32 = jnp.float32
BF16 = jnp.bfloat16
FIRST_AT = 8
WEIGHT_AT = 16
COUNT_AT = 6


def lane_ids(shape):
    return lax.broadcasted_iota(jnp.int32, shape, len(shape) - 1)


def row_ids(shape):
    return lax.broadcasted_iota(jnp.int32, shape, len(shape) - 2)


def split3(x):
    hi = x.astype(BF16)
    rest = x - hi.astype(F32)
    mid = rest.astype(BF16)
    low = (rest - mid.astype(F32)).astype(BF16)
    return hi, mid, low


def dot3(x, onehot, dims):
    parts = [
        lax.dot_general(part, onehot, (dims, ((), ())), preferred_element_type=F32)
        for part in split3(x)
    ]
    return parts[0] + (parts[1] + parts[2])


def fill_stencil(vs, field, up, down, left, right, lower, upper):
    tile = (CP, LANES)
    lane, sub = lane_ids(tile), row_ids(tile)
    for d in range(NVAR):
        for j in range(CS):
            x = field(d, j)
            vs[d, j] = x
            vs[6 + d, j] = field(d, j - 1) if j > 0 else up(d)
            vs[12 + d, j] = field(d, j + 1) if j < CS - 1 else down(d)
            vs[18 + d, j] = jnp.where(
                sub == 0, jnp.broadcast_to(left(d, j), tile), pltpu.roll(x, 1, 0)
            )
            vs[24 + d, j] = jnp.where(
                sub == CP - 1, jnp.broadcast_to(right(d, j), tile), pltpu.roll(x, CP - 1, 0)
            )
            vs[30 + d, j] = jnp.where(lane == 0, lower(d, j), pltpu.roll(x, 1, 1))
            vs[36 + d, j] = jnp.where(lane == LANES - 1, upper(d, j), pltpu.roll(x, LANES - 1, 1))


def image_of(jac_ref, vs, c):
    acc = jnp.zeros((CS, CP, LANES), F32)
    for s in range(7):
        for d in range(NVAR):
            acc = acc + jac_ref[s, c, d].astype(F32) * vs[6 * s + d]
    return acc


def edges_kernel(adj_ref, up_ref, down_ref, left_ref, right_ref, sems):
    adj = adj_ref.at[0]
    copies = [
        pltpu.make_async_copy(adj.at[:, 0], up_ref, sems.at[0]),
        pltpu.make_async_copy(adj.at[:, CS - 1], down_ref, sems.at[1]),
        pltpu.make_async_copy(adj.at[:, :, 0], left_ref, sems.at[2]),
        pltpu.make_async_copy(adj.at[:, :, CP - 1], right_ref, sems.at[3]),
    ]
    for copy in copies:
        copy.start()
    for copy in copies:
        copy.wait()


def interior_kernel(
    adj_hbm, src_hbm, tau_hbm, jac_hbm, part_ref, rec_ref, jac_ref, src_ref, tau_ref, adj_ref, vs,
    image, sems,
):
    row = lax.axis_index("row")
    outlet = (1 - row) * (LANES - 1)
    ghost = 6 - row
    tile = (CP, LANES)
    zero = jnp.zeros(tile, F32)
    lane = lane_ids(tile)
    load_adj = pltpu.make_async_copy(adj_hbm.at[0], adj_ref, sems.at[0])
    load_jac = [
        pltpu.make_async_copy(jac_hbm.at[0, s], jac_ref.at[s], sems.at[1 + s]) for s in range(7)
    ]
    load_tau = pltpu.make_async_copy(tau_hbm.at[0], tau_ref, sems.at[8])
    load_src = pltpu.make_async_copy(src_hbm.at[0], src_ref, sems.at[9])
    for copy in [load_adj] + load_jac + [load_tau, load_src]:
        copy.start()
    load_adj.wait()
    fill_stencil(
        vs,
        lambda d, j: adj_ref[d, j],
        lambda d: zero,
        lambda d: zero,
        lambda d, j: zero,
        lambda d, j: zero,
        lambda d, j: zero,
        lambda d, j: zero,
    )
    for s in range(7):
        load_jac[s].wait()

        def apply(c, carry):
            acc = jnp.zeros((CS, CP, LANES), F32) if s == 0 else image[c]
            for d in range(NVAR):
                acc = acc + jac_ref[s, c, d].astype(F32) * vs[6 * s + d]
            image[c] = acc
            return carry

        lax.fori_loop(0, NVAR, apply, 0)
    load_tau.wait()
    load_src.wait()

    def finish(c, carry):
        weights, sums = (list(x) for x in carry)
        f0 = adj_ref[c]
        part_ref[c] = f0 + tau_ref[...] * (src_ref[c] - image[c])
        for j in range(CS):
            for d in range(NVAR):
                at = WEIGHT_AT + 8 * d + c
                moved = pltpu.roll(jac_ref[ghost, c, d, j].astype(F32), at + 1 - row, 1)
                weights[j] = jnp.where(lane == at, moved, weights[j])
            sums[j] = jnp.where(lane == c, pltpu.roll(f0[j], c + 1 - row, 1), sums[j])
        return tuple(weights), tuple(sums)

    ones = jnp.where(lane == COUNT_AT, 1.0, 0.0).astype(F32)
    weights, sums = lax.fori_loop(0, NVAR, finish, ((zero,) * CS, (ones,) * CS))
    for j in range(CS):
        tau_out = jnp.sum(jnp.where(lane == outlet, tau_ref[j], 0.0), axis=1, keepdims=True)
        rec_ref[j] = sums[j] + weights[j] * tau_out


def inner_sides():
    span = lax.axis_index("span")
    return (
        jnp.where(span > 0, 1.0, 0.0).astype(F32),
        jnp.where(span < lax.axis_size("span") - 1, 1.0, 0.0).astype(F32),
    )


def fill_sides(sides, left_ref, right_ref):
    tile = (CP, LANES)
    sub = row_ids(tile)
    for d in range(NVAR):
        for j in range(CS):
            sides[d, j] = jnp.where(
                sub == 0, jnp.broadcast_to(left_ref[d, j : j + 1], tile), 0.0
            )
            sides[NVAR + d, j] = jnp.where(
                sub == CP - 1, jnp.broadcast_to(right_ref[d, j : j + 1], tile), 0.0
            )


def edge_terms(jac_ref, sides, up_ref, down_ref, keep, c):
    acc = jnp.zeros((CS, CP, LANES), F32)
    first = jnp.zeros((CP, LANES), F32)
    last = jnp.zeros((CP, LANES), F32)
    for d in range(NVAR):
        acc = acc + jac_ref[3, c, d].astype(F32) * sides[d]
        acc = acc + jac_ref[4, c, d].astype(F32) * sides[NVAR + d]
        first = first + jac_ref[1, c, d, 0].astype(F32) * up_ref[d]
        last = last + jac_ref[2, c, d, CS - 1].astype(F32) * down_ref[d]
    lost = [acc[j] for j in range(CS)]
    lost[0] = lost[0] + first * keep[0]
    lost[CS - 1] = lost[CS - 1] + last * keep[1]
    return lost


def edge_kernel(
    part_ref, rec_in, jac_ref, tau_ref, up_ref, down_ref, left_ref, right_ref,
    f1_ref, msg_ref, rec, to_up_ref, to_down_ref, to_left_ref, to_right_ref, sides,
):
    row = lax.axis_index("row")
    keep = inner_sides()
    tile = (CP, LANES)
    lane, sub = lane_ids(tile), row_ids(tile)
    fill_sides(sides, left_ref, right_ref)

    def body(c, sums):
        sums = list(sums)
        lost = edge_terms(jac_ref, sides, up_ref, down_ref, keep, c)
        at = FIRST_AT + c
        for j in range(CS):
            new = part_ref[c, j] - tau_ref[j] * lost[j]
            f1_ref[c, j] = new
            sums[j] = jnp.where(lane == at, pltpu.roll(new, at + 1 - row, 1), sums[j])
        return tuple(sums)

    sums = lax.fori_loop(0, NVAR, body, tuple(rec_in[j] for j in range(CS)))
    rows = []
    for j in range(CS):
        rec[j] = sums[j]
        rows.append(jnp.sum(sums[j], axis=0, keepdims=True))
    halves = [
        jnp.broadcast_to(rows[2 * h] + pltpu.roll(rows[2 * h + 1], 64, 1), tile) for h in range(2)
    ]
    packed = jnp.where(sub % 2 == 0, halves[0], halves[1])
    for i in range(msg_ref.shape[0] // CP):
        msg_ref[CP * i : CP * (i + 1)] = packed
    to_up_ref[0:NVAR] = f1_ref[:, 0]
    to_up_ref[NVAR] = rec[0]
    to_down_ref[0:NVAR] = f1_ref[:, CS - 1]
    to_down_ref[NVAR] = rec[CS - 1]
    for c in range(NVAR):
        to_left_ref[c] = f1_ref[c, :, 0, :]
        to_right_ref[c] = f1_ref[c, :, CP - 1, :]
    to_left_ref[NVAR] = rec[:, 0, :]
    to_right_ref[NVAR] = rec[:, CP - 1, :]


def weight_sum(x):
    for by in (32, 16, 8):
        x = x + pltpu.roll(x, LANES - by, 1)
    return x


def spread(values, first):
    lane = lane_ids(values.shape)
    out = jnp.zeros(values.shape, F32)
    for d in range(NVAR):
        at = first + d
        out = jnp.where(
            lane // 8 == d + WEIGHT_AT // 8,
            jnp.broadcast_to(values[:, at : at + 1], values.shape),
            out,
        )
    return out


def outlet_lanes(row):
    return (1 - row) * (LANES - 1), (1 - row) * (LANES - 2) + row


def settle_kernel(
    bands_ref, f1_ref, src_ref, tau_ref, jac_ref, cell_ref, owner_ref,
    part_ref, pack_ref, ids_ref, seen_ref, node_ref, vs,
):
    row = lax.axis_index("row")
    outlet, inner = outlet_lanes(row)
    ghost = 6 - row
    tile = (CP, LANES)
    zero = jnp.zeros(tile, F32)
    lane = lane_ids(tile)
    fill_stencil(
        vs,
        lambda d, j: f1_ref[d, j],
        lambda d: zero,
        lambda d: zero,
        lambda d, j: zero,
        lambda d, j: zero,
        lambda d, j: zero,
        lambda d, j: zero,
    )
    for n in range(6):
        for j in range(CS):
            pack_ref[n, j] = zero

    def advance(c, carry):
        part_ref[c] = f1_ref[c] + tau_ref[...] * (src_ref[c] - image_of(jac_ref, vs, c))
        for n in range(6):
            point = n if n < 5 else ghost
            extra = 1 - row if n < 5 else 2 - 3 * row
            for j in range(CS):
                pack = pack_ref[n, j]
                for d in range(NVAR):
                    at = WEIGHT_AT + 8 * d + c
                    moved = pltpu.roll(jac_ref[point, c, d, j].astype(F32), at + extra, 1)
                    pack = jnp.where(lane == at, moved, pack)
                pack_ref[n, j] = pack
        return carry

    lax.fori_loop(0, NVAR, advance, 0)
    for j in range(CS):
        steps = [
            jnp.sum(jnp.where(lane == at, tau_ref[j], 0.0), axis=1, keepdims=True)
            for at in (outlet, inner)
        ]
        for n in range(6):
            pack_ref[n, j] = pack_ref[n, j] * steps[n // 5]
    square = (LANES, LANES)
    lines = ids_ref.shape[0] // 2
    line = row_ids((lines, LANES))
    first_cell = CS * (line // CP) + 2 * (line % 2)
    even_cell = (lane_ids((lines, LANES)) == first_cell).astype(F32).astype(BF16)
    for of_row in range(2):
        bands = bands_ref[of_row : of_row + 1].astype(F32)
        pair = jnp.where(
            row_ids(square) < LANES // 2,
            jnp.broadcast_to(bands, square),
            jnp.broadcast_to(pltpu.roll(bands, LANES - 1, 1), square),
        )
        ids_ref[lines * of_row : lines * (of_row + 1)] = lax.dot_general(
            even_cell, pair.astype(BF16), (((1,), (1,)), ((), ())), preferred_element_type=F32
        )
    cells = cell_ref[0, 0]
    for j in range(CS):
        here = row_ids(tile) + CP * j == cells // LANES
        for n, at in enumerate((outlet, inner)):
            seen_ref[n, j] = jnp.where(here & (cells % LANES == at), 1.0, 0.0).astype(F32)
    picked = (row_ids(square) == owner_ref[0, 0] % LANES).astype(F32).astype(BF16)
    for n in range(3):
        node_ref[:, LANES * n : LANES * (n + 1)] = picked


def settle_edges_kernel(
    part_ref, jac_ref, tau_ref, up_ref, down_ref, left_ref, right_ref, cell_ref,
    part2_ref, face_ref, sides,
):
    keep = inner_sides()
    tile = (CP, LANES)
    fill_sides(sides, left_ref, right_ref)

    def body(c, carry):
        lost = edge_terms(jac_ref, sides, up_ref, down_ref, keep, c)
        for j in range(CS):
            part2_ref[c, j] = part_ref[c, j] - tau_ref[j] * lost[j]
        return carry

    lax.fori_loop(0, NVAR, body, 0)
    cells = cell_ref[0, 0]
    square = (LANES, LANES)
    axial_pick = (row_ids(square) == cells % LANES).astype(F32).astype(BF16)
    picked = dot3(part2_ref[...].reshape(NVAR * CS * CP, LANES), axial_pick, ((1,), (0,)))
    here = row_ids((CS * CP, LANES)) == cells // LANES
    for c in range(NVAR):
        block = picked[c * CS * CP : (c + 1) * CS * CP]
        face_ref[c : c + 1] = jnp.sum(jnp.where(here, block, 0.0), axis=0, keepdims=True)


def cycle_kernel(
    bands_ref, part_ref, rec_ref, pack_ref, ids_ref, all_ref, up_ref, down_ref, left_ref, right_ref,
    seen_ref, node_ref, face_ref, owner_ref, weight_ref, out_hbm, dense_ref, field, sem,
):
    row = lax.axis_index("row")
    span = lax.axis_index("span")
    outlet, inner = outlet_lanes(row)
    keep = inner_sides()
    tile = (CP, LANES)
    lane, sub = lane_ids(tile), row_ids(tile)
    last_cell = bands_ref.shape[1] - 1
    wanted = [
        bands_ref[row, jnp.clip(span * CS - 1 + t, 0, last_cell)].astype(F32)
        for t in range(CS + 2)
    ]
    half = all_ref.shape[0] // 2
    zero = jnp.zeros(tile, F32)

    def body(i, sums):
        sums = list(sums)
        for n, of_row in enumerate((1 - row, row)):
            at = pl.multiple_of(of_row * half + i * CP, CP)
            ids, values = ids_ref[pl.ds(at, CP), :], all_ref[pl.ds(at, CP), :]
            for t, band in enumerate(wanted):
                k = (CS + 2) * n + t
                sums[k] = sums[k] + jnp.where(ids == band, values, 0.0)
        return tuple(sums)

    sums = lax.fori_loop(0, half // CP, body, (zero,) * (2 * CS + 4), unroll=4)

    def folded(parts):
        rows = [jnp.sum(x, axis=0, keepdims=True) for x in parts]
        whole = jnp.concatenate(rows + [rows[-1]] * (CP - len(rows)), axis=0)
        whole = whole + pltpu.roll(whole, 64, 1)
        return whole, jnp.broadcast_to(whole[:, COUNT_AT : COUNT_AT + 1], tile)

    other, other_count = folded(sums[: CS + 2])
    mine, my_count = folded(sums[CS + 2 :])
    spread0 = spread(other / other_count, 0)
    lost = weight_sum(other * spread(mine / my_count, 0))
    cycle1 = (other - pltpu.roll(lost, LANES - (WEIGHT_AT - FIRST_AT), 1)) / other_count
    spread1 = spread(cycle1, FIRST_AT)

    def shift_of(record, values):
        moved = weight_sum(record * values)
        return moved, spread(moved, WEIGHT_AT)

    own = [shift_of(rec_ref[j], spread0[j + 1 : j + 2]) for j in range(CS)]
    above = shift_of(up_ref[NVAR], spread0[:1])[1] * keep[0]
    below = shift_of(down_ref[NVAR], spread0[CS + 1 : CS + 2])[1] * keep[1]
    left = shift_of(left_ref[NVAR], spread0[1 : 1 + CS])[1]
    right = shift_of(right_ref[NVAR], spread0[1 : 1 + CS])[1]
    changes = []
    for j in range(CS):
        x = own[j][1]
        total = pack_ref[0, j] * x - rec_ref[j] * spread1[j + 1 : j + 2]
        total = total + pack_ref[1, j] * (own[j - 1][1] if j > 0 else above)
        total = total + pack_ref[2, j] * (own[j + 1][1] if j < CS - 1 else below)
        total = total + pack_ref[3, j] * jnp.where(
            sub == 0, jnp.broadcast_to(left[j : j + 1], tile), pltpu.roll(x, 1, 0)
        )
        total = total + pack_ref[4, j] * jnp.where(
            sub == CP - 1, jnp.broadcast_to(right[j : j + 1], tile), pltpu.roll(x, CP - 1, 0)
        )
        changes.append((weight_sum(total) - own[j][0], weight_sum(pack_ref[5, j] * x)))
    terms = [jnp.zeros((1, LANES), F32)] * 3
    for c in range(NVAR):
        at = WEIGHT_AT + c
        seen = zero
        for j in range(CS):
            first, second = (jnp.broadcast_to(x[:, at : at + 1], tile) for x in changes[j])
            moved = jnp.where(lane == outlet, first, jnp.where(lane == inner, second, 0.0))
            field[0, c, j] = part_ref[c, j] + moved
            seen = seen + (seen_ref[0, j] * first + seen_ref[1, j] * second)
        value = face_ref[c : c + 1] + jnp.sum(seen, axis=0, keepdims=True)
        for k in range(3):
            at = NVAR * k + c
            terms[k] = terms[k] + weight_ref[0, 0, 0, at : at + 1] * value
    write = pltpu.make_async_copy(field, out_hbm, sem)
    write.start()
    shape = dense_ref.shape
    line = row_ids(shape)
    device = (line * 43691) >> 17
    here = device == owner_ref[0, 0] // LANES
    cycle_rows = (24, LANES)
    coord = row_ids(cycle_rows) % 3
    pieces = []
    for parts in zip(*(split3(x) for x in terms)):
        wide = [jnp.broadcast_to(x.astype(F32), cycle_rows) for x in parts]
        pattern = jnp.where(coord == 0, wide[0], jnp.where(coord == 1, wide[1], wide[2]))
        pattern = jnp.concatenate([pattern] * (shape[0] // 24), axis=0)
        pieces.append(jnp.where(here, pattern, 0.0).astype(BF16))
    dense_ref[...] = lax.dot_general(
        jnp.concatenate(pieces, axis=1),
        node_ref[...],
        (((1,), (1,)), ((), ())),
        preferred_element_type=F32,
    )
    write.wait()


def third_kernel(parts_ref, out_ref):
    folded = jnp.sum(parts_ref[...].reshape(-1, 24, LANES), axis=0)
    coord = row_ids(folded.shape) % 3
    for k in range(3):
        out_ref[k] = jnp.sum(jnp.where(coord == k, folded, 0.0), axis=0, keepdims=True)


VM = pl.BlockSpec(memory_space=pltpu.VMEM)
SM = pl.BlockSpec(memory_space=pltpu.SMEM)
PARAMS = pltpu.CompilerParams(vmem_limit_bytes=32 * 1024 * 1024)


HBM = pl.BlockSpec(memory_space=pltpu.HBM)


def in_hbm(x):
    return pltpu.with_memory_space_constraint(x, pltpu.HBM)


def call(kernel, name, outs, in_specs, scratch=(), cost=None, out_specs=None):
    outs = [out if isinstance(out[0], tuple) else (out, F32) for out in outs]
    return pl.pallas_call(
        kernel,
        out_shape=tuple(jax.ShapeDtypeStruct(shape, dtype) for shape, dtype in outs),
        in_specs=in_specs,
        out_specs=out_specs or (VM,) * len(outs),
        scratch_shapes=list(scratch),
        compiler_params=PARAMS,
        cost_estimate=cost,
        name=name,
    )


def shifted(value, axis, by):
    devices = lax.axis_size(axis)
    return lax.ppermute(value, axis, [(i, (i + by) % devices) for i in range(devices)])


def over_span(to_up, to_down):
    return shifted(to_down, "span", 1), shifted(to_up, "span", -1)


def over_pitch(to_left, to_right):
    return shifted(to_right, "pitch", 1), shifted(to_left, "pitch", -1)


def on_device(
    adjoint, source, pseudo_step, jac_blocks, band_map, face_cell, face_owner, face_weight
):
    rows, spans, pitches = (lax.axis_size(name) for name in ("row", "span", "pitch"))
    devices = rows * spans * pitches
    peers = spans * pitches
    block = (NVAR, CS, CP, LANES)
    edge = (NVAR, CP, LANES)
    side = (NVAR, CS, LANES)
    edges = call(
        edges_kernel,
        "edges",
        [edge, edge, side, side],
        in_specs=[HBM],
        scratch=[pltpu.SemaphoreType.DMA((4,))],
    )(in_hbm(adjoint))
    halo = over_span(*edges[:2]) + over_pitch(*edges[2:])
    part, record, jac, src, tau = call(
        interior_kernel,
        "interior",
        [block, (CS, CP, LANES), ((7, NVAR) + block, BF16), block, (CS, CP, LANES)],
        in_specs=[HBM] * 4,
        scratch=[
            pltpu.VMEM(block, F32),
            pltpu.VMEM((7 * NVAR, CS, CP, LANES), F32),
            pltpu.VMEM(block, F32),
            pltpu.SemaphoreType.DMA((10,)),
        ],
        cost=pl.CostEstimate(flops=9_000_000, bytes_accessed=3_000_000, transcendentals=0),
    )(*(in_hbm(x) for x in (adjoint, source, pseudo_step, jac_blocks)))
    edge = (NVAR + 1, CP, LANES)
    side = (NVAR + 1, CS, LANES)
    first, message, full_record, *sends = call(
        edge_kernel,
        "edge_update",
        [block, (2 * devices, LANES), (CS, CP, LANES), edge, edge, side, side],
        in_specs=[VM] * 8,
        scratch=[pltpu.VMEM((2 * NVAR, CS, CP, LANES), F32)],
    )(part, record, jac, tau, *halo)
    records = lax.all_to_all(
        message.reshape(devices, 1, 2 * LANES), ("row", "span", "pitch"), 0, 0
    ).reshape(2 * devices, LANES)
    halo = over_span(*sends[:2]) + over_pitch(*sends[2:])
    part, packs, ids, seen, picks = call(
        settle_kernel,
        "settle",
        [
            block, (6, CS, CP, LANES), ((2 * devices, LANES), F32), (2, CS, CP, LANES),
            ((LANES, 3 * LANES), BF16),
        ],
        in_specs=[VM] * 7,
        scratch=[pltpu.VMEM((7 * NVAR, CS, CP, LANES), F32)],
        cost=pl.CostEstimate(flops=9_000_000, bytes_accessed=3_000_000, transcendentals=0),
    )(band_map, first, src, tau, jac, face_cell, face_owner)
    part, faces = call(
        settle_edges_kernel,
        "settle_edges",
        [block, (CP, LANES)],
        in_specs=[VM] * 8,
        scratch=[pltpu.VMEM((2 * NVAR, CS, CP, LANES), F32)],
        cost=pl.CostEstimate(flops=3_000_000, bytes_accessed=2_000_000, transcendentals=0),
    )(part, jac, tau, *halo, face_cell)
    field, dense = call(
        cycle_kernel,
        "cycle_update",
        [(1,) + block, (3 * peers, LANES)],
        in_specs=[SM] + [VM] * 14,
        out_specs=(HBM, VM),
        scratch=[pltpu.VMEM((1,) + block, F32), pltpu.SemaphoreType.DMA],
    )(
        band_map, part, full_record, packs, ids, records, *halo, seen, picks, faces, face_owner,
        face_weight,
    )
    parts = lax.all_to_all(dense.reshape(peers, 1, 3 * LANES), ("span", "pitch"), 0, 0)
    (nodes,) = call(third_kernel, "node_sums", [(3, 1, LANES)], in_specs=[VM])(
        parts.reshape(3 * peers, LANES)
    )
    return field, nodes.transpose(1, 0, 2)


def solution(mesh):
    in_specs = (
        P("row", None, "span", "pitch", None),
        P("row", None, "span", "pitch", None),
        P("row", "span", "pitch", None),
        P("row", None, None, None, "span", "pitch", None),
        P(),
        P("row", "span", "pitch", None),
        P("row", "span", "pitch", None),
        P("row", "span", "pitch", None, None),
    )
    out_specs = (P("row", None, "span", "pitch", None), P("row", None, ("span", "pitch")))
    return jax.shard_map(
        on_device, mesh=mesh, in_specs=in_specs, out_specs=out_specs, check_vma=False
    )
```

```python
import jax
import jax.numpy as jnp
from jax import lax
from jax.experimental import pallas as pl
from jax.experimental.pallas import tpu as pltpu
from jax.sharding import PartitionSpec as P

NVAR = 6
CS = 4
CP = 8
LANES = 128
F32 = jnp.float32
BF16 = jnp.bfloat16
FIRST_AT = 8
WEIGHT_AT = 16
COUNT_AT = 6
PITCH_PAD = 7


def lane_ids(shape):
    return lax.broadcasted_iota(jnp.int32, shape, len(shape) - 1)


def row_ids(shape):
    return lax.broadcasted_iota(jnp.int32, shape, len(shape) - 2)


def split3(x):
    hi = x.astype(BF16)
    rest = x - hi.astype(F32)
    mid = rest.astype(BF16)
    low = (rest - mid.astype(F32)).astype(BF16)
    return hi, mid, low


def dot3(x, onehot, dims):
    parts = [
        lax.dot_general(part, onehot, (dims, ((), ())), preferred_element_type=F32)
        for part in split3(x)
    ]
    return parts[0] + (parts[1] + parts[2])


def fill_stencil(vs, field, up, down, left, right, lower, upper):
    tile = (CP, LANES)
    lane, sub = lane_ids(tile), row_ids(tile)
    for d in range(NVAR):
        for j in range(CS):
            x = field(d, j)
            vs[d, j] = x
            vs[6 + d, j] = field(d, j - 1) if j > 0 else up(d)
            vs[12 + d, j] = field(d, j + 1) if j < CS - 1 else down(d)
            vs[18 + d, j] = jnp.where(
                sub == 0, jnp.broadcast_to(left(d, j), tile), pltpu.roll(x, 1, 0)
            )
            vs[24 + d, j] = jnp.where(
                sub == CP - 1, jnp.broadcast_to(right(d, j), tile), pltpu.roll(x, CP - 1, 0)
            )
            vs[30 + d, j] = jnp.where(lane == 0, lower(d, j), pltpu.roll(x, 1, 1))
            vs[36 + d, j] = jnp.where(lane == LANES - 1, upper(d, j), pltpu.roll(x, LANES - 1, 1))


def image_of(jac_ref, vs, c):
    acc = jnp.zeros((CS, CP, LANES), F32)
    for s in range(7):
        for d in range(NVAR):
            acc = acc + jac_ref[s, c, d].astype(F32) * vs[6 * s + d]
    return acc


def edges_kernel(adj_ref, left_ref, right_ref, up_ref, down_ref, sems):
    adj = adj_ref.at[0]
    left_rows, right_rows = (ref.at[:NVAR] for ref in (left_ref, right_ref))
    copies = [
        pltpu.make_async_copy(adj.at[:, 0], up_ref, sems.at[0]),
        pltpu.make_async_copy(adj.at[:, CS - 1], down_ref, sems.at[1]),
        pltpu.make_async_copy(adj.at[:, :, 0], left_rows, sems.at[2]),
        pltpu.make_async_copy(adj.at[:, :, CP - 1], right_rows, sems.at[3]),
    ]
    for copy in copies:
        copy.start()
    for ref in (left_ref, right_ref):
        ref[NVAR:] = jnp.zeros((PITCH_PAD, CS, LANES), F32)
    for copy in copies:
        copy.wait()


def interior_kernel(
    adj_hbm, src_hbm, tau_hbm, jac_hbm, part_ref, rec_ref, jac_ref, src_ref, tau_ref, adj_ref, vs,
    image, sems,
):
    row = lax.axis_index("row")
    outlet = (1 - row) * (LANES - 1)
    ghost = 6 - row
    tile = (CP, LANES)
    zero = jnp.zeros(tile, F32)
    lane = lane_ids(tile)
    load_adj = pltpu.make_async_copy(adj_hbm.at[0], adj_ref, sems.at[0])
    load_jac = [
        pltpu.make_async_copy(jac_hbm.at[0, s], jac_ref.at[s], sems.at[1 + s]) for s in range(7)
    ]
    load_tau = pltpu.make_async_copy(tau_hbm.at[0], tau_ref, sems.at[8])
    load_src = pltpu.make_async_copy(src_hbm.at[0], src_ref, sems.at[9])
    for copy in [load_adj] + load_jac + [load_tau, load_src]:
        copy.start()
    load_adj.wait()
    fill_stencil(
        vs,
        lambda d, j: adj_ref[d, j],
        lambda d: zero,
        lambda d: zero,
        lambda d, j: zero,
        lambda d, j: zero,
        lambda d, j: zero,
        lambda d, j: zero,
    )
    for s in range(7):
        load_jac[s].wait()

        def apply(c, carry):
            acc = jnp.zeros((CS, CP, LANES), F32) if s == 0 else image[c]
            for d in range(NVAR):
                acc = acc + jac_ref[s, c, d].astype(F32) * vs[6 * s + d]
            image[c] = acc
            return carry

        lax.fori_loop(0, NVAR, apply, 0)
    load_tau.wait()
    load_src.wait()

    def finish(c, carry):
        weights, sums = (list(x) for x in carry)
        f0 = adj_ref[c]
        part_ref[c] = f0 + tau_ref[...] * (src_ref[c] - image[c])
        for j in range(CS):
            for d in range(NVAR):
                at = WEIGHT_AT + 8 * d + c
                moved = pltpu.roll(jac_ref[ghost, c, d, j].astype(F32), at + 1 - row, 1)
                weights[j] = jnp.where(lane == at, moved, weights[j])
            sums[j] = jnp.where(lane == c, pltpu.roll(f0[j], c + 1 - row, 1), sums[j])
        return tuple(weights), tuple(sums)

    ones = jnp.where(lane == COUNT_AT, 1.0, 0.0).astype(F32)
    weights, sums = lax.fori_loop(0, NVAR, finish, ((zero,) * CS, (ones,) * CS))
    for j in range(CS):
        tau_out = jnp.sum(jnp.where(lane == outlet, tau_ref[j], 0.0), axis=1, keepdims=True)
        rec_ref[j] = sums[j] + weights[j] * tau_out


def inner_sides():
    span = lax.axis_index("span")
    return (
        jnp.where(span > 0, 1.0, 0.0).astype(F32),
        jnp.where(span < lax.axis_size("span") - 1, 1.0, 0.0).astype(F32),
    )


def fill_sides(sides, left_ref, right_ref):
    tile = (CP, LANES)
    sub = row_ids(tile)
    for d in range(NVAR):
        for j in range(CS):
            sides[d, j] = jnp.where(
                sub == 0, jnp.broadcast_to(left_ref[d, j : j + 1], tile), 0.0
            )
            sides[NVAR + d, j] = jnp.where(
                sub == CP - 1, jnp.broadcast_to(right_ref[d, j : j + 1], tile), 0.0
            )


def edge_terms(jac_ref, sides, up_ref, down_ref, keep, c):
    acc = jnp.zeros((CS, CP, LANES), F32)
    first = jnp.zeros((CP, LANES), F32)
    last = jnp.zeros((CP, LANES), F32)
    for d in range(NVAR):
        acc = acc + jac_ref[3, c, d].astype(F32) * sides[d]
        acc = acc + jac_ref[4, c, d].astype(F32) * sides[NVAR + d]
        first = first + jac_ref[1, c, d, 0].astype(F32) * up_ref[d]
        last = last + jac_ref[2, c, d, CS - 1].astype(F32) * down_ref[d]
    lost = [acc[j] for j in range(CS)]
    lost[0] = lost[0] + first * keep[0]
    lost[CS - 1] = lost[CS - 1] + last * keep[1]
    return lost


def edge_kernel(
    part_ref, rec_in, jac_ref, tau_ref, left_ref, right_ref, up_ref, down_ref,
    f1_ref, msg_ref, rec, to_left_ref, to_right_ref, to_up_ref, to_down_ref, sides,
):
    row = lax.axis_index("row")
    keep = inner_sides()
    tile = (CP, LANES)
    lane, sub = lane_ids(tile), row_ids(tile)
    fill_sides(sides, left_ref, right_ref)

    def body(c, sums):
        sums = list(sums)
        lost = edge_terms(jac_ref, sides, up_ref, down_ref, keep, c)
        at = FIRST_AT + c
        for j in range(CS):
            new = part_ref[c, j] - tau_ref[j] * lost[j]
            f1_ref[c, j] = new
            sums[j] = jnp.where(lane == at, pltpu.roll(new, at + 1 - row, 1), sums[j])
        return tuple(sums)

    sums = lax.fori_loop(0, NVAR, body, tuple(rec_in[j] for j in range(CS)))
    rows = []
    for j in range(CS):
        rec[j] = sums[j]
        rows.append(jnp.sum(sums[j], axis=0, keepdims=True))
    halves = [
        jnp.broadcast_to(rows[2 * h] + pltpu.roll(rows[2 * h + 1], 64, 1), tile) for h in range(2)
    ]
    packed = jnp.where(sub % 2 == 0, halves[0], halves[1])
    for i in range(msg_ref.shape[0] // CP):
        msg_ref[CP * i : CP * (i + 1)] = packed
    to_up_ref[0:NVAR] = f1_ref[:, 0]
    to_up_ref[NVAR] = rec[0]
    to_down_ref[0:NVAR] = f1_ref[:, CS - 1]
    to_down_ref[NVAR] = rec[CS - 1]
    for c in range(NVAR):
        to_left_ref[c] = f1_ref[c, :, 0, :]
        to_right_ref[c] = f1_ref[c, :, CP - 1, :]
    to_left_ref[NVAR] = rec[:, 0, :]
    to_right_ref[NVAR] = rec[:, CP - 1, :]
    for ref in (to_left_ref, to_right_ref):
        ref[NVAR + 1 :] = jnp.zeros((PITCH_PAD + 1, CS, LANES), F32)


def weight_sum(x):
    for by in (32, 16, 8):
        x = x + pltpu.roll(x, LANES - by, 1)
    return x


def spread(values, first):
    lane = lane_ids(values.shape)
    out = jnp.zeros(values.shape, F32)
    for d in range(NVAR):
        at = first + d
        out = jnp.where(
            lane // 8 == d + WEIGHT_AT // 8,
            jnp.broadcast_to(values[:, at : at + 1], values.shape),
            out,
        )
    return out


def outlet_lanes(row):
    return (1 - row) * (LANES - 1), (1 - row) * (LANES - 2) + row


def settle_kernel(
    bands_ref, f1_ref, src_ref, tau_ref, jac_ref, cell_ref, owner_ref,
    part_ref, pack_ref, ids_ref, seen_ref, node_ref, vs,
):
    row = lax.axis_index("row")
    outlet, inner = outlet_lanes(row)
    ghost = 6 - row
    tile = (CP, LANES)
    zero = jnp.zeros(tile, F32)
    lane = lane_ids(tile)
    fill_stencil(
        vs,
        lambda d, j: f1_ref[d, j],
        lambda d: zero,
        lambda d: zero,
        lambda d, j: zero,
        lambda d, j: zero,
        lambda d, j: zero,
        lambda d, j: zero,
    )
    for n in range(6):
        for j in range(CS):
            pack_ref[n, j] = zero

    def advance(c, carry):
        part_ref[c] = f1_ref[c] + tau_ref[...] * (src_ref[c] - image_of(jac_ref, vs, c))
        for n in range(6):
            point = n if n < 5 else ghost
            extra = 1 - row if n < 5 else 2 - 3 * row
            for j in range(CS):
                pack = pack_ref[n, j]
                for d in range(NVAR):
                    at = WEIGHT_AT + 8 * d + c
                    moved = pltpu.roll(jac_ref[point, c, d, j].astype(F32), at + extra, 1)
                    pack = jnp.where(lane == at, moved, pack)
                pack_ref[n, j] = pack
        return carry

    lax.fori_loop(0, NVAR, advance, 0)
    for j in range(CS):
        steps = [
            jnp.sum(jnp.where(lane == at, tau_ref[j], 0.0), axis=1, keepdims=True)
            for at in (outlet, inner)
        ]
        for n in range(6):
            pack_ref[n, j] = pack_ref[n, j] * steps[n // 5]
    square = (LANES, LANES)
    lines = ids_ref.shape[0] // 2
    line = row_ids((lines, LANES))
    first_cell = CS * (line // CP) + 2 * (line % 2)
    even_cell = (lane_ids((lines, LANES)) == first_cell).astype(F32).astype(BF16)
    for of_row in range(2):
        bands = bands_ref[of_row : of_row + 1].astype(F32)
        pair = jnp.where(
            row_ids(square) < LANES // 2,
            jnp.broadcast_to(bands, square),
            jnp.broadcast_to(pltpu.roll(bands, LANES - 1, 1), square),
        )
        ids_ref[lines * of_row : lines * (of_row + 1)] = lax.dot_general(
            even_cell, pair.astype(BF16), (((1,), (1,)), ((), ())), preferred_element_type=F32
        )
    cells = cell_ref[0, 0]
    for j in range(CS):
        here = row_ids(tile) + CP * j == cells // LANES
        for n, at in enumerate((outlet, inner)):
            seen_ref[n, j] = jnp.where(here & (cells % LANES == at), 1.0, 0.0).astype(F32)
    picked = (row_ids(square) == owner_ref[0, 0] % LANES).astype(F32).astype(BF16)
    for n in range(3):
        node_ref[:, LANES * n : LANES * (n + 1)] = picked


def settle_edges_kernel(
    part_ref, jac_ref, tau_ref, left_ref, right_ref, up_ref, down_ref, cell_ref,
    part2_ref, face_ref, sides,
):
    keep = inner_sides()
    tile = (CP, LANES)
    fill_sides(sides, left_ref, right_ref)

    def body(c, carry):
        lost = edge_terms(jac_ref, sides, up_ref, down_ref, keep, c)
        for j in range(CS):
            part2_ref[c, j] = part_ref[c, j] - tau_ref[j] * lost[j]
        return carry

    lax.fori_loop(0, NVAR, body, 0)
    cells = cell_ref[0, 0]
    square = (LANES, LANES)
    axial_pick = (row_ids(square) == cells % LANES).astype(F32).astype(BF16)
    picked = dot3(part2_ref[...].reshape(NVAR * CS * CP, LANES), axial_pick, ((1,), (0,)))
    here = row_ids((CS * CP, LANES)) == cells // LANES
    for c in range(NVAR):
        block = picked[c * CS * CP : (c + 1) * CS * CP]
        face_ref[c : c + 1] = jnp.sum(jnp.where(here, block, 0.0), axis=0, keepdims=True)


def cycle_kernel(
    bands_ref, part_ref, rec_ref, pack_ref, ids_ref, all_ref, left_ref, right_ref, up_ref, down_ref,
    seen_ref, node_ref, face_ref, owner_ref, weight_ref, out_hbm, dense_ref, field, sem,
):
    row = lax.axis_index("row")
    span = lax.axis_index("span")
    outlet, inner = outlet_lanes(row)
    keep = inner_sides()
    tile = (CP, LANES)
    lane, sub = lane_ids(tile), row_ids(tile)
    last_cell = bands_ref.shape[1] - 1
    wanted = [
        bands_ref[row, jnp.clip(span * CS - 1 + t, 0, last_cell)].astype(F32)
        for t in range(CS + 2)
    ]
    half = all_ref.shape[0] // 2
    zero = jnp.zeros(tile, F32)

    def body(i, sums):
        sums = list(sums)
        for n, of_row in enumerate((1 - row, row)):
            at = pl.multiple_of(of_row * half + i * CP, CP)
            ids, values = ids_ref[pl.ds(at, CP), :], all_ref[pl.ds(at, CP), :]
            for t, band in enumerate(wanted):
                k = (CS + 2) * n + t
                sums[k] = sums[k] + jnp.where(ids == band, values, 0.0)
        return tuple(sums)

    sums = lax.fori_loop(0, half // CP, body, (zero,) * (2 * CS + 4), unroll=4)

    def folded(parts):
        rows = [jnp.sum(x, axis=0, keepdims=True) for x in parts]
        whole = jnp.concatenate(rows + [rows[-1]] * (CP - len(rows)), axis=0)
        whole = whole + pltpu.roll(whole, 64, 1)
        return whole, jnp.broadcast_to(whole[:, COUNT_AT : COUNT_AT + 1], tile)

    other, other_count = folded(sums[: CS + 2])
    mine, my_count = folded(sums[CS + 2 :])
    spread0 = spread(other / other_count, 0)
    lost = weight_sum(other * spread(mine / my_count, 0))
    cycle1 = (other - pltpu.roll(lost, LANES - (WEIGHT_AT - FIRST_AT), 1)) / other_count
    spread1 = spread(cycle1, FIRST_AT)

    def shift_of(record, values):
        moved = weight_sum(record * values)
        return moved, spread(moved, WEIGHT_AT)

    own = [shift_of(rec_ref[j], spread0[j + 1 : j + 2]) for j in range(CS)]
    above = shift_of(up_ref[NVAR], spread0[:1])[1] * keep[0]
    below = shift_of(down_ref[NVAR], spread0[CS + 1 : CS + 2])[1] * keep[1]
    left = shift_of(left_ref[NVAR], spread0[1 : 1 + CS])[1]
    right = shift_of(right_ref[NVAR], spread0[1 : 1 + CS])[1]
    changes = []
    for j in range(CS):
        x = own[j][1]
        total = pack_ref[0, j] * x - rec_ref[j] * spread1[j + 1 : j + 2]
        total = total + pack_ref[1, j] * (own[j - 1][1] if j > 0 else above)
        total = total + pack_ref[2, j] * (own[j + 1][1] if j < CS - 1 else below)
        total = total + pack_ref[3, j] * jnp.where(
            sub == 0, jnp.broadcast_to(left[j : j + 1], tile), pltpu.roll(x, 1, 0)
        )
        total = total + pack_ref[4, j] * jnp.where(
            sub == CP - 1, jnp.broadcast_to(right[j : j + 1], tile), pltpu.roll(x, CP - 1, 0)
        )
        changes.append((weight_sum(total) - own[j][0], weight_sum(pack_ref[5, j] * x)))
    terms = [jnp.zeros((1, LANES), F32)] * 3
    for c in range(NVAR):
        at = WEIGHT_AT + c
        seen = zero
        for j in range(CS):
            first, second = (jnp.broadcast_to(x[:, at : at + 1], tile) for x in changes[j])
            moved = jnp.where(lane == outlet, first, jnp.where(lane == inner, second, 0.0))
            field[0, c, j] = part_ref[c, j] + moved
            seen = seen + (seen_ref[0, j] * first + seen_ref[1, j] * second)
        value = face_ref[c : c + 1] + jnp.sum(seen, axis=0, keepdims=True)
        for k in range(3):
            at = NVAR * k + c
            terms[k] = terms[k] + weight_ref[0, 0, 0, at : at + 1] * value
    write = pltpu.make_async_copy(field, out_hbm, sem)
    write.start()
    shape = dense_ref.shape
    line = row_ids(shape)
    device = (line * 43691) >> 17
    here = device == owner_ref[0, 0] // LANES
    cycle_rows = (24, LANES)
    coord = row_ids(cycle_rows) % 3
    pieces = []
    for parts in zip(*(split3(x) for x in terms)):
        wide = [jnp.broadcast_to(x.astype(F32), cycle_rows) for x in parts]
        pattern = jnp.where(coord == 0, wide[0], jnp.where(coord == 1, wide[1], wide[2]))
        pattern = jnp.concatenate([pattern] * (shape[0] // 24), axis=0)
        pieces.append(jnp.where(here, pattern, 0.0).astype(BF16))
    dense_ref[...] = lax.dot_general(
        jnp.concatenate(pieces, axis=1),
        node_ref[...],
        (((1,), (1,)), ((), ())),
        preferred_element_type=F32,
    )
    write.wait()


def third_kernel(parts_ref, out_ref):
    folded = jnp.sum(parts_ref[...].reshape(-1, 24, LANES), axis=0)
    coord = row_ids(folded.shape) % 3
    for k in range(3):
        out_ref[k] = jnp.sum(jnp.where(coord == k, folded, 0.0), axis=0, keepdims=True)


VM = pl.BlockSpec(memory_space=pltpu.VMEM)
SM = pl.BlockSpec(memory_space=pltpu.SMEM)
PARAMS = pltpu.CompilerParams(vmem_limit_bytes=32 * 1024 * 1024)


HBM = pl.BlockSpec(memory_space=pltpu.HBM)


def in_hbm(x):
    return pltpu.with_memory_space_constraint(x, pltpu.HBM)


def call(kernel, name, outs, in_specs, scratch=(), cost=None, out_specs=None):
    outs = [out if isinstance(out[0], tuple) else (out, F32) for out in outs]
    return pl.pallas_call(
        kernel,
        out_shape=tuple(jax.ShapeDtypeStruct(shape, dtype) for shape, dtype in outs),
        in_specs=in_specs,
        out_specs=out_specs or (VM,) * len(outs),
        scratch_shapes=list(scratch),
        compiler_params=PARAMS,
        cost_estimate=cost,
        name=name,
    )


def shifted(value, axis, by):
    devices = lax.axis_size(axis)
    return lax.ppermute(value, axis, [(i, (i + by) % devices) for i in range(devices)])


def over_span(to_up, to_down):
    return shifted(to_down, "span", 1), shifted(to_up, "span", -1)


def over_pitch(to_left, to_right):
    return shifted(to_right, "pitch", 1), shifted(to_left, "pitch", -1)


def on_device(
    adjoint, source, pseudo_step, jac_blocks, band_map, face_cell, face_owner, face_weight
):
    rows, spans, pitches = (lax.axis_size(name) for name in ("row", "span", "pitch"))
    devices = rows * spans * pitches
    peers = spans * pitches
    block = (NVAR, CS, CP, LANES)
    edge = (NVAR, CP, LANES)
    side = (NVAR + PITCH_PAD, CS, LANES)
    edges = call(
        edges_kernel,
        "edges",
        [side, side, edge, edge],
        in_specs=[HBM],
        scratch=[pltpu.SemaphoreType.DMA((4,))],
    )(in_hbm(adjoint))
    halo = over_pitch(*edges[:2]) + over_span(*edges[2:])
    part, record, jac, src, tau = call(
        interior_kernel,
        "interior",
        [block, (CS, CP, LANES), ((7, NVAR) + block, BF16), block, (CS, CP, LANES)],
        in_specs=[HBM] * 4,
        scratch=[
            pltpu.VMEM(block, F32),
            pltpu.VMEM((7 * NVAR, CS, CP, LANES), F32),
            pltpu.VMEM(block, F32),
            pltpu.SemaphoreType.DMA((10,)),
        ],
        cost=pl.CostEstimate(flops=9_000_000, bytes_accessed=3_000_000, transcendentals=0),
    )(*(in_hbm(x) for x in (adjoint, source, pseudo_step, jac_blocks)))
    edge = (NVAR + 1, CP, LANES)
    side = (NVAR + 1 + PITCH_PAD + 1, CS, LANES)
    first, message, full_record, *sends = call(
        edge_kernel,
        "edge_update",
        [block, (2 * devices, LANES), (CS, CP, LANES), side, side, edge, edge],
        in_specs=[VM] * 8,
        scratch=[pltpu.VMEM((2 * NVAR, CS, CP, LANES), F32)],
    )(part, record, jac, tau, *halo)
    records = lax.all_to_all(
        message.reshape(devices, 1, 2 * LANES), ("row", "span", "pitch"), 0, 0
    ).reshape(2 * devices, LANES)
    halo = over_pitch(*sends[:2]) + over_span(*sends[2:])
    part, packs, ids, seen, picks = call(
        settle_kernel,
        "settle",
        [
            block, (6, CS, CP, LANES), ((2 * devices, LANES), F32), (2, CS, CP, LANES),
            ((LANES, 3 * LANES), BF16),
        ],
        in_specs=[VM] * 7,
        scratch=[pltpu.VMEM((7 * NVAR, CS, CP, LANES), F32)],
        cost=pl.CostEstimate(flops=9_000_000, bytes_accessed=3_000_000, transcendentals=0),
    )(band_map, first, src, tau, jac, face_cell, face_owner)
    part, faces = call(
        settle_edges_kernel,
        "settle_edges",
        [block, (CP, LANES)],
        in_specs=[VM] * 8,
        scratch=[pltpu.VMEM((2 * NVAR, CS, CP, LANES), F32)],
        cost=pl.CostEstimate(flops=3_000_000, bytes_accessed=2_000_000, transcendentals=0),
    )(part, jac, tau, *halo, face_cell)
    field, dense = call(
        cycle_kernel,
        "cycle_update",
        [(1,) + block, (3 * peers, LANES)],
        in_specs=[SM] + [VM] * 14,
        out_specs=(HBM, VM),
        scratch=[pltpu.VMEM((1,) + block, F32), pltpu.SemaphoreType.DMA],
    )(
        band_map, part, full_record, packs, ids, records, *halo, seen, picks, faces, face_owner,
        face_weight,
    )
    parts = lax.all_to_all(dense.reshape(peers, 1, 3 * LANES), ("span", "pitch"), 0, 0)
    (nodes,) = call(third_kernel, "node_sums", [(3, 1, LANES)], in_specs=[VM])(
        parts.reshape(3 * peers, LANES)
    )
    return field, nodes.transpose(1, 0, 2)


def solution(mesh):
    in_specs = (
        P("row", None, "span", "pitch", None),
        P("row", None, "span", "pitch", None),
        P("row", "span", "pitch", None),
        P("row", None, None, None, "span", "pitch", None),
        P(),
        P("row", "span", "pitch", None),
        P("row", "span", "pitch", None),
        P("row", "span", "pitch", None, None),
    )
    out_specs = (P("row", None, "span", "pitch", None), P("row", None, ("span", "pitch")))
    return jax.shard_map(
        on_device, mesh=mesh, in_specs=in_specs, out_specs=out_specs, check_vma=False
    )
```

```python
import jax
import jax.numpy as jnp
from jax import lax
from jax.experimental import pallas as pl
from jax.experimental.pallas import tpu as pltpu
from jax.sharding import PartitionSpec as P

NVAR = 6
CS = 4
CP = 8
LANES = 128
F32 = jnp.float32
BF16 = jnp.bfloat16
FIRST_AT = 8
WEIGHT_AT = 16
COUNT_AT = 6


def lane_ids(shape):
    return lax.broadcasted_iota(jnp.int32, shape, len(shape) - 1)


def row_ids(shape):
    return lax.broadcasted_iota(jnp.int32, shape, len(shape) - 2)


def split3(x):
    hi = x.astype(BF16)
    rest = x - hi.astype(F32)
    mid = rest.astype(BF16)
    low = (rest - mid.astype(F32)).astype(BF16)
    return hi, mid, low


def dot3(x, onehot, dims):
    parts = [
        lax.dot_general(part, onehot, (dims, ((), ())), preferred_element_type=F32)
        for part in split3(x)
    ]
    return parts[0] + (parts[1] + parts[2])


def fill_stencil(vs, field, up, down, left, right, lower, upper):
    tile = (CP, LANES)
    lane, sub = lane_ids(tile), row_ids(tile)
    for d in range(NVAR):
        for j in range(CS):
            x = field(d, j)
            vs[d, j] = x
            vs[6 + d, j] = field(d, j - 1) if j > 0 else up(d)
            vs[12 + d, j] = field(d, j + 1) if j < CS - 1 else down(d)
            vs[18 + d, j] = jnp.where(
                sub == 0, jnp.broadcast_to(left(d, j), tile), pltpu.roll(x, 1, 0)
            )
            vs[24 + d, j] = jnp.where(
                sub == CP - 1, jnp.broadcast_to(right(d, j), tile), pltpu.roll(x, CP - 1, 0)
            )
            vs[30 + d, j] = jnp.where(lane == 0, lower(d, j), pltpu.roll(x, 1, 1))
            vs[36 + d, j] = jnp.where(lane == LANES - 1, upper(d, j), pltpu.roll(x, LANES - 1, 1))


def image_of(jac_ref, vs, c):
    acc = jnp.zeros((CS, CP, LANES), F32)
    for s in range(7):
        for d in range(NVAR):
            acc = acc + jac_ref[s, c, d].astype(F32) * vs[6 * s + d]
    return acc


def edges_kernel(adj_ref, up_ref, down_ref, left_ref, right_ref, sems):
    adj = adj_ref.at[0]
    copies = [
        pltpu.make_async_copy(adj.at[:, 0], up_ref, sems.at[0]),
        pltpu.make_async_copy(adj.at[:, CS - 1], down_ref, sems.at[1]),
        pltpu.make_async_copy(adj.at[:, :, 0], left_ref, sems.at[2]),
        pltpu.make_async_copy(adj.at[:, :, CP - 1], right_ref, sems.at[3]),
    ]
    for copy in copies:
        copy.start()
    for copy in copies:
        copy.wait()


def interior_kernel(
    adj_hbm, src_hbm, tau_hbm, jac_hbm, part_ref, rec_ref, jac_ref, src_ref, tau_ref, adj_ref, vs,
    image, sems,
):
    row = lax.axis_index("row")
    outlet = (1 - row) * (LANES - 1)
    ghost = 6 - row
    tile = (CP, LANES)
    zero = jnp.zeros(tile, F32)
    lane = lane_ids(tile)
    load_adj = pltpu.make_async_copy(adj_hbm.at[0], adj_ref, sems.at[0])
    load_jac = [
        pltpu.make_async_copy(jac_hbm.at[0, s], jac_ref.at[s], sems.at[1 + s]) for s in range(7)
    ]
    load_tau = pltpu.make_async_copy(tau_hbm.at[0], tau_ref, sems.at[8])
    load_src = pltpu.make_async_copy(src_hbm.at[0], src_ref, sems.at[9])
    for copy in [load_adj] + load_jac + [load_tau, load_src]:
        copy.start()
    load_adj.wait()
    fill_stencil(
        vs,
        lambda d, j: adj_ref[d, j],
        lambda d: zero,
        lambda d: zero,
        lambda d, j: zero,
        lambda d, j: zero,
        lambda d, j: zero,
        lambda d, j: zero,
    )
    for s in range(7):
        load_jac[s].wait()

        def apply(c, carry):
            acc = jnp.zeros((CS, CP, LANES), F32) if s == 0 else image[c]
            for d in range(NVAR):
                acc = acc + jac_ref[s, c, d].astype(F32) * vs[6 * s + d]
            image[c] = acc
            return carry

        lax.fori_loop(0, NVAR, apply, 0)
    load_tau.wait()
    load_src.wait()

    def finish(c, carry):
        weights, sums = (list(x) for x in carry)
        f0 = adj_ref[c]
        part_ref[c] = f0 + tau_ref[...] * (src_ref[c] - image[c])
        for j in range(CS):
            for d in range(NVAR):
                at = WEIGHT_AT + 8 * d + c
                moved = pltpu.roll(jac_ref[ghost, c, d, j].astype(F32), at + 1 - row, 1)
                weights[j] = jnp.where(lane == at, moved, weights[j])
            sums[j] = jnp.where(lane == c, pltpu.roll(f0[j], c + 1 - row, 1), sums[j])
        return tuple(weights), tuple(sums)

    ones = jnp.where(lane == COUNT_AT, 1.0, 0.0).astype(F32)
    weights, sums = lax.fori_loop(0, NVAR, finish, ((zero,) * CS, (ones,) * CS))
    for j in range(CS):
        tau_out = jnp.sum(jnp.where(lane == outlet, tau_ref[j], 0.0), axis=1, keepdims=True)
        rec_ref[j] = sums[j] + weights[j] * tau_out


def inner_sides():
    span = lax.axis_index("span")
    return (
        jnp.where(span > 0, 1.0, 0.0).astype(F32),
        jnp.where(span < lax.axis_size("span") - 1, 1.0, 0.0).astype(F32),
    )


def fill_sides(sides, left_ref, right_ref):
    tile = (CP, LANES)
    sub = row_ids(tile)
    for d in range(NVAR):
        for j in range(CS):
            sides[d, j] = jnp.where(
                sub == 0, jnp.broadcast_to(left_ref[d, j : j + 1], tile), 0.0
            )
            sides[NVAR + d, j] = jnp.where(
                sub == CP - 1, jnp.broadcast_to(right_ref[d, j : j + 1], tile), 0.0
            )


def edge_terms(jac_ref, sides, up_ref, down_ref, keep, c):
    acc = jnp.zeros((CS, CP, LANES), F32)
    first = jnp.zeros((CP, LANES), F32)
    last = jnp.zeros((CP, LANES), F32)
    for d in range(NVAR):
        acc = acc + jac_ref[3, c, d].astype(F32) * sides[d]
        acc = acc + jac_ref[4, c, d].astype(F32) * sides[NVAR + d]
        first = first + jac_ref[1, c, d, 0].astype(F32) * up_ref[d]
        last = last + jac_ref[2, c, d, CS - 1].astype(F32) * down_ref[d]
    lost = [acc[j] for j in range(CS)]
    lost[0] = lost[0] + first * keep[0]
    lost[CS - 1] = lost[CS - 1] + last * keep[1]
    return lost


def edge_kernel(
    part_ref, rec_in, jac_ref, tau_ref, up_ref, down_ref, left_ref, right_ref,
    f1_ref, msg_hbm, rec, to_up_ref, to_down_ref, to_left_ref, to_right_ref, sides, copies, sems,
):
    row = lax.axis_index("row")
    keep = inner_sides()
    tile = (CP, LANES)
    lane, sub = lane_ids(tile), row_ids(tile)
    fill_sides(sides, left_ref, right_ref)

    def body(c, sums):
        sums = list(sums)
        lost = edge_terms(jac_ref, sides, up_ref, down_ref, keep, c)
        at = FIRST_AT + c
        for j in range(CS):
            new = part_ref[c, j] - tau_ref[j] * lost[j]
            f1_ref[c, j] = new
            sums[j] = jnp.where(lane == at, pltpu.roll(new, at + 1 - row, 1), sums[j])
        return tuple(sums)

    sums = lax.fori_loop(0, NVAR, body, tuple(rec_in[j] for j in range(CS)))
    rows = []
    for j in range(CS):
        rec[j] = sums[j]
        rows.append(jnp.sum(sums[j], axis=0, keepdims=True))
    halves = [
        jnp.broadcast_to(rows[2 * h] + pltpu.roll(rows[2 * h + 1], 64, 1), tile) for h in range(2)
    ]
    packed = jnp.where(sub % 2 == 0, halves[0], halves[1])
    lines = copies.shape[0]
    for i in range(lines // CP):
        copies[CP * i : CP * (i + 1)] = packed
    writes = [
        pltpu.make_async_copy(copies, msg_hbm.at[pl.ds(lines * i, lines)], sems.at[i])
        for i in range(msg_hbm.shape[0] // lines)
    ]
    for write in writes:
        write.start()
    to_up_ref[0:NVAR] = f1_ref[:, 0]
    to_up_ref[NVAR] = rec[0]
    to_down_ref[0:NVAR] = f1_ref[:, CS - 1]
    to_down_ref[NVAR] = rec[CS - 1]
    for c in range(NVAR):
        to_left_ref[c] = f1_ref[c, :, 0, :]
        to_right_ref[c] = f1_ref[c, :, CP - 1, :]
    to_left_ref[NVAR] = rec[:, 0, :]
    to_right_ref[NVAR] = rec[:, CP - 1, :]
    for write in writes:
        write.wait()


def weight_sum(x):
    for by in (32, 16, 8):
        x = x + pltpu.roll(x, LANES - by, 1)
    return x


def spread(values, first):
    lane = lane_ids(values.shape)
    out = jnp.zeros(values.shape, F32)
    for d in range(NVAR):
        at = first + d
        out = jnp.where(
            lane // 8 == d + WEIGHT_AT // 8,
            jnp.broadcast_to(values[:, at : at + 1], values.shape),
            out,
        )
    return out


def outlet_lanes(row):
    return (1 - row) * (LANES - 1), (1 - row) * (LANES - 2) + row


def settle_kernel(
    bands_ref, f1_ref, src_ref, tau_ref, jac_ref, cell_ref, owner_ref,
    part_ref, pack_ref, ids_ref, seen_ref, node_ref, vs,
):
    row = lax.axis_index("row")
    outlet, inner = outlet_lanes(row)
    ghost = 6 - row
    tile = (CP, LANES)
    zero = jnp.zeros(tile, F32)
    lane = lane_ids(tile)
    fill_stencil(
        vs,
        lambda d, j: f1_ref[d, j],
        lambda d: zero,
        lambda d: zero,
        lambda d, j: zero,
        lambda d, j: zero,
        lambda d, j: zero,
        lambda d, j: zero,
    )
    for n in range(6):
        for j in range(CS):
            pack_ref[n, j] = zero

    def advance(c, carry):
        part_ref[c] = f1_ref[c] + tau_ref[...] * (src_ref[c] - image_of(jac_ref, vs, c))
        for n in range(6):
            point = n if n < 5 else ghost
            extra = 1 - row if n < 5 else 2 - 3 * row
            for j in range(CS):
                pack = pack_ref[n, j]
                for d in range(NVAR):
                    at = WEIGHT_AT + 8 * d + c
                    moved = pltpu.roll(jac_ref[point, c, d, j].astype(F32), at + extra, 1)
                    pack = jnp.where(lane == at, moved, pack)
                pack_ref[n, j] = pack
        return carry

    lax.fori_loop(0, NVAR, advance, 0)
    for j in range(CS):
        steps = [
            jnp.sum(jnp.where(lane == at, tau_ref[j], 0.0), axis=1, keepdims=True)
            for at in (outlet, inner)
        ]
        for n in range(6):
            pack_ref[n, j] = pack_ref[n, j] * steps[n // 5]
    square = (LANES, LANES)
    lines = ids_ref.shape[0] // 2
    line = row_ids((lines, LANES))
    first_cell = CS * (line // CP) + 2 * (line % 2)
    even_cell = (lane_ids((lines, LANES)) == first_cell).astype(F32).astype(BF16)
    for of_row in range(2):
        bands = bands_ref[of_row : of_row + 1].astype(F32)
        pair = jnp.where(
            row_ids(square) < LANES // 2,
            jnp.broadcast_to(bands, square),
            jnp.broadcast_to(pltpu.roll(bands, LANES - 1, 1), square),
        )
        ids_ref[lines * of_row : lines * (of_row + 1)] = lax.dot_general(
            even_cell, pair.astype(BF16), (((1,), (1,)), ((), ())), preferred_element_type=F32
        )
    cells = cell_ref[0, 0]
    for j in range(CS):
        here = row_ids(tile) + CP * j == cells // LANES
        for n, at in enumerate((outlet, inner)):
            seen_ref[n, j] = jnp.where(here & (cells % LANES == at), 1.0, 0.0).astype(F32)
    picked = (row_ids(square) == owner_ref[0, 0] % LANES).astype(F32).astype(BF16)
    for n in range(3):
        node_ref[:, LANES * n : LANES * (n + 1)] = picked


def settle_edges_kernel(
    part_ref, jac_ref, tau_ref, up_ref, down_ref, left_ref, right_ref, cell_ref,
    part2_ref, face_ref, sides,
):
    keep = inner_sides()
    tile = (CP, LANES)
    fill_sides(sides, left_ref, right_ref)

    def body(c, carry):
        lost = edge_terms(jac_ref, sides, up_ref, down_ref, keep, c)
        for j in range(CS):
            part2_ref[c, j] = part_ref[c, j] - tau_ref[j] * lost[j]
        return carry

    lax.fori_loop(0, NVAR, body, 0)
    cells = cell_ref[0, 0]
    square = (LANES, LANES)
    axial_pick = (row_ids(square) == cells % LANES).astype(F32).astype(BF16)
    picked = dot3(part2_ref[...].reshape(NVAR * CS * CP, LANES), axial_pick, ((1,), (0,)))
    here = row_ids((CS * CP, LANES)) == cells // LANES
    for c in range(NVAR):
        block = picked[c * CS * CP : (c + 1) * CS * CP]
        face_ref[c : c + 1] = jnp.sum(jnp.where(here, block, 0.0), axis=0, keepdims=True)


def cycle_kernel(
    bands_ref, part_ref, rec_ref, pack_ref, ids_ref, all_ref, up_ref, down_ref, left_ref, right_ref,
    seen_ref, node_ref, face_ref, owner_ref, weight_ref, out_hbm, dense_ref, field, sem,
):
    row = lax.axis_index("row")
    span = lax.axis_index("span")
    outlet, inner = outlet_lanes(row)
    keep = inner_sides()
    tile = (CP, LANES)
    lane, sub = lane_ids(tile), row_ids(tile)
    last_cell = bands_ref.shape[1] - 1
    wanted = [
        bands_ref[row, jnp.clip(span * CS - 1 + t, 0, last_cell)].astype(F32)
        for t in range(CS + 2)
    ]
    half = all_ref.shape[0] // 2
    zero = jnp.zeros(tile, F32)

    def body(i, sums):
        sums = list(sums)
        for n, of_row in enumerate((1 - row, row)):
            at = pl.multiple_of(of_row * half + i * CP, CP)
            ids, values = ids_ref[pl.ds(at, CP), :], all_ref[pl.ds(at, CP), :]
            for t, band in enumerate(wanted):
                k = (CS + 2) * n + t
                sums[k] = sums[k] + jnp.where(ids == band, values, 0.0)
        return tuple(sums)

    sums = lax.fori_loop(0, half // CP, body, (zero,) * (2 * CS + 4), unroll=4)

    def folded(parts):
        rows = [jnp.sum(x, axis=0, keepdims=True) for x in parts]
        whole = jnp.concatenate(rows + [rows[-1]] * (CP - len(rows)), axis=0)
        whole = whole + pltpu.roll(whole, 64, 1)
        return whole, jnp.broadcast_to(whole[:, COUNT_AT : COUNT_AT + 1], tile)

    other, other_count = folded(sums[: CS + 2])
    mine, my_count = folded(sums[CS + 2 :])
    spread0 = spread(other / other_count, 0)
    lost = weight_sum(other * spread(mine / my_count, 0))
    cycle1 = (other - pltpu.roll(lost, LANES - (WEIGHT_AT - FIRST_AT), 1)) / other_count
    spread1 = spread(cycle1, FIRST_AT)

    def shift_of(record, values):
        moved = weight_sum(record * values)
        return moved, spread(moved, WEIGHT_AT)

    own = [shift_of(rec_ref[j], spread0[j + 1 : j + 2]) for j in range(CS)]
    above = shift_of(up_ref[NVAR], spread0[:1])[1] * keep[0]
    below = shift_of(down_ref[NVAR], spread0[CS + 1 : CS + 2])[1] * keep[1]
    left = shift_of(left_ref[NVAR], spread0[1 : 1 + CS])[1]
    right = shift_of(right_ref[NVAR], spread0[1 : 1 + CS])[1]
    changes = []
    for j in range(CS):
        x = own[j][1]
        total = pack_ref[0, j] * x - rec_ref[j] * spread1[j + 1 : j + 2]
        total = total + pack_ref[1, j] * (own[j - 1][1] if j > 0 else above)
        total = total + pack_ref[2, j] * (own[j + 1][1] if j < CS - 1 else below)
        total = total + pack_ref[3, j] * jnp.where(
            sub == 0, jnp.broadcast_to(left[j : j + 1], tile), pltpu.roll(x, 1, 0)
        )
        total = total + pack_ref[4, j] * jnp.where(
            sub == CP - 1, jnp.broadcast_to(right[j : j + 1], tile), pltpu.roll(x, CP - 1, 0)
        )
        changes.append((weight_sum(total) - own[j][0], weight_sum(pack_ref[5, j] * x)))
    wide = [
        [
            [jnp.broadcast_to(x[:, WEIGHT_AT + c : WEIGHT_AT + c + 1], tile) for x in changes[j]]
            for j in range(CS)
        ]
        for c in range(NVAR)
    ]
    for c in range(NVAR):
        for j in range(CS):
            first, second = wide[c][j]
            moved = jnp.where(lane == outlet, first, jnp.where(lane == inner, second, 0.0))
            field[0, c, j] = part_ref[c, j] + moved
    write = pltpu.make_async_copy(field, out_hbm, sem)
    write.start()
    terms = [jnp.zeros((1, LANES), F32)] * 3
    for c in range(NVAR):
        seen = zero
        for j in range(CS):
            first, second = wide[c][j]
            seen = seen + (seen_ref[0, j] * first + seen_ref[1, j] * second)
        value = face_ref[c : c + 1] + jnp.sum(seen, axis=0, keepdims=True)
        for k in range(3):
            at = NVAR * k + c
            terms[k] = terms[k] + weight_ref[0, 0, 0, at : at + 1] * value
    shape = dense_ref.shape
    line = row_ids(shape)
    device = (line * 43691) >> 17
    here = device == owner_ref[0, 0] // LANES
    cycle_rows = (24, LANES)
    coord = row_ids(cycle_rows) % 3
    pieces = []
    for parts in zip(*(split3(x) for x in terms)):
        wide = [jnp.broadcast_to(x.astype(F32), cycle_rows) for x in parts]
        pattern = jnp.where(coord == 0, wide[0], jnp.where(coord == 1, wide[1], wide[2]))
        pattern = jnp.concatenate([pattern] * (shape[0] // 24), axis=0)
        pieces.append(jnp.where(here, pattern, 0.0).astype(BF16))
    dense_ref[...] = lax.dot_general(
        jnp.concatenate(pieces, axis=1),
        node_ref[...],
        (((1,), (1,)), ((), ())),
        preferred_element_type=F32,
    )
    write.wait()


VM = pl.BlockSpec(memory_space=pltpu.VMEM)
SM = pl.BlockSpec(memory_space=pltpu.SMEM)
PARAMS = pltpu.CompilerParams(vmem_limit_bytes=32 * 1024 * 1024)


HBM = pl.BlockSpec(memory_space=pltpu.HBM)


def in_hbm(x):
    return pltpu.with_memory_space_constraint(x, pltpu.HBM)


def call(kernel, name, outs, in_specs, scratch=(), cost=None, out_specs=None):
    outs = [out if isinstance(out[0], tuple) else (out, F32) for out in outs]
    return pl.pallas_call(
        kernel,
        out_shape=tuple(jax.ShapeDtypeStruct(shape, dtype) for shape, dtype in outs),
        in_specs=in_specs,
        out_specs=out_specs or (VM,) * len(outs),
        scratch_shapes=list(scratch),
        compiler_params=PARAMS,
        cost_estimate=cost,
        name=name,
    )


def shifted(value, axis, by):
    devices = lax.axis_size(axis)
    return lax.ppermute(value, axis, [(i, (i + by) % devices) for i in range(devices)])


def over_span(to_up, to_down):
    return shifted(to_down, "span", 1), shifted(to_up, "span", -1)


def over_pitch(to_left, to_right):
    return shifted(to_right, "pitch", 1), shifted(to_left, "pitch", -1)


def on_device(
    adjoint, source, pseudo_step, jac_blocks, band_map, face_cell, face_owner, face_weight
):
    rows, spans, pitches = (lax.axis_size(name) for name in ("row", "span", "pitch"))
    devices = rows * spans * pitches
    peers = spans * pitches
    block = (NVAR, CS, CP, LANES)
    edge = (NVAR, CP, LANES)
    side = (NVAR, CS, LANES)
    edges = call(
        edges_kernel,
        "edges",
        [edge, edge, side, side],
        in_specs=[HBM],
        scratch=[pltpu.SemaphoreType.DMA((4,))],
    )(in_hbm(adjoint))
    halo = over_span(*edges[:2]) + over_pitch(*edges[2:])
    part, record, jac, src, tau = call(
        interior_kernel,
        "interior",
        [block, (CS, CP, LANES), ((7, NVAR) + block, BF16), block, (CS, CP, LANES)],
        in_specs=[HBM] * 4,
        scratch=[
            pltpu.VMEM(block, F32),
            pltpu.VMEM((7 * NVAR, CS, CP, LANES), F32),
            pltpu.VMEM(block, F32),
            pltpu.SemaphoreType.DMA((10,)),
        ],
        cost=pl.CostEstimate(flops=9_000_000, bytes_accessed=3_000_000, transcendentals=0),
    )(*(in_hbm(x) for x in (adjoint, source, pseudo_step, jac_blocks)))
    edge = (NVAR + 1, CP, LANES)
    side = (NVAR + 1, CS, LANES)
    first, message, full_record, *sends = call(
        edge_kernel,
        "edge_update",
        [block, (2 * devices, LANES), (CS, CP, LANES), edge, edge, side, side],
        in_specs=[VM] * 8,
        out_specs=(VM, HBM) + (VM,) * 5,
        scratch=[
            pltpu.VMEM((2 * NVAR, CS, CP, LANES), F32),
            pltpu.VMEM((2 * devices // 8, LANES), F32),
            pltpu.SemaphoreType.DMA((8,)),
        ],
    )(part, record, jac, tau, *halo)
    records = lax.all_to_all(
        message.reshape(devices, 1, 2 * LANES), ("row", "span", "pitch"), 0, 0
    ).reshape(2 * devices, LANES)
    halo = over_span(*sends[:2]) + over_pitch(*sends[2:])
    part, packs, ids, seen, picks = call(
        settle_kernel,
        "settle",
        [
            block, (6, CS, CP, LANES), ((2 * devices, LANES), F32), (2, CS, CP, LANES),
            ((LANES, 3 * LANES), BF16),
        ],
        in_specs=[VM] * 7,
        scratch=[pltpu.VMEM((7 * NVAR, CS, CP, LANES), F32)],
        cost=pl.CostEstimate(flops=9_000_000, bytes_accessed=3_000_000, transcendentals=0),
    )(band_map, first, src, tau, jac, face_cell, face_owner)
    part, faces = call(
        settle_edges_kernel,
        "settle_edges",
        [block, (CP, LANES)],
        in_specs=[VM] * 8,
        scratch=[pltpu.VMEM((2 * NVAR, CS, CP, LANES), F32)],
        cost=pl.CostEstimate(flops=3_000_000, bytes_accessed=2_000_000, transcendentals=0),
    )(part, jac, tau, *halo, face_cell)
    field, dense = call(
        cycle_kernel,
        "cycle_update",
        [(1,) + block, (3 * peers, LANES)],
        in_specs=[SM] + [VM] * 14,
        out_specs=(HBM, VM),
        scratch=[pltpu.VMEM((1,) + block, F32), pltpu.SemaphoreType.DMA],
    )(
        band_map, part, full_record, packs, ids, records, *halo, seen, picks, faces, face_owner,
        face_weight,
    )
    parts = lax.all_to_all(dense.reshape(peers, 1, 3 * LANES), ("span", "pitch"), 0, 0)
    nodes = jnp.sum(parts, axis=(0, 1)).reshape(1, 3, LANES)
    return field, nodes


def solution(mesh):
    in_specs = (
        P("row", None, "span", "pitch", None),
        P("row", None, "span", "pitch", None),
        P("row", "span", "pitch", None),
        P("row", None, None, None, "span", "pitch", None),
        P(),
        P("row", "span", "pitch", None),
        P("row", "span", "pitch", None),
        P("row", "span", "pitch", None, None),
    )
    out_specs = (P("row", None, "span", "pitch", None), P("row", None, ("span", "pitch")))
    return jax.shard_map(
        on_device, mesh=mesh, in_specs=in_specs, out_specs=out_specs, check_vma=False
    )
```

```python
import jax
import jax.numpy as jnp
from jax import lax
from jax.experimental import pallas as pl
from jax.experimental.pallas import tpu as pltpu
from jax.sharding import PartitionSpec as P

NVAR = 6
CS = 4
CP = 8
LANES = 128
F32 = jnp.float32
BF16 = jnp.bfloat16
FIRST_AT = 8
WEIGHT_AT = 16
COUNT_AT = 6


def lane_ids(shape):
    return lax.broadcasted_iota(jnp.int32, shape, len(shape) - 1)


def row_ids(shape):
    return lax.broadcasted_iota(jnp.int32, shape, len(shape) - 2)


def split3(x):
    hi = x.astype(BF16)
    rest = x - hi.astype(F32)
    mid = rest.astype(BF16)
    low = (rest - mid.astype(F32)).astype(BF16)
    return hi, mid, low


def dot3(x, onehot, dims):
    parts = [
        lax.dot_general(part, onehot, (dims, ((), ())), preferred_element_type=F32)
        for part in split3(x)
    ]
    return parts[0] + (parts[1] + parts[2])


def fill_stencil(vs, field, up, down, left, right, lower, upper):
    tile = (CP, LANES)
    lane, sub = lane_ids(tile), row_ids(tile)
    for d in range(NVAR):
        for j in range(CS):
            x = field(d, j)
            vs[d, j] = x
            vs[6 + d, j] = field(d, j - 1) if j > 0 else up(d)
            vs[12 + d, j] = field(d, j + 1) if j < CS - 1 else down(d)
            vs[18 + d, j] = jnp.where(
                sub == 0, jnp.broadcast_to(left(d, j), tile), pltpu.roll(x, 1, 0)
            )
            vs[24 + d, j] = jnp.where(
                sub == CP - 1, jnp.broadcast_to(right(d, j), tile), pltpu.roll(x, CP - 1, 0)
            )
            vs[30 + d, j] = jnp.where(lane == 0, lower(d, j), pltpu.roll(x, 1, 1))
            vs[36 + d, j] = jnp.where(lane == LANES - 1, upper(d, j), pltpu.roll(x, LANES - 1, 1))


def image_of(jac_ref, vs, c):
    acc = jnp.zeros((CS, CP, LANES), F32)
    for s in range(7):
        for d in range(NVAR):
            acc = acc + jac_ref[s, c, d].astype(F32) * vs[6 * s + d]
    return acc


def edges_kernel(adj_ref, up_ref, down_ref, left_ref, right_ref, sems):
    adj = adj_ref.at[0]
    copies = [
        pltpu.make_async_copy(adj.at[:, 0], up_ref, sems.at[0]),
        pltpu.make_async_copy(adj.at[:, CS - 1], down_ref, sems.at[1]),
        pltpu.make_async_copy(adj.at[:, :, 0], left_ref, sems.at[2]),
        pltpu.make_async_copy(adj.at[:, :, CP - 1], right_ref, sems.at[3]),
    ]
    for copy in copies:
        copy.start()
    for copy in copies:
        copy.wait()


def interior_kernel(
    adj_hbm, src_hbm, tau_hbm, jac_hbm, part_ref, rec_ref, jac_ref, src_ref, tau_ref, adj_ref, vs,
    image, sems,
):
    row = lax.axis_index("row")
    outlet = (1 - row) * (LANES - 1)
    ghost = 6 - row
    tile = (CP, LANES)
    zero = jnp.zeros(tile, F32)
    lane = lane_ids(tile)
    load_adj = pltpu.make_async_copy(adj_hbm.at[0], adj_ref, sems.at[0])
    load_jac = [
        pltpu.make_async_copy(jac_hbm.at[0, s], jac_ref.at[s], sems.at[1 + s]) for s in range(7)
    ]
    load_tau = pltpu.make_async_copy(tau_hbm.at[0], tau_ref, sems.at[8])
    load_src = pltpu.make_async_copy(src_hbm.at[0], src_ref, sems.at[9])
    order = (5, 6, 0, 1, 2, 3, 4)
    for copy in [load_adj] + [load_jac[s] for s in order] + [load_tau, load_src]:
        copy.start()
    load_adj.wait()
    fill_stencil(
        vs,
        lambda d, j: adj_ref[d, j],
        lambda d: zero,
        lambda d: zero,
        lambda d, j: zero,
        lambda d, j: zero,
        lambda d, j: zero,
        lambda d, j: zero,
    )

    def image_part(c, points, acc):
        for s in points:
            for d in range(NVAR):
                acc = acc + jac_ref[s, c, d].astype(F32) * vs[6 * s + d]
        return acc

    load_jac[5].wait()
    load_jac[6].wait()

    def axial(c, carry):
        weights, sums = (list(x) for x in carry)
        image[c] = image_part(c, (5, 6), jnp.zeros((CS, CP, LANES), F32))
        for j in range(CS):
            for d in range(NVAR):
                at = WEIGHT_AT + 8 * d + c
                moved = pltpu.roll(jac_ref[ghost, c, d, j].astype(F32), at + 1 - row, 1)
                weights[j] = jnp.where(lane == at, moved, weights[j])
            sums[j] = jnp.where(lane == c, pltpu.roll(adj_ref[c, j], c + 1 - row, 1), sums[j])
        return tuple(weights), tuple(sums)

    ones = jnp.where(lane == COUNT_AT, 1.0, 0.0).astype(F32)
    weights, sums = lax.fori_loop(0, NVAR, axial, ((zero,) * CS, (ones,) * CS))
    load_tau.wait()
    for j in range(CS):
        tau_out = jnp.sum(jnp.where(lane == outlet, tau_ref[j], 0.0), axis=1, keepdims=True)
        rec_ref[j] = sums[j] + weights[j] * tau_out
    for s in range(5):
        load_jac[s].wait()
    load_src.wait()

    def finish(c, carry):
        lost = image_part(c, range(5), image[c])
        part_ref[c] = adj_ref[c] + tau_ref[...] * (src_ref[c] - lost)
        return carry

    lax.fori_loop(0, NVAR, finish, 0)


def inner_sides():
    span = lax.axis_index("span")
    return (
        jnp.where(span > 0, 1.0, 0.0).astype(F32),
        jnp.where(span < lax.axis_size("span") - 1, 1.0, 0.0).astype(F32),
    )


def fill_sides(sides, left_ref, right_ref):
    tile = (CP, LANES)
    sub = row_ids(tile)
    for d in range(NVAR):
        for j in range(CS):
            sides[d, j] = jnp.where(
                sub == 0, jnp.broadcast_to(left_ref[d, j : j + 1], tile), 0.0
            )
            sides[NVAR + d, j] = jnp.where(
                sub == CP - 1, jnp.broadcast_to(right_ref[d, j : j + 1], tile), 0.0
            )


def edge_terms(jac_ref, sides, up_ref, down_ref, keep, c):
    acc = jnp.zeros((CS, CP, LANES), F32)
    first = jnp.zeros((CP, LANES), F32)
    last = jnp.zeros((CP, LANES), F32)
    for d in range(NVAR):
        acc = acc + jac_ref[3, c, d].astype(F32) * sides[d]
        acc = acc + jac_ref[4, c, d].astype(F32) * sides[NVAR + d]
        first = first + jac_ref[1, c, d, 0].astype(F32) * up_ref[d]
        last = last + jac_ref[2, c, d, CS - 1].astype(F32) * down_ref[d]
    lost = [acc[j] for j in range(CS)]
    lost[0] = lost[0] + first * keep[0]
    lost[CS - 1] = lost[CS - 1] + last * keep[1]
    return lost


def edge_kernel(
    part_ref, rec_in, jac_ref, tau_ref, up_ref, down_ref, left_ref, right_ref,
    f1_ref, msg_hbm, rec, to_up_ref, to_down_ref, to_left_ref, to_right_ref, sides, copies, sems,
):
    row = lax.axis_index("row")
    keep = inner_sides()
    tile = (CP, LANES)
    lane, sub = lane_ids(tile), row_ids(tile)
    fill_sides(sides, left_ref, right_ref)

    def body(c, sums):
        sums = list(sums)
        lost = edge_terms(jac_ref, sides, up_ref, down_ref, keep, c)
        at = FIRST_AT + c
        for j in range(CS):
            new = part_ref[c, j] - tau_ref[j] * lost[j]
            f1_ref[c, j] = new
            sums[j] = jnp.where(lane == at, pltpu.roll(new, at + 1 - row, 1), sums[j])
        return tuple(sums)

    sums = lax.fori_loop(0, NVAR, body, tuple(rec_in[j] for j in range(CS)))
    rows = []
    for j in range(CS):
        rec[j] = sums[j]
        rows.append(jnp.sum(sums[j], axis=0, keepdims=True))
    halves = [
        jnp.broadcast_to(rows[2 * h] + pltpu.roll(rows[2 * h + 1], 64, 1), tile) for h in range(2)
    ]
    packed = jnp.where(sub % 2 == 0, halves[0], halves[1])
    lines = copies.shape[0]
    for i in range(lines // CP):
        copies[CP * i : CP * (i + 1)] = packed
    writes = [
        pltpu.make_async_copy(copies, msg_hbm.at[pl.ds(lines * i, lines)], sems.at[i])
        for i in range(msg_hbm.shape[0] // lines)
    ]
    for write in writes:
        write.start()
    to_up_ref[0:NVAR] = f1_ref[:, 0]
    to_up_ref[NVAR] = rec[0]
    to_down_ref[0:NVAR] = f1_ref[:, CS - 1]
    to_down_ref[NVAR] = rec[CS - 1]
    for c in range(NVAR):
        to_left_ref[c] = f1_ref[c, :, 0, :]
        to_right_ref[c] = f1_ref[c, :, CP - 1, :]
    to_left_ref[NVAR] = rec[:, 0, :]
    to_right_ref[NVAR] = rec[:, CP - 1, :]
    for write in writes:
        write.wait()


def weight_sum(x):
    moved = [pltpu.roll(x, LANES - 8 * d, 1) for d in range(1, NVAR)]
    return ((x + moved[0]) + (moved[1] + moved[2])) + (moved[3] + moved[4])


def spread(values, first):
    lane = lane_ids(values.shape)
    out = jnp.zeros(values.shape, F32)
    for d in range(NVAR):
        at = first + d
        out = jnp.where(
            lane // 8 == d + WEIGHT_AT // 8,
            jnp.broadcast_to(values[:, at : at + 1], values.shape),
            out,
        )
    return out


def outlet_lanes(row):
    return (1 - row) * (LANES - 1), (1 - row) * (LANES - 2) + row


def settle_kernel(
    bands_ref, f1_ref, src_ref, tau_ref, jac_ref, cell_ref, owner_ref,
    part_ref, pack_ref, ids_ref, seen_ref, node_ref, vs,
):
    row = lax.axis_index("row")
    outlet, inner = outlet_lanes(row)
    ghost = 6 - row
    tile = (CP, LANES)
    zero = jnp.zeros(tile, F32)
    lane = lane_ids(tile)
    fill_stencil(
        vs,
        lambda d, j: f1_ref[d, j],
        lambda d: zero,
        lambda d: zero,
        lambda d, j: zero,
        lambda d, j: zero,
        lambda d, j: zero,
        lambda d, j: zero,
    )
    for n in range(6):
        for j in range(CS):
            pack_ref[n, j] = zero

    def advance(c, carry):
        part_ref[c] = f1_ref[c] + tau_ref[...] * (src_ref[c] - image_of(jac_ref, vs, c))
        for n in range(6):
            point = n if n < 5 else ghost
            extra = 1 - row if n < 5 else 2 - 3 * row
            for j in range(CS):
                pack = pack_ref[n, j]
                for d in range(NVAR):
                    at = WEIGHT_AT + 8 * d + c
                    moved = pltpu.roll(jac_ref[point, c, d, j].astype(F32), at + extra, 1)
                    pack = jnp.where(lane == at, moved, pack)
                pack_ref[n, j] = pack
        return carry

    lax.fori_loop(0, NVAR, advance, 0)
    for j in range(CS):
        steps = [
            jnp.sum(jnp.where(lane == at, tau_ref[j], 0.0), axis=1, keepdims=True)
            for at in (outlet, inner)
        ]
        for n in range(6):
            pack_ref[n, j] = pack_ref[n, j] * steps[n // 5]
    square = (LANES, LANES)
    lines = ids_ref.shape[0] // 2
    line = row_ids((lines, LANES))
    first_cell = CS * (line // CP) + 2 * (line % 2)
    even_cell = (lane_ids((lines, LANES)) == first_cell).astype(F32).astype(BF16)
    for of_row in range(2):
        bands = bands_ref[of_row : of_row + 1].astype(F32)
        pair = jnp.where(
            row_ids(square) < LANES // 2,
            jnp.broadcast_to(bands, square),
            jnp.broadcast_to(pltpu.roll(bands, LANES - 1, 1), square),
        )
        ids_ref[lines * of_row : lines * (of_row + 1)] = lax.dot_general(
            even_cell, pair.astype(BF16), (((1,), (1,)), ((), ())), preferred_element_type=F32
        )
    cells = cell_ref[0, 0]
    for j in range(CS):
        here = row_ids(tile) + CP * j == cells // LANES
        for n, at in enumerate((outlet, inner)):
            seen_ref[n, j] = jnp.where(here & (cells % LANES == at), 1.0, 0.0).astype(F32)
    picked = (row_ids(square) == owner_ref[0, 0] % LANES).astype(F32).astype(BF16)
    for n in range(3):
        node_ref[:, LANES * n : LANES * (n + 1)] = picked


def settle_edges_kernel(
    part_ref, jac_ref, tau_ref, up_ref, down_ref, left_ref, right_ref, cell_ref,
    part2_ref, face_ref, sides,
):
    keep = inner_sides()
    tile = (CP, LANES)
    fill_sides(sides, left_ref, right_ref)

    def body(c, carry):
        lost = edge_terms(jac_ref, sides, up_ref, down_ref, keep, c)
        for j in range(CS):
            part2_ref[c, j] = part_ref[c, j] - tau_ref[j] * lost[j]
        return carry

    lax.fori_loop(0, NVAR, body, 0)
    cells = cell_ref[0, 0]
    square = (LANES, LANES)
    axial_pick = (row_ids(square) == cells % LANES).astype(F32).astype(BF16)
    picked = dot3(part2_ref[...].reshape(NVAR * CS * CP, LANES), axial_pick, ((1,), (0,)))
    here = row_ids((CS * CP, LANES)) == cells // LANES
    for c in range(NVAR):
        block = picked[c * CS * CP : (c + 1) * CS * CP]
        face_ref[c : c + 1] = jnp.sum(jnp.where(here, block, 0.0), axis=0, keepdims=True)


def cycle_kernel(
    bands_ref, part_ref, rec_ref, pack_ref, ids_ref, all_ref, up_ref, down_ref, left_ref, right_ref,
    seen_ref, node_ref, face_ref, owner_ref, weight_ref, out_hbm, dense_ref, field, sem,
):
    row = lax.axis_index("row")
    span = lax.axis_index("span")
    outlet, inner = outlet_lanes(row)
    keep = inner_sides()
    tile = (CP, LANES)
    lane, sub = lane_ids(tile), row_ids(tile)
    last_cell = bands_ref.shape[1] - 1
    wanted = [
        bands_ref[row, jnp.clip(span * CS - 1 + t, 0, last_cell)].astype(F32)
        for t in range(CS + 2)
    ]
    half = all_ref.shape[0] // 2
    zero = jnp.zeros(tile, F32)

    def body(i, sums):
        sums = list(sums)
        for n, of_row in enumerate((1 - row, row)):
            at = pl.multiple_of(of_row * half + i * CP, CP)
            ids, values = ids_ref[pl.ds(at, CP), :], all_ref[pl.ds(at, CP), :]
            for t, band in enumerate(wanted):
                k = (CS + 2) * n + t
                sums[k] = sums[k] + jnp.where(ids == band, values, 0.0)
        return tuple(sums)

    sums = lax.fori_loop(0, half // CP, body, (zero,) * (2 * CS + 4), unroll=8)

    def folded(parts):
        rows = [jnp.sum(x, axis=0, keepdims=True) for x in parts]
        whole = jnp.concatenate(rows + [rows[-1]] * (CP - len(rows)), axis=0)
        whole = whole + pltpu.roll(whole, 64, 1)
        return whole, jnp.broadcast_to(whole[:, COUNT_AT : COUNT_AT + 1], tile)

    other, other_count = folded(sums[: CS + 2])
    mine, my_count = folded(sums[CS + 2 :])
    spread0 = spread(other / other_count, 0)
    lost = weight_sum(other * spread(mine / my_count, 0))
    cycle1 = (other - pltpu.roll(lost, LANES - (WEIGHT_AT - FIRST_AT), 1)) / other_count
    spread1 = spread(cycle1, FIRST_AT)

    def shift_of(record, values):
        moved = weight_sum(record * values)
        return moved, spread(moved, WEIGHT_AT)

    own = [shift_of(rec_ref[j], spread0[j + 1 : j + 2]) for j in range(CS)]
    above = shift_of(up_ref[NVAR], spread0[:1])[1] * keep[0]
    below = shift_of(down_ref[NVAR], spread0[CS + 1 : CS + 2])[1] * keep[1]
    left = shift_of(left_ref[NVAR], spread0[1 : 1 + CS])[1]
    right = shift_of(right_ref[NVAR], spread0[1 : 1 + CS])[1]
    changes = []
    for j in range(CS):
        x = own[j][1]
        total = pack_ref[0, j] * x - rec_ref[j] * spread1[j + 1 : j + 2]
        total = total + pack_ref[1, j] * (own[j - 1][1] if j > 0 else above)
        total = total + pack_ref[2, j] * (own[j + 1][1] if j < CS - 1 else below)
        total = total + pack_ref[3, j] * jnp.where(
            sub == 0, jnp.broadcast_to(left[j : j + 1], tile), pltpu.roll(x, 1, 0)
        )
        total = total + pack_ref[4, j] * jnp.where(
            sub == CP - 1, jnp.broadcast_to(right[j : j + 1], tile), pltpu.roll(x, CP - 1, 0)
        )
        changes.append((weight_sum(total) - own[j][0], weight_sum(pack_ref[5, j] * x)))
    wide = [
        [
            [jnp.broadcast_to(x[:, WEIGHT_AT + c : WEIGHT_AT + c + 1], tile) for x in changes[j]]
            for j in range(CS)
        ]
        for c in range(NVAR)
    ]
    for c in range(NVAR):
        for j in range(CS):
            first, second = wide[c][j]
            moved = jnp.where(lane == outlet, first, jnp.where(lane == inner, second, 0.0))
            field[0, c, j] = part_ref[c, j] + moved
    write = pltpu.make_async_copy(field, out_hbm, sem)
    write.start()
    terms = [jnp.zeros((1, LANES), F32)] * 3
    for c in range(NVAR):
        seen = zero
        for j in range(CS):
            first, second = wide[c][j]
            seen = seen + (seen_ref[0, j] * first + seen_ref[1, j] * second)
        value = face_ref[c : c + 1] + jnp.sum(seen, axis=0, keepdims=True)
        for k in range(3):
            at = NVAR * k + c
            terms[k] = terms[k] + weight_ref[0, 0, 0, at : at + 1] * value
    shape = dense_ref.shape
    line = row_ids(shape)
    device = (line * 43691) >> 17
    here = device == owner_ref[0, 0] // LANES
    cycle_rows = (24, LANES)
    coord = row_ids(cycle_rows) % 3
    pieces = []
    for parts in zip(*(split3(x) for x in terms)):
        wide = [jnp.broadcast_to(x.astype(F32), cycle_rows) for x in parts]
        pattern = jnp.where(coord == 0, wide[0], jnp.where(coord == 1, wide[1], wide[2]))
        pattern = jnp.concatenate([pattern] * (shape[0] // 24), axis=0)
        pieces.append(jnp.where(here, pattern, 0.0).astype(BF16))
    dense_ref[...] = lax.dot_general(
        jnp.concatenate(pieces, axis=1),
        node_ref[...],
        (((1,), (1,)), ((), ())),
        preferred_element_type=F32,
    )
    write.wait()


VM = pl.BlockSpec(memory_space=pltpu.VMEM)
SM = pl.BlockSpec(memory_space=pltpu.SMEM)
PARAMS = pltpu.CompilerParams(vmem_limit_bytes=32 * 1024 * 1024)


HBM = pl.BlockSpec(memory_space=pltpu.HBM)


def in_hbm(x):
    return pltpu.with_memory_space_constraint(x, pltpu.HBM)


def call(kernel, name, outs, in_specs, scratch=(), cost=None, out_specs=None):
    outs = [out if isinstance(out[0], tuple) else (out, F32) for out in outs]
    return pl.pallas_call(
        kernel,
        out_shape=tuple(jax.ShapeDtypeStruct(shape, dtype) for shape, dtype in outs),
        in_specs=in_specs,
        out_specs=out_specs or (VM,) * len(outs),
        scratch_shapes=list(scratch),
        compiler_params=PARAMS,
        cost_estimate=cost,
        name=name,
    )


def shifted(value, axis, by):
    devices = lax.axis_size(axis)
    return lax.ppermute(value, axis, [(i, (i + by) % devices) for i in range(devices)])


def over_span(to_up, to_down):
    return shifted(to_down, "span", 1), shifted(to_up, "span", -1)


def over_pitch(to_left, to_right):
    return shifted(to_right, "pitch", 1), shifted(to_left, "pitch", -1)


def on_device(
    adjoint, source, pseudo_step, jac_blocks, band_map, face_cell, face_owner, face_weight
):
    rows, spans, pitches = (lax.axis_size(name) for name in ("row", "span", "pitch"))
    devices = rows * spans * pitches
    peers = spans * pitches
    block = (NVAR, CS, CP, LANES)
    edge = (NVAR, CP, LANES)
    side = (NVAR, CS, LANES)
    edges = call(
        edges_kernel,
        "edges",
        [edge, edge, side, side],
        in_specs=[HBM],
        scratch=[pltpu.SemaphoreType.DMA((4,))],
    )(in_hbm(adjoint))
    halo = over_span(*edges[:2]) + over_pitch(*edges[2:])
    part, record, jac, src, tau = call(
        interior_kernel,
        "interior",
        [block, (CS, CP, LANES), ((7, NVAR) + block, BF16), block, (CS, CP, LANES)],
        in_specs=[HBM] * 4,
        scratch=[
            pltpu.VMEM(block, F32),
            pltpu.VMEM((7 * NVAR, CS, CP, LANES), F32),
            pltpu.VMEM(block, F32),
            pltpu.SemaphoreType.DMA((10,)),
        ],
        cost=pl.CostEstimate(flops=9_000_000, bytes_accessed=3_000_000, transcendentals=0),
    )(*(in_hbm(x) for x in (adjoint, source, pseudo_step, jac_blocks)))
    edge = (NVAR + 1, CP, LANES)
    side = (NVAR + 1, CS, LANES)
    first, message, full_record, *sends = call(
        edge_kernel,
        "edge_update",
        [block, (2 * devices, LANES), (CS, CP, LANES), edge, edge, side, side],
        in_specs=[VM] * 8,
        out_specs=(VM, HBM) + (VM,) * 5,
        scratch=[
            pltpu.VMEM((2 * NVAR, CS, CP, LANES), F32),
            pltpu.VMEM((2 * devices // 8, LANES), F32),
            pltpu.SemaphoreType.DMA((8,)),
        ],
    )(part, record, jac, tau, *halo)
    records = lax.all_to_all(
        message.reshape(devices, 1, 2 * LANES), ("row", "span", "pitch"), 0, 0
    ).reshape(2 * devices, LANES)
    halo = over_span(*sends[:2]) + over_pitch(*sends[2:])
    part, packs, ids, seen, picks = call(
        settle_kernel,
        "settle",
        [
            block, (6, CS, CP, LANES), ((2 * devices, LANES), F32), (2, CS, CP, LANES),
            ((LANES, 3 * LANES), BF16),
        ],
        in_specs=[VM] * 7,
        scratch=[pltpu.VMEM((7 * NVAR, CS, CP, LANES), F32)],
        cost=pl.CostEstimate(flops=9_000_000, bytes_accessed=3_000_000, transcendentals=0),
    )(band_map, first, src, tau, jac, face_cell, face_owner)
    part, faces = call(
        settle_edges_kernel,
        "settle_edges",
        [block, (CP, LANES)],
        in_specs=[VM] * 8,
        scratch=[pltpu.VMEM((2 * NVAR, CS, CP, LANES), F32)],
        cost=pl.CostEstimate(flops=3_000_000, bytes_accessed=2_000_000, transcendentals=0),
    )(part, jac, tau, *halo, face_cell)
    field, dense = call(
        cycle_kernel,
        "cycle_update",
        [(1,) + block, (3 * peers, LANES)],
        in_specs=[SM] + [VM] * 14,
        out_specs=(HBM, VM),
        scratch=[pltpu.VMEM((1,) + block, F32), pltpu.SemaphoreType.DMA],
    )(
        band_map, part, full_record, packs, ids, records, *halo, seen, picks, faces, face_owner,
        face_weight,
    )
    parts = lax.all_to_all(dense.reshape(peers, 1, 3 * LANES), ("span", "pitch"), 0, 0)
    nodes = jnp.sum(parts, axis=(0, 1)).reshape(1, 3, LANES)
    return field, nodes


def solution(mesh):
    in_specs = (
        P("row", None, "span", "pitch", None),
        P("row", None, "span", "pitch", None),
        P("row", "span", "pitch", None),
        P("row", None, None, None, "span", "pitch", None),
        P(),
        P("row", "span", "pitch", None),
        P("row", "span", "pitch", None),
        P("row", "span", "pitch", None, None),
    )
    out_specs = (P("row", None, "span", "pitch", None), P("row", None, ("span", "pitch")))
    return jax.shard_map(
        on_device, mesh=mesh, in_specs=in_specs, out_specs=out_specs, check_vma=False
    )
```

```python
import jax
import jax.numpy as jnp
from jax import lax
from jax.experimental import pallas as pl
from jax.experimental.pallas import tpu as pltpu
from jax.sharding import PartitionSpec as P

NVAR = 6
CS = 4
CP = 8
LANES = 128
F32 = jnp.float32
BF16 = jnp.bfloat16
FIRST_AT = 8
WEIGHT_AT = 16
COUNT_AT = 6


def lane_ids(shape):
    return lax.broadcasted_iota(jnp.int32, shape, len(shape) - 1)


def row_ids(shape):
    return lax.broadcasted_iota(jnp.int32, shape, len(shape) - 2)


def split3(x):
    hi = x.astype(BF16)
    rest = x - hi.astype(F32)
    mid = rest.astype(BF16)
    low = (rest - mid.astype(F32)).astype(BF16)
    return hi, mid, low


def dot3(x, onehot, dims):
    parts = [
        lax.dot_general(part, onehot, (dims, ((), ())), preferred_element_type=F32)
        for part in split3(x)
    ]
    return parts[0] + (parts[1] + parts[2])


def fill_stencil(vs, field, up, down, left, right, lower, upper):
    tile = (CP, LANES)
    lane, sub = lane_ids(tile), row_ids(tile)
    for d in range(NVAR):
        for j in range(CS):
            x = field(d, j)
            vs[d, j] = x
            vs[6 + d, j] = field(d, j - 1) if j > 0 else up(d)
            vs[12 + d, j] = field(d, j + 1) if j < CS - 1 else down(d)
            vs[18 + d, j] = jnp.where(
                sub == 0, jnp.broadcast_to(left(d, j), tile), pltpu.roll(x, 1, 0)
            )
            vs[24 + d, j] = jnp.where(
                sub == CP - 1, jnp.broadcast_to(right(d, j), tile), pltpu.roll(x, CP - 1, 0)
            )
            vs[30 + d, j] = jnp.where(lane == 0, lower(d, j), pltpu.roll(x, 1, 1))
            vs[36 + d, j] = jnp.where(lane == LANES - 1, upper(d, j), pltpu.roll(x, LANES - 1, 1))


def image_of(jac_ref, vs, c):
    acc = jnp.zeros((CS, CP, LANES), F32)
    for s in range(7):
        for d in range(NVAR):
            acc = acc + jac_ref[s, c, d].astype(F32) * vs[6 * s + d]
    return acc


def edges_kernel(adj_ref, up_ref, down_ref, left_ref, right_ref, sems):
    adj = adj_ref.at[0]
    copies = [
        pltpu.make_async_copy(adj.at[:, 0], up_ref, sems.at[0]),
        pltpu.make_async_copy(adj.at[:, CS - 1], down_ref, sems.at[1]),
        pltpu.make_async_copy(adj.at[:, :, 0], left_ref, sems.at[2]),
        pltpu.make_async_copy(adj.at[:, :, CP - 1], right_ref, sems.at[3]),
    ]
    for copy in copies:
        copy.start()
    for copy in copies:
        copy.wait()


def interior_kernel(adj_ref, src_ref, tau_ref, jac_ref, part_ref, rec_ref, vs):
    row = lax.axis_index("row")
    outlet = (1 - row) * (LANES - 1)
    ghost = 6 - row
    tile = (CP, LANES)
    zero = jnp.zeros(tile, F32)
    lane = lane_ids(tile)
    fill_stencil(
        vs,
        lambda d, j: adj_ref[d, j],
        lambda d: zero,
        lambda d: zero,
        lambda d, j: zero,
        lambda d, j: zero,
        lambda d, j: zero,
        lambda d, j: zero,
    )

    def advance(c, carry):
        weights, sums = (list(x) for x in carry)
        part_ref[c] = adj_ref[c] + tau_ref[...] * (src_ref[c] - image_of(jac_ref, vs, c))
        for j in range(CS):
            for d in range(NVAR):
                at = WEIGHT_AT + 8 * d + c
                moved = pltpu.roll(jac_ref[ghost, c, d, j].astype(F32), at + 1 - row, 1)
                weights[j] = jnp.where(lane == at, moved, weights[j])
            sums[j] = jnp.where(lane == c, pltpu.roll(adj_ref[c, j], c + 1 - row, 1), sums[j])
        return tuple(weights), tuple(sums)

    ones = jnp.where(lane == COUNT_AT, 1.0, 0.0).astype(F32)
    weights, sums = lax.fori_loop(0, NVAR, advance, ((zero,) * CS, (ones,) * CS))
    for j in range(CS):
        tau_out = jnp.sum(jnp.where(lane == outlet, tau_ref[j], 0.0), axis=1, keepdims=True)
        rec_ref[j] = sums[j] + weights[j] * tau_out


def inner_sides():
    span = lax.axis_index("span")
    return (
        jnp.where(span > 0, 1.0, 0.0).astype(F32),
        jnp.where(span < lax.axis_size("span") - 1, 1.0, 0.0).astype(F32),
    )


def fill_sides(sides, left_ref, right_ref):
    tile = (CP, LANES)
    sub = row_ids(tile)
    for d in range(NVAR):
        for j in range(CS):
            sides[d, j] = jnp.where(
                sub == 0, jnp.broadcast_to(left_ref[d, j : j + 1], tile), 0.0
            )
            sides[NVAR + d, j] = jnp.where(
                sub == CP - 1, jnp.broadcast_to(right_ref[d, j : j + 1], tile), 0.0
            )


def edge_terms(jac_ref, sides, up_ref, down_ref, keep, c):
    acc = jnp.zeros((CS, CP, LANES), F32)
    first = jnp.zeros((CP, LANES), F32)
    last = jnp.zeros((CP, LANES), F32)
    for d in range(NVAR):
        acc = acc + jac_ref[3, c, d].astype(F32) * sides[d]
        acc = acc + jac_ref[4, c, d].astype(F32) * sides[NVAR + d]
        first = first + jac_ref[1, c, d, 0].astype(F32) * up_ref[d]
        last = last + jac_ref[2, c, d, CS - 1].astype(F32) * down_ref[d]
    lost = [acc[j] for j in range(CS)]
    lost[0] = lost[0] + first * keep[0]
    lost[CS - 1] = lost[CS - 1] + last * keep[1]
    return lost


def edge_kernel(
    part_ref, rec_in, jac_ref, tau_ref, up_ref, down_ref, left_ref, right_ref,
    f1_ref, msg_hbm, rec, to_up_ref, to_down_ref, to_left_ref, to_right_ref, sides, copies, sems,
):
    row = lax.axis_index("row")
    keep = inner_sides()
    tile = (CP, LANES)
    lane, sub = lane_ids(tile), row_ids(tile)
    fill_sides(sides, left_ref, right_ref)

    def body(c, sums):
        sums = list(sums)
        lost = edge_terms(jac_ref, sides, up_ref, down_ref, keep, c)
        at = FIRST_AT + c
        for j in range(CS):
            new = part_ref[c, j] - tau_ref[j] * lost[j]
            f1_ref[c, j] = new
            sums[j] = jnp.where(lane == at, pltpu.roll(new, at + 1 - row, 1), sums[j])
        return tuple(sums)

    sums = lax.fori_loop(0, NVAR, body, tuple(rec_in[j] for j in range(CS)))
    rows = []
    for j in range(CS):
        rec[j] = sums[j]
        rows.append(jnp.sum(sums[j], axis=0, keepdims=True))
    halves = [
        jnp.broadcast_to(rows[2 * h] + pltpu.roll(rows[2 * h + 1], 64, 1), tile) for h in range(2)
    ]
    packed = jnp.where(sub % 2 == 0, halves[0], halves[1])
    lines = copies.shape[0]
    for i in range(lines // CP):
        copies[CP * i : CP * (i + 1)] = packed
    writes = [
        pltpu.make_async_copy(copies, msg_hbm.at[pl.ds(lines * i, lines)], sems.at[i])
        for i in range(msg_hbm.shape[0] // lines)
    ]
    for write in writes:
        write.start()
    to_up_ref[0:NVAR] = f1_ref[:, 0]
    to_up_ref[NVAR] = rec[0]
    to_down_ref[0:NVAR] = f1_ref[:, CS - 1]
    to_down_ref[NVAR] = rec[CS - 1]
    for c in range(NVAR):
        to_left_ref[c] = f1_ref[c, :, 0, :]
        to_right_ref[c] = f1_ref[c, :, CP - 1, :]
    to_left_ref[NVAR] = rec[:, 0, :]
    to_right_ref[NVAR] = rec[:, CP - 1, :]
    for write in writes:
        write.wait()


def weight_sum(x):
    moved = [pltpu.roll(x, LANES - 8 * d, 1) for d in range(1, NVAR)]
    return ((x + moved[0]) + (moved[1] + moved[2])) + (moved[3] + moved[4])


def spread(values, first):
    lane = lane_ids(values.shape)
    out = jnp.zeros(values.shape, F32)
    for d in range(NVAR):
        at = first + d
        out = jnp.where(
            lane // 8 == d + WEIGHT_AT // 8,
            jnp.broadcast_to(values[:, at : at + 1], values.shape),
            out,
        )
    return out


def outlet_lanes(row):
    return (1 - row) * (LANES - 1), (1 - row) * (LANES - 2) + row


def settle_kernel(
    bands_ref, f1_ref, src_ref, tau_ref, jac_ref, cell_ref, owner_ref,
    part_ref, pack_ref, ids_ref, seen_ref, node_ref, vs,
):
    row = lax.axis_index("row")
    outlet, inner = outlet_lanes(row)
    ghost = 6 - row
    tile = (CP, LANES)
    zero = jnp.zeros(tile, F32)
    lane = lane_ids(tile)
    fill_stencil(
        vs,
        lambda d, j: f1_ref[d, j],
        lambda d: zero,
        lambda d: zero,
        lambda d, j: zero,
        lambda d, j: zero,
        lambda d, j: zero,
        lambda d, j: zero,
    )
    for n in range(6):
        for j in range(CS):
            pack_ref[n, j] = zero

    def advance(c, carry):
        part_ref[c] = f1_ref[c] + tau_ref[...] * (src_ref[c] - image_of(jac_ref, vs, c))
        for n in range(6):
            point = n if n < 5 else ghost
            extra = 1 - row if n < 5 else 2 - 3 * row
            for j in range(CS):
                pack = pack_ref[n, j]
                for d in range(NVAR):
                    at = WEIGHT_AT + 8 * d + c
                    moved = pltpu.roll(jac_ref[point, c, d, j].astype(F32), at + extra, 1)
                    pack = jnp.where(lane == at, moved, pack)
                pack_ref[n, j] = pack
        return carry

    lax.fori_loop(0, NVAR, advance, 0)
    for j in range(CS):
        steps = [
            jnp.sum(jnp.where(lane == at, tau_ref[j], 0.0), axis=1, keepdims=True)
            for at in (outlet, inner)
        ]
        for n in range(6):
            pack_ref[n, j] = pack_ref[n, j] * steps[n // 5]
    square = (LANES, LANES)
    lines = ids_ref.shape[0] // 2
    line = row_ids((lines, LANES))
    first_cell = CS * (line // CP) + 2 * (line % 2)
    even_cell = (lane_ids((lines, LANES)) == first_cell).astype(F32).astype(BF16)
    for of_row in range(2):
        bands = bands_ref[of_row : of_row + 1].astype(F32)
        pair = jnp.where(
            row_ids(square) < LANES // 2,
            jnp.broadcast_to(bands, square),
            jnp.broadcast_to(pltpu.roll(bands, LANES - 1, 1), square),
        )
        ids_ref[lines * of_row : lines * (of_row + 1)] = lax.dot_general(
            even_cell, pair.astype(BF16), (((1,), (1,)), ((), ())), preferred_element_type=F32
        )
    cells = cell_ref[0, 0]
    for j in range(CS):
        here = row_ids(tile) + CP * j == cells // LANES
        for n, at in enumerate((outlet, inner)):
            seen_ref[n, j] = jnp.where(here & (cells % LANES == at), 1.0, 0.0).astype(F32)
    picked = (row_ids(square) == owner_ref[0, 0] % LANES).astype(F32).astype(BF16)
    for n in range(3):
        node_ref[:, LANES * n : LANES * (n + 1)] = picked


def settle_edges_kernel(
    part_ref, jac_ref, tau_ref, up_ref, down_ref, left_ref, right_ref, cell_ref,
    part2_ref, face_ref, sides,
):
    keep = inner_sides()
    tile = (CP, LANES)
    fill_sides(sides, left_ref, right_ref)

    def body(c, carry):
        lost = edge_terms(jac_ref, sides, up_ref, down_ref, keep, c)
        for j in range(CS):
            part2_ref[c, j] = part_ref[c, j] - tau_ref[j] * lost[j]
        return carry

    lax.fori_loop(0, NVAR, body, 0)
    cells = cell_ref[0, 0]
    square = (LANES, LANES)
    axial_pick = (row_ids(square) == cells % LANES).astype(F32).astype(BF16)
    picked = dot3(part2_ref[...].reshape(NVAR * CS * CP, LANES), axial_pick, ((1,), (0,)))
    here = row_ids((CS * CP, LANES)) == cells // LANES
    for c in range(NVAR):
        block = picked[c * CS * CP : (c + 1) * CS * CP]
        face_ref[c : c + 1] = jnp.sum(jnp.where(here, block, 0.0), axis=0, keepdims=True)


def cycle_kernel(
    bands_ref, part_ref, rec_ref, pack_ref, ids_ref, all_ref, up_ref, down_ref, left_ref, right_ref,
    seen_ref, node_ref, face_ref, owner_ref, weight_ref, out_hbm, dense_ref, field, sem,
):
    row = lax.axis_index("row")
    span = lax.axis_index("span")
    outlet, inner = outlet_lanes(row)
    keep = inner_sides()
    tile = (CP, LANES)
    lane, sub = lane_ids(tile), row_ids(tile)
    last_cell = bands_ref.shape[1] - 1
    wanted = [
        bands_ref[row, jnp.clip(span * CS - 1 + t, 0, last_cell)].astype(F32)
        for t in range(CS + 2)
    ]
    half = all_ref.shape[0] // 2
    zero = jnp.zeros(tile, F32)

    def body(i, sums):
        sums = list(sums)
        for n, of_row in enumerate((1 - row, row)):
            at = pl.multiple_of(of_row * half + i * CP, CP)
            ids, values = ids_ref[pl.ds(at, CP), :], all_ref[pl.ds(at, CP), :]
            for t, band in enumerate(wanted):
                k = (CS + 2) * n + t
                sums[k] = sums[k] + jnp.where(ids == band, values, 0.0)
        return tuple(sums)

    sums = lax.fori_loop(0, half // CP, body, (zero,) * (2 * CS + 4), unroll=8)

    def folded(parts):
        rows = [jnp.sum(x, axis=0, keepdims=True) for x in parts]
        whole = jnp.concatenate(rows + [rows[-1]] * (CP - len(rows)), axis=0)
        whole = whole + pltpu.roll(whole, 64, 1)
        return whole, jnp.broadcast_to(whole[:, COUNT_AT : COUNT_AT + 1], tile)

    other, other_count = folded(sums[: CS + 2])
    mine, my_count = folded(sums[CS + 2 :])
    spread0 = spread(other / other_count, 0)
    lost = weight_sum(other * spread(mine / my_count, 0))
    cycle1 = (other - pltpu.roll(lost, LANES - (WEIGHT_AT - FIRST_AT), 1)) / other_count
    spread1 = spread(cycle1, FIRST_AT)

    def shift_of(record, values):
        moved = weight_sum(record * values)
        return moved, spread(moved, WEIGHT_AT)

    own = [shift_of(rec_ref[j], spread0[j + 1 : j + 2]) for j in range(CS)]
    above = shift_of(up_ref[NVAR], spread0[:1])[1] * keep[0]
    below = shift_of(down_ref[NVAR], spread0[CS + 1 : CS + 2])[1] * keep[1]
    left = shift_of(left_ref[NVAR], spread0[1 : 1 + CS])[1]
    right = shift_of(right_ref[NVAR], spread0[1 : 1 + CS])[1]
    changes = []
    for j in range(CS):
        x = own[j][1]
        total = pack_ref[0, j] * x - rec_ref[j] * spread1[j + 1 : j + 2]
        total = total + pack_ref[1, j] * (own[j - 1][1] if j > 0 else above)
        total = total + pack_ref[2, j] * (own[j + 1][1] if j < CS - 1 else below)
        total = total + pack_ref[3, j] * jnp.where(
            sub == 0, jnp.broadcast_to(left[j : j + 1], tile), pltpu.roll(x, 1, 0)
        )
        total = total + pack_ref[4, j] * jnp.where(
            sub == CP - 1, jnp.broadcast_to(right[j : j + 1], tile), pltpu.roll(x, CP - 1, 0)
        )
        changes.append((weight_sum(total) - own[j][0], weight_sum(pack_ref[5, j] * x)))
    wide = [
        [
            [jnp.broadcast_to(x[:, WEIGHT_AT + c : WEIGHT_AT + c + 1], tile) for x in changes[j]]
            for j in range(CS)
        ]
        for c in range(NVAR)
    ]
    for c in range(NVAR):
        for j in range(CS):
            first, second = wide[c][j]
            moved = jnp.where(lane == outlet, first, jnp.where(lane == inner, second, 0.0))
            field[0, c, j] = part_ref[c, j] + moved
    write = pltpu.make_async_copy(field, out_hbm, sem)
    write.start()
    terms = [jnp.zeros((1, LANES), F32)] * 3
    for c in range(NVAR):
        seen = zero
        for j in range(CS):
            first, second = wide[c][j]
            seen = seen + (seen_ref[0, j] * first + seen_ref[1, j] * second)
        value = face_ref[c : c + 1] + jnp.sum(seen, axis=0, keepdims=True)
        for k in range(3):
            at = NVAR * k + c
            terms[k] = terms[k] + weight_ref[0, 0, 0, at : at + 1] * value
    shape = dense_ref.shape
    line = row_ids(shape)
    device = (line * 43691) >> 17
    here = device == owner_ref[0, 0] // LANES
    cycle_rows = (24, LANES)
    coord = row_ids(cycle_rows) % 3
    pieces = []
    for parts in zip(*(split3(x) for x in terms)):
        wide = [jnp.broadcast_to(x.astype(F32), cycle_rows) for x in parts]
        pattern = jnp.where(coord == 0, wide[0], jnp.where(coord == 1, wide[1], wide[2]))
        pattern = jnp.concatenate([pattern] * (shape[0] // 24), axis=0)
        pieces.append(jnp.where(here, pattern, 0.0).astype(BF16))
    dense_ref[...] = lax.dot_general(
        jnp.concatenate(pieces, axis=1),
        node_ref[...],
        (((1,), (1,)), ((), ())),
        preferred_element_type=F32,
    )
    write.wait()


VM = pl.BlockSpec(memory_space=pltpu.VMEM)
SM = pl.BlockSpec(memory_space=pltpu.SMEM)
PARAMS = pltpu.CompilerParams(vmem_limit_bytes=32 * 1024 * 1024)


HBM = pl.BlockSpec(memory_space=pltpu.HBM)


def in_hbm(x):
    return pltpu.with_memory_space_constraint(x, pltpu.HBM)


def call(kernel, name, outs, in_specs, scratch=(), cost=None, out_specs=None):
    outs = [out if isinstance(out[0], tuple) else (out, F32) for out in outs]
    return pl.pallas_call(
        kernel,
        out_shape=tuple(jax.ShapeDtypeStruct(shape, dtype) for shape, dtype in outs),
        in_specs=in_specs,
        out_specs=out_specs or (VM,) * len(outs),
        scratch_shapes=list(scratch),
        compiler_params=PARAMS,
        cost_estimate=cost,
        name=name,
    )


def shifted(value, axis, by):
    devices = lax.axis_size(axis)
    return lax.ppermute(value, axis, [(i, (i + by) % devices) for i in range(devices)])


def over_span(to_up, to_down):
    return shifted(to_down, "span", 1), shifted(to_up, "span", -1)


def over_pitch(to_left, to_right):
    return shifted(to_right, "pitch", 1), shifted(to_left, "pitch", -1)


def on_device(
    adjoint, source, pseudo_step, jac_blocks, band_map, face_cell, face_owner, face_weight
):
    rows, spans, pitches = (lax.axis_size(name) for name in ("row", "span", "pitch"))
    devices = rows * spans * pitches
    peers = spans * pitches
    block = (NVAR, CS, CP, LANES)
    edge = (NVAR, CP, LANES)
    side = (NVAR, CS, LANES)
    edges = call(
        edges_kernel,
        "edges",
        [edge, edge, side, side],
        in_specs=[HBM],
        scratch=[pltpu.SemaphoreType.DMA((4,))],
        cost=pl.CostEstimate(flops=2_000_000_000, bytes_accessed=30_000_000, transcendentals=0),
    )(in_hbm(adjoint))
    halo = over_span(*edges[:2]) + over_pitch(*edges[2:])
    jac, src, tau = jac_blocks[0], source[0], pseudo_step[0]
    part, record = call(
        interior_kernel,
        "interior",
        [block, (CS, CP, LANES)],
        in_specs=[VM] * 4,
        scratch=[pltpu.VMEM((7 * NVAR, CS, CP, LANES), F32)],
        cost=pl.CostEstimate(flops=9_000_000, bytes_accessed=3_000_000, transcendentals=0),
    )(adjoint[0], src, tau, jac)
    edge = (NVAR + 1, CP, LANES)
    side = (NVAR + 1, CS, LANES)
    first, message, full_record, *sends = call(
        edge_kernel,
        "edge_update",
        [block, (2 * devices, LANES), (CS, CP, LANES), edge, edge, side, side],
        in_specs=[VM] * 8,
        out_specs=(VM, HBM) + (VM,) * 5,
        scratch=[
            pltpu.VMEM((2 * NVAR, CS, CP, LANES), F32),
            pltpu.VMEM((2 * devices // 8, LANES), F32),
            pltpu.SemaphoreType.DMA((8,)),
        ],
    )(part, record, jac, tau, *halo)
    records = lax.all_to_all(
        message.reshape(devices, 1, 2 * LANES), ("row", "span", "pitch"), 0, 0
    ).reshape(2 * devices, LANES)
    halo = over_span(*sends[:2]) + over_pitch(*sends[2:])
    part, packs, ids, seen, picks = call(
        settle_kernel,
        "settle",
        [
            block, (6, CS, CP, LANES), ((2 * devices, LANES), F32), (2, CS, CP, LANES),
            ((LANES, 3 * LANES), BF16),
        ],
        in_specs=[VM] * 7,
        scratch=[pltpu.VMEM((7 * NVAR, CS, CP, LANES), F32)],
        cost=pl.CostEstimate(flops=9_000_000, bytes_accessed=3_000_000, transcendentals=0),
    )(band_map, first, src, tau, jac, face_cell, face_owner)
    part, faces = call(
        settle_edges_kernel,
        "settle_edges",
        [block, (CP, LANES)],
        in_specs=[VM] * 8,
        scratch=[pltpu.VMEM((2 * NVAR, CS, CP, LANES), F32)],
        cost=pl.CostEstimate(flops=3_000_000, bytes_accessed=2_000_000, transcendentals=0),
    )(part, jac, tau, *halo, face_cell)
    field, dense = call(
        cycle_kernel,
        "cycle_update",
        [(1,) + block, (3 * peers, LANES)],
        in_specs=[SM] + [VM] * 14,
        out_specs=(HBM, VM),
        scratch=[pltpu.VMEM((1,) + block, F32), pltpu.SemaphoreType.DMA],
    )(
        band_map, part, full_record, packs, ids, records, *halo, seen, picks, faces, face_owner,
        face_weight,
    )
    parts = lax.all_to_all(dense.reshape(peers, 1, 3 * LANES), ("span", "pitch"), 0, 0)
    nodes = jnp.sum(parts, axis=(0, 1)).reshape(1, 3, LANES)
    return field, nodes


def solution(mesh):
    in_specs = (
        P("row", None, "span", "pitch", None),
        P("row", None, "span", "pitch", None),
        P("row", "span", "pitch", None),
        P("row", None, None, None, "span", "pitch", None),
        P(),
        P("row", "span", "pitch", None),
        P("row", "span", "pitch", None),
        P("row", "span", "pitch", None, None),
    )
    out_specs = (P("row", None, "span", "pitch", None), P("row", None, ("span", "pitch")))
    return jax.shard_map(
        on_device, mesh=mesh, in_specs=in_specs, out_specs=out_specs, check_vma=False
    )
```

```python
import jax
import jax.numpy as jnp
from jax import lax
from jax.experimental import pallas as pl
from jax.experimental.pallas import tpu as pltpu
from jax.sharding import PartitionSpec as P

NVAR = 6
CS = 4
CP = 8
LANES = 128
F32 = jnp.float32
BF16 = jnp.bfloat16
FIRST_AT = 8
WEIGHT_AT = 16
COUNT_AT = 6
FAR_COPIES = 5


def lane_ids(shape):
    return lax.broadcasted_iota(jnp.int32, shape, len(shape) - 1)


def row_ids(shape):
    return lax.broadcasted_iota(jnp.int32, shape, len(shape) - 2)


def split3(x):
    hi = x.astype(BF16)
    rest = x - hi.astype(F32)
    mid = rest.astype(BF16)
    low = (rest - mid.astype(F32)).astype(BF16)
    return hi, mid, low


def dot3(x, onehot, dims):
    parts = [
        lax.dot_general(part, onehot, (dims, ((), ())), preferred_element_type=F32)
        for part in split3(x)
    ]
    return parts[0] + (parts[1] + parts[2])


def fill_stencil(vs, field, up, down, left, right, lower, upper):
    tile = (CP, LANES)
    lane, sub = lane_ids(tile), row_ids(tile)
    for d in range(NVAR):
        for j in range(CS):
            x = field(d, j)
            vs[d, j] = x
            vs[6 + d, j] = field(d, j - 1) if j > 0 else up(d)
            vs[12 + d, j] = field(d, j + 1) if j < CS - 1 else down(d)
            vs[18 + d, j] = jnp.where(
                sub == 0, jnp.broadcast_to(left(d, j), tile), pltpu.roll(x, 1, 0)
            )
            vs[24 + d, j] = jnp.where(
                sub == CP - 1, jnp.broadcast_to(right(d, j), tile), pltpu.roll(x, CP - 1, 0)
            )
            vs[30 + d, j] = jnp.where(lane == 0, lower(d, j), pltpu.roll(x, 1, 1))
            vs[36 + d, j] = jnp.where(lane == LANES - 1, upper(d, j), pltpu.roll(x, LANES - 1, 1))


def image_of(jac_ref, vs, c):
    acc = jnp.zeros((CS, CP, LANES), F32)
    for s in range(7):
        for d in range(NVAR):
            acc = acc + jac_ref[s, c, d].astype(F32) * vs[6 * s + d]
    return acc


def edges_kernel(adj_ref, up_ref, down_ref, left_ref, right_ref, sems):
    adj = adj_ref.at[0]
    copies = [
        pltpu.make_async_copy(adj.at[:, 0], up_ref, sems.at[0]),
        pltpu.make_async_copy(adj.at[:, CS - 1], down_ref, sems.at[1]),
        pltpu.make_async_copy(adj.at[:, :, 0], left_ref, sems.at[2]),
        pltpu.make_async_copy(adj.at[:, :, CP - 1], right_ref, sems.at[3]),
    ]
    for copy in copies:
        copy.start()
    for copy in copies:
        copy.wait()


def interior_kernel(adj_ref, src_ref, tau_ref, jac_ref, part_ref, rec_ref, vs):
    row = lax.axis_index("row")
    outlet = (1 - row) * (LANES - 1)
    ghost = 6 - row
    tile = (CP, LANES)
    zero = jnp.zeros(tile, F32)
    lane = lane_ids(tile)
    fill_stencil(
        vs,
        lambda d, j: adj_ref[d, j],
        lambda d: zero,
        lambda d: zero,
        lambda d, j: zero,
        lambda d, j: zero,
        lambda d, j: zero,
        lambda d, j: zero,
    )

    def advance(c, carry):
        weights, sums = (list(x) for x in carry)
        part_ref[c] = adj_ref[c] + tau_ref[...] * (src_ref[c] - image_of(jac_ref, vs, c))
        for j in range(CS):
            for d in range(NVAR):
                at = WEIGHT_AT + 8 * d + c
                moved = pltpu.roll(jac_ref[ghost, c, d, j].astype(F32), at + 1 - row, 1)
                weights[j] = jnp.where(lane == at, moved, weights[j])
            sums[j] = jnp.where(lane == c, pltpu.roll(adj_ref[c, j], c + 1 - row, 1), sums[j])
        return tuple(weights), tuple(sums)

    ones = jnp.where(lane == COUNT_AT, 1.0, 0.0).astype(F32)
    weights, sums = lax.fori_loop(0, NVAR, advance, ((zero,) * CS, (ones,) * CS))
    for j in range(CS):
        tau_out = jnp.sum(jnp.where(lane == outlet, tau_ref[j], 0.0), axis=1, keepdims=True)
        rec_ref[j] = sums[j] + weights[j] * tau_out


def inner_sides():
    span = lax.axis_index("span")
    return (
        jnp.where(span > 0, 1.0, 0.0).astype(F32),
        jnp.where(span < lax.axis_size("span") - 1, 1.0, 0.0).astype(F32),
    )


def fill_sides(sides, left_ref, right_ref):
    tile = (CP, LANES)
    sub = row_ids(tile)
    for d in range(NVAR):
        for j in range(CS):
            sides[d, j] = jnp.where(
                sub == 0, jnp.broadcast_to(left_ref[d, j : j + 1], tile), 0.0
            )
            sides[NVAR + d, j] = jnp.where(
                sub == CP - 1, jnp.broadcast_to(right_ref[d, j : j + 1], tile), 0.0
            )


def edge_terms(jac_ref, sides, up_ref, down_ref, keep, c):
    acc = jnp.zeros((CS, CP, LANES), F32)
    first = jnp.zeros((CP, LANES), F32)
    last = jnp.zeros((CP, LANES), F32)
    for d in range(NVAR):
        acc = acc + jac_ref[3, c, d].astype(F32) * sides[d]
        acc = acc + jac_ref[4, c, d].astype(F32) * sides[NVAR + d]
        first = first + jac_ref[1, c, d, 0].astype(F32) * up_ref[d]
        last = last + jac_ref[2, c, d, CS - 1].astype(F32) * down_ref[d]
    lost = [acc[j] for j in range(CS)]
    lost[0] = lost[0] + first * keep[0]
    lost[CS - 1] = lost[CS - 1] + last * keep[1]
    return lost


def edge_kernel(
    part_ref, rec_in, jac_ref, tau_ref, up_ref, down_ref, left_ref, right_ref,
    f1_ref, msg_ref, rec, to_up_ref, to_down_ref, to_left_ref, to_right_ref, sides,
):
    row = lax.axis_index("row")
    keep = inner_sides()
    tile = (CP, LANES)
    lane, sub = lane_ids(tile), row_ids(tile)
    fill_sides(sides, left_ref, right_ref)

    def body(c, sums):
        sums = list(sums)
        lost = edge_terms(jac_ref, sides, up_ref, down_ref, keep, c)
        at = FIRST_AT + c
        for j in range(CS):
            new = part_ref[c, j] - tau_ref[j] * lost[j]
            f1_ref[c, j] = new
            sums[j] = jnp.where(lane == at, pltpu.roll(new, at + 1 - row, 1), sums[j])
        return tuple(sums)

    sums = lax.fori_loop(0, NVAR, body, tuple(rec_in[j] for j in range(CS)))
    rows = []
    for j in range(CS):
        rec[j] = sums[j]
        rows.append(jnp.sum(sums[j], axis=0, keepdims=True))
    halves = [
        jnp.broadcast_to(rows[2 * h] + pltpu.roll(rows[2 * h + 1], 64, 1), tile) for h in range(2)
    ]
    packed = jnp.where(sub % 2 == 0, halves[0], halves[1])
    for i in range(msg_ref.shape[0] // CP):
        msg_ref[CP * i : CP * (i + 1)] = packed
    to_up_ref[0:NVAR] = f1_ref[:, 0]
    to_up_ref[NVAR] = rec[0]
    to_down_ref[0:NVAR] = f1_ref[:, CS - 1]
    to_down_ref[NVAR] = rec[CS - 1]
    for c in range(NVAR):
        to_left_ref[c] = f1_ref[c, :, 0, :]
        to_right_ref[c] = f1_ref[c, :, CP - 1, :]
    to_left_ref[NVAR] = rec[:, 0, :]
    to_right_ref[NVAR] = rec[:, CP - 1, :]


def weight_sum(x):
    moved = [pltpu.roll(x, LANES - 8 * d, 1) for d in range(1, NVAR)]
    return ((x + moved[0]) + (moved[1] + moved[2])) + (moved[3] + moved[4])


def spread(values, first):
    lane = lane_ids(values.shape)
    out = jnp.zeros(values.shape, F32)
    for d in range(NVAR):
        at = first + d
        out = jnp.where(
            lane // 8 == d + WEIGHT_AT // 8,
            jnp.broadcast_to(values[:, at : at + 1], values.shape),
            out,
        )
    return out


def outlet_lanes(row):
    return (1 - row) * (LANES - 1), (1 - row) * (LANES - 2) + row


def settle_kernel(
    bands_ref, f1_ref, src_ref, tau_ref, jac_ref, cell_ref, owner_ref,
    part_ref, pack_ref, ids_ref, seen_ref, node_ref, vs,
):
    row = lax.axis_index("row")
    outlet, inner = outlet_lanes(row)
    ghost = 6 - row
    tile = (CP, LANES)
    zero = jnp.zeros(tile, F32)
    lane = lane_ids(tile)
    fill_stencil(
        vs,
        lambda d, j: f1_ref[d, j],
        lambda d: zero,
        lambda d: zero,
        lambda d, j: zero,
        lambda d, j: zero,
        lambda d, j: zero,
        lambda d, j: zero,
    )
    for n in range(6):
        for j in range(CS):
            pack_ref[n, j] = zero

    def advance(c, carry):
        part_ref[c] = f1_ref[c] + tau_ref[...] * (src_ref[c] - image_of(jac_ref, vs, c))
        for n in range(6):
            point = n if n < 5 else ghost
            extra = 1 - row if n < 5 else 2 - 3 * row
            for j in range(CS):
                pack = pack_ref[n, j]
                for d in range(NVAR):
                    at = WEIGHT_AT + 8 * d + c
                    moved = pltpu.roll(jac_ref[point, c, d, j].astype(F32), at + extra, 1)
                    pack = jnp.where(lane == at, moved, pack)
                pack_ref[n, j] = pack
        return carry

    lax.fori_loop(0, NVAR, advance, 0)
    for j in range(CS):
        steps = [
            jnp.sum(jnp.where(lane == at, tau_ref[j], 0.0), axis=1, keepdims=True)
            for at in (outlet, inner)
        ]
        for n in range(6):
            pack_ref[n, j] = pack_ref[n, j] * steps[n // 5]
    square = (LANES, LANES)
    lines = ids_ref.shape[0] // 2
    even_cell = (lane_ids((lines, LANES)) == 2 * row_ids((lines, LANES))).astype(F32).astype(BF16)
    for of_row in range(2):
        bands = bands_ref[of_row : of_row + 1].astype(F32)
        pair = jnp.where(
            row_ids(square) < LANES // 2,
            jnp.broadcast_to(bands, square),
            jnp.broadcast_to(pltpu.roll(bands, LANES - 1, 1), square),
        )
        ids_ref[lines * of_row : lines * (of_row + 1)] = lax.dot_general(
            even_cell, pair.astype(BF16), (((1,), (1,)), ((), ())), preferred_element_type=F32
        )
    cells = cell_ref[0, 0]
    for j in range(CS):
        here = row_ids(tile) + CP * j == cells // LANES
        for n, at in enumerate((outlet, inner)):
            seen_ref[n, j] = jnp.where(here & (cells % LANES == at), 1.0, 0.0).astype(F32)
    picked = (row_ids(square) == owner_ref[0, 0] % LANES).astype(F32).astype(BF16)
    for n in range(3):
        node_ref[:, LANES * n : LANES * (n + 1)] = picked


def settle_edges_kernel(
    part_ref, jac_ref, tau_ref, up_ref, down_ref, left_ref, right_ref, cell_ref,
    part2_ref, face_ref, sides,
):
    keep = inner_sides()
    tile = (CP, LANES)
    fill_sides(sides, left_ref, right_ref)

    def body(c, carry):
        lost = edge_terms(jac_ref, sides, up_ref, down_ref, keep, c)
        for j in range(CS):
            part2_ref[c, j] = part_ref[c, j] - tau_ref[j] * lost[j]
        return carry

    lax.fori_loop(0, NVAR, body, 0)
    cells = cell_ref[0, 0]
    square = (LANES, LANES)
    axial_pick = (row_ids(square) == cells % LANES).astype(F32).astype(BF16)
    picked = dot3(part2_ref[...].reshape(NVAR * CS * CP, LANES), axial_pick, ((1,), (0,)))
    here = row_ids((CS * CP, LANES)) == cells // LANES
    for c in range(NVAR):
        block = picked[c * CS * CP : (c + 1) * CS * CP]
        face_ref[c : c + 1] = jnp.sum(jnp.where(here, block, 0.0), axis=0, keepdims=True)


def bands_kernel(
    bands_ref, ids_ref, all_ref, to_left_ref, to_right_ref, sum_ref, left_ref, right_ref
):
    row = lax.axis_index("row")
    span = lax.axis_index("span")
    tile = (CP, LANES)
    last_cell = bands_ref.shape[1] - 1
    wanted = [
        bands_ref[row, jnp.clip(span * CS - 1 + t, 0, last_cell)].astype(F32)
        for t in range(CS + 2)
    ]
    half = all_ref.shape[0] // 2

    def folded(of_row):
        sums = [jnp.zeros(tile, F32)] * (CS + 2)
        for i in range(half // CP):
            at = pl.multiple_of(of_row * half + i * CP, CP)
            ids, values = ids_ref[pl.ds(at, CP), :], all_ref[pl.ds(at, CP), :]
            sums = [x + jnp.where(ids == band, values, 0.0) for x, band in zip(sums, wanted)]
        rows = [jnp.sum(x, axis=0, keepdims=True) for x in sums]
        whole = jnp.concatenate(rows + [rows[-1]] * (CP - len(rows)), axis=0)
        return whole + pltpu.roll(whole, 64, 1)

    total = jnp.where(lane_ids(tile) < LANES // 2, folded(1 - row), folded(row))
    for n in range(FAR_COPIES):
        sum_ref[n] = total
    for out_ref, in_ref in ((left_ref, to_left_ref), (right_ref, to_right_ref)):
        out_ref[: NVAR + 1] = in_ref[...]
        out_ref[NVAR + 1] = total[:CS]
        out_ref[NVAR + 2] = total[CS:]


def cycle_kernel(
    part_ref, rec_ref, pack_ref, sum_ref, far_ref, up_ref, down_ref, left_ref, right_ref,
    seen_ref, node_ref, face_ref, owner_ref, weight_ref, out_hbm, dense_ref, field, sem,
):
    row = lax.axis_index("row")
    outlet, inner = outlet_lanes(row)
    keep = inner_sides()
    tile = (CP, LANES)
    lane, sub = lane_ids(tile), row_ids(tile)
    zero = jnp.zeros(tile, F32)
    sides = [
        jnp.concatenate([ref[NVAR + 1], ref[NVAR + 2]], axis=0) for ref in (left_ref, right_ref)
    ]
    other = (sum_ref[0] + far_ref[0]) + (sides[0] + sides[1])
    mine = pltpu.roll(other, LANES // 2, 1)
    other_count, my_count = (
        jnp.broadcast_to(x[:, COUNT_AT : COUNT_AT + 1], tile) for x in (other, mine)
    )
    spread0 = spread(other / other_count, 0)
    lost = weight_sum(other * spread(mine / my_count, 0))
    cycle1 = (other - pltpu.roll(lost, LANES - (WEIGHT_AT - FIRST_AT), 1)) / other_count
    spread1 = spread(cycle1, FIRST_AT)

    def shift_of(record, values):
        moved = weight_sum(record * values)
        return moved, spread(moved, WEIGHT_AT)

    own = [shift_of(rec_ref[j], spread0[j + 1 : j + 2]) for j in range(CS)]
    above = shift_of(up_ref[NVAR], spread0[:1])[1] * keep[0]
    below = shift_of(down_ref[NVAR], spread0[CS + 1 : CS + 2])[1] * keep[1]
    left = shift_of(left_ref[NVAR], spread0[1 : 1 + CS])[1]
    right = shift_of(right_ref[NVAR], spread0[1 : 1 + CS])[1]
    changes = []
    for j in range(CS):
        x = own[j][1]
        total = pack_ref[0, j] * x - rec_ref[j] * spread1[j + 1 : j + 2]
        total = total + pack_ref[1, j] * (own[j - 1][1] if j > 0 else above)
        total = total + pack_ref[2, j] * (own[j + 1][1] if j < CS - 1 else below)
        total = total + pack_ref[3, j] * jnp.where(
            sub == 0, jnp.broadcast_to(left[j : j + 1], tile), pltpu.roll(x, 1, 0)
        )
        total = total + pack_ref[4, j] * jnp.where(
            sub == CP - 1, jnp.broadcast_to(right[j : j + 1], tile), pltpu.roll(x, CP - 1, 0)
        )
        changes.append((weight_sum(total) - own[j][0], weight_sum(pack_ref[5, j] * x)))
    terms = [jnp.zeros((1, LANES), F32)] * 3
    for c in range(NVAR):
        at = WEIGHT_AT + c
        seen = zero
        for j in range(CS):
            first, second = (jnp.broadcast_to(x[:, at : at + 1], tile) for x in changes[j])
            moved = jnp.where(lane == outlet, first, jnp.where(lane == inner, second, 0.0))
            field[0, c, j] = part_ref[c, j] + moved
            seen = seen + (seen_ref[0, j] * first + seen_ref[1, j] * second)
        value = face_ref[c : c + 1] + jnp.sum(seen, axis=0, keepdims=True)
        for k in range(3):
            at = NVAR * k + c
            terms[k] = terms[k] + weight_ref[0, 0, 0, at : at + 1] * value
    write = pltpu.make_async_copy(field, out_hbm, sem)
    write.start()
    shape = dense_ref.shape
    line = row_ids(shape)
    device = (line * 43691) >> 17
    here = device == owner_ref[0, 0] // LANES
    cycle_rows = (24, LANES)
    coord = row_ids(cycle_rows) % 3
    pieces = []
    for parts in zip(*(split3(x) for x in terms)):
        wide = [jnp.broadcast_to(x.astype(F32), cycle_rows) for x in parts]
        pattern = jnp.where(coord == 0, wide[0], jnp.where(coord == 1, wide[1], wide[2]))
        pattern = jnp.concatenate([pattern] * (shape[0] // 24), axis=0)
        pieces.append(jnp.where(here, pattern, 0.0).astype(BF16))
    dense_ref[...] = lax.dot_general(
        jnp.concatenate(pieces, axis=1),
        node_ref[...],
        (((1,), (1,)), ((), ())),
        preferred_element_type=F32,
    )
    write.wait()


def third_kernel(parts_ref, out_ref):
    folded = jnp.sum(parts_ref[...].reshape(-1, 24, LANES), axis=0)
    coord = row_ids(folded.shape) % 3
    for k in range(3):
        out_ref[k] = jnp.sum(jnp.where(coord == k, folded, 0.0), axis=0, keepdims=True)


VM = pl.BlockSpec(memory_space=pltpu.VMEM)
SM = pl.BlockSpec(memory_space=pltpu.SMEM)
PARAMS = pltpu.CompilerParams(vmem_limit_bytes=32 * 1024 * 1024)


HBM = pl.BlockSpec(memory_space=pltpu.HBM)


def in_hbm(x):
    return pltpu.with_memory_space_constraint(x, pltpu.HBM)


def call(kernel, name, outs, in_specs, scratch=(), cost=None, out_specs=None):
    outs = [out if isinstance(out[0], tuple) else (out, F32) for out in outs]
    return pl.pallas_call(
        kernel,
        out_shape=tuple(jax.ShapeDtypeStruct(shape, dtype) for shape, dtype in outs),
        in_specs=in_specs,
        out_specs=out_specs or (VM,) * len(outs),
        scratch_shapes=list(scratch),
        compiler_params=PARAMS,
        cost_estimate=cost,
        name=name,
    )


def shifted(value, axis, by):
    devices = lax.axis_size(axis)
    return lax.ppermute(value, axis, [(i, (i + by) % devices) for i in range(devices)])


def over_span(to_up, to_down):
    return shifted(to_down, "span", 1), shifted(to_up, "span", -1)


def over_pitch(to_left, to_right):
    return shifted(to_right, "pitch", 1), shifted(to_left, "pitch", -1)


def on_device(
    adjoint, source, pseudo_step, jac_blocks, band_map, face_cell, face_owner, face_weight
):
    rows, spans, pitches = (lax.axis_size(name) for name in ("row", "span", "pitch"))
    groups = rows * spans
    peers = spans * pitches
    block = (NVAR, CS, CP, LANES)
    edge = (NVAR, CP, LANES)
    side = (NVAR, CS, LANES)
    edges = call(
        edges_kernel,
        "edges",
        [edge, edge, side, side],
        in_specs=[HBM],
        scratch=[pltpu.SemaphoreType.DMA((4,))],
        cost=pl.CostEstimate(flops=2_000_000_000, bytes_accessed=30_000_000, transcendentals=0),
    )(in_hbm(adjoint))
    halo = over_span(*edges[:2]) + over_pitch(*edges[2:])
    jac, src, tau = jac_blocks[0], source[0], pseudo_step[0]
    part, record = call(
        interior_kernel,
        "interior",
        [block, (CS, CP, LANES)],
        in_specs=[VM] * 4,
        scratch=[pltpu.VMEM((7 * NVAR, CS, CP, LANES), F32)],
        cost=pl.CostEstimate(flops=9_000_000, bytes_accessed=3_000_000, transcendentals=0),
    )(adjoint[0], src, tau, jac)
    edge = (NVAR + 1, CP, LANES)
    side = (NVAR + 1, CS, LANES)
    first, message, full_record, *sends = call(
        edge_kernel,
        "edge_update",
        [block, (2 * groups, LANES), (CS, CP, LANES), edge, edge, side, side],
        in_specs=[VM] * 8,
        scratch=[pltpu.VMEM((2 * NVAR, CS, CP, LANES), F32)],
    )(part, record, jac, tau, *halo)
    records = lax.all_to_all(
        message.reshape(groups, 1, 2 * LANES), ("row", "span"), 0, 0
    ).reshape(2 * groups, LANES)
    halo = over_span(*sends[:2])
    part, packs, ids, seen, picks = call(
        settle_kernel,
        "settle",
        [
            block, (6, CS, CP, LANES), ((2 * groups, LANES), F32), (2, CS, CP, LANES),
            ((LANES, 3 * LANES), BF16),
        ],
        in_specs=[VM] * 7,
        scratch=[pltpu.VMEM((7 * NVAR, CS, CP, LANES), F32)],
        cost=pl.CostEstimate(flops=9_000_000, bytes_accessed=3_000_000, transcendentals=0),
    )(band_map, first, src, tau, jac, face_cell, face_owner)
    tail = (NVAR + 3, CS, LANES)
    sums, *sides = call(
        bands_kernel, "band_sums", [(FAR_COPIES, CP, LANES), tail, tail], in_specs=[SM] + [VM] * 4
    )(band_map, ids, records, *sends[2:])
    halo = halo + over_pitch(*sides)
    far = shifted(sums, "pitch", 2)
    part, faces = call(
        settle_edges_kernel,
        "settle_edges",
        [block, (CP, LANES)],
        in_specs=[VM] * 8,
        scratch=[pltpu.VMEM((2 * NVAR, CS, CP, LANES), F32)],
        cost=pl.CostEstimate(flops=3_000_000, bytes_accessed=2_000_000, transcendentals=0),
    )(part, jac, tau, *halo, face_cell)
    field, dense = call(
        cycle_kernel,
        "cycle_update",
        [(1,) + block, (3 * peers, LANES)],
        in_specs=[VM] * 14,
        out_specs=(HBM, VM),
        scratch=[pltpu.VMEM((1,) + block, F32), pltpu.SemaphoreType.DMA],
    )(
        part, full_record, packs, sums, far, *halo, seen, picks, faces, face_owner, face_weight,
    )
    parts = lax.all_to_all(dense.reshape(peers, 1, 3 * LANES), ("span", "pitch"), 0, 0)
    (nodes,) = call(third_kernel, "node_sums", [(3, 1, LANES)], in_specs=[VM])(
        parts.reshape(3 * peers, LANES)
    )
    return field, nodes.transpose(1, 0, 2)


def solution(mesh):
    in_specs = (
        P("row", None, "span", "pitch", None),
        P("row", None, "span", "pitch", None),
        P("row", "span", "pitch", None),
        P("row", None, None, None, "span", "pitch", None),
        P(),
        P("row", "span", "pitch", None),
        P("row", "span", "pitch", None),
        P("row", "span", "pitch", None, None),
    )
    out_specs = (P("row", None, "span", "pitch", None), P("row", None, ("span", "pitch")))
    return jax.shard_map(
        on_device, mesh=mesh, in_specs=in_specs, out_specs=out_specs, check_vma=False
    )
```

```python
import jax
import jax.numpy as jnp
from jax import lax
from jax.experimental import pallas as pl
from jax.experimental.pallas import tpu as pltpu
from jax.sharding import PartitionSpec as P

NVAR = 6
CS = 4
CP = 8
LANES = 128
F32 = jnp.float32
BF16 = jnp.bfloat16
FIRST_AT = 8
WEIGHT_AT = 16
COUNT_AT = 6


def lane_ids(shape):
    return lax.broadcasted_iota(jnp.int32, shape, len(shape) - 1)


def row_ids(shape):
    return lax.broadcasted_iota(jnp.int32, shape, len(shape) - 2)


def split3(x):
    hi = x.astype(BF16)
    rest = x - hi.astype(F32)
    mid = rest.astype(BF16)
    low = (rest - mid.astype(F32)).astype(BF16)
    return hi, mid, low


def dot3(x, onehot):
    return jnp.dot(
        jnp.concatenate(split3(x), axis=1),
        jnp.concatenate([onehot] * 3, axis=0),
        preferred_element_type=F32,
    )


def fill_stencil(vs, field, up, down, left, right, lower, upper):
    tile = (CP, LANES)
    lane, sub = lane_ids(tile), row_ids(tile)
    for d in range(NVAR):
        for j in range(CS):
            x = field(d, j)
            vs[d, j] = x
            vs[6 + d, j] = field(d, j - 1) if j > 0 else up(d)
            vs[12 + d, j] = field(d, j + 1) if j < CS - 1 else down(d)
            vs[18 + d, j] = jnp.where(
                sub == 0, jnp.broadcast_to(left(d, j), tile), pltpu.roll(x, 1, 0)
            )
            vs[24 + d, j] = jnp.where(
                sub == CP - 1, jnp.broadcast_to(right(d, j), tile), pltpu.roll(x, CP - 1, 0)
            )
            vs[30 + d, j] = jnp.where(lane == 0, lower(d, j), pltpu.roll(x, 1, 1))
            vs[36 + d, j] = jnp.where(lane == LANES - 1, upper(d, j), pltpu.roll(x, LANES - 1, 1))


def image_of(jac_ref, vs, c):
    acc = jnp.zeros((CS, CP, LANES), F32)
    for s in range(7):
        for d in range(NVAR):
            acc = acc + jac_ref[s, c, d].astype(F32) * vs[6 * s + d]
    return acc


def edges_kernel(adj_ref, up_ref, down_ref, left_ref, right_ref, sems):
    adj = adj_ref.at[0]
    copies = [
        pltpu.make_async_copy(adj.at[:, 0], up_ref, sems.at[0]),
        pltpu.make_async_copy(adj.at[:, CS - 1], down_ref, sems.at[1]),
        pltpu.make_async_copy(adj.at[:, :, 0], left_ref, sems.at[2]),
        pltpu.make_async_copy(adj.at[:, :, CP - 1], right_ref, sems.at[3]),
    ]
    for copy in copies:
        copy.start()
    for copy in copies:
        copy.wait()


def interior_kernel(adj_ref, src_ref, tau_ref, jac_ref, part_ref, rec_ref, vs):
    row = lax.axis_index("row")
    outlet = (1 - row) * (LANES - 1)
    ghost = 6 - row
    tile = (CP, LANES)
    zero = jnp.zeros(tile, F32)
    lane = lane_ids(tile)
    fill_stencil(
        vs,
        lambda d, j: adj_ref[d, j],
        lambda d: zero,
        lambda d: zero,
        lambda d, j: zero,
        lambda d, j: zero,
        lambda d, j: zero,
        lambda d, j: zero,
    )

    def advance(c, carry):
        weights, sums = (list(x) for x in carry)
        part_ref[c] = adj_ref[c] + tau_ref[...] * (src_ref[c] - image_of(jac_ref, vs, c))
        for j in range(CS):
            for d in range(NVAR):
                at = WEIGHT_AT + 8 * d + c
                moved = pltpu.roll(jac_ref[ghost, c, d, j].astype(F32), at + 1 - row, 1)
                weights[j] = jnp.where(lane == at, moved, weights[j])
            sums[j] = jnp.where(lane == c, pltpu.roll(adj_ref[c, j], c + 1 - row, 1), sums[j])
        return tuple(weights), tuple(sums)

    ones = jnp.where(lane == COUNT_AT, 1.0, 0.0).astype(F32)
    weights, sums = lax.fori_loop(0, NVAR, advance, ((zero,) * CS, (ones,) * CS))
    for j in range(CS):
        tau_out = jnp.sum(jnp.where(lane == outlet, tau_ref[j], 0.0), axis=1, keepdims=True)
        rec_ref[j] = sums[j] + weights[j] * tau_out


def inner_sides():
    span = lax.axis_index("span")
    return (
        jnp.where(span > 0, 1.0, 0.0).astype(F32),
        jnp.where(span < lax.axis_size("span") - 1, 1.0, 0.0).astype(F32),
    )


def fill_sides(sides, left_ref, right_ref):
    tile = (CP, LANES)
    sub = row_ids(tile)
    for d in range(NVAR):
        for j in range(CS):
            sides[d, j] = jnp.where(
                sub == 0, jnp.broadcast_to(left_ref[d, j : j + 1], tile), 0.0
            )
            sides[NVAR + d, j] = jnp.where(
                sub == CP - 1, jnp.broadcast_to(right_ref[d, j : j + 1], tile), 0.0
            )


def edge_terms(jac_ref, sides, up_ref, down_ref, keep, c):
    acc = jnp.zeros((CS, CP, LANES), F32)
    first = jnp.zeros((CP, LANES), F32)
    last = jnp.zeros((CP, LANES), F32)
    for d in range(NVAR):
        acc = acc + jac_ref[3, c, d].astype(F32) * sides[d]
        acc = acc + jac_ref[4, c, d].astype(F32) * sides[NVAR + d]
        first = first + jac_ref[1, c, d, 0].astype(F32) * up_ref[d]
        last = last + jac_ref[2, c, d, CS - 1].astype(F32) * down_ref[d]
    lost = [acc[j] for j in range(CS)]
    lost[0] = lost[0] + first * keep[0]
    lost[CS - 1] = lost[CS - 1] + last * keep[1]
    return lost


def edge_kernel(
    part_ref, rec_in, jac_ref, tau_ref, up_ref, down_ref, left_ref, right_ref,
    f1_ref, msg_hbm, rec, to_up_ref, to_down_ref, to_left_ref, to_right_ref, sides, copies, sems,
):
    row = lax.axis_index("row")
    keep = inner_sides()
    tile = (CP, LANES)
    lane, sub = lane_ids(tile), row_ids(tile)
    fill_sides(sides, left_ref, right_ref)

    def body(c, sums):
        sums = list(sums)
        lost = edge_terms(jac_ref, sides, up_ref, down_ref, keep, c)
        at = FIRST_AT + c
        for j in range(CS):
            new = part_ref[c, j] - tau_ref[j] * lost[j]
            f1_ref[c, j] = new
            sums[j] = jnp.where(lane == at, pltpu.roll(new, at + 1 - row, 1), sums[j])
        return tuple(sums)

    sums = lax.fori_loop(0, NVAR, body, tuple(rec_in[j] for j in range(CS)))
    rows = []
    for j in range(CS):
        rec[j] = sums[j]
        rows.append(jnp.sum(sums[j], axis=0, keepdims=True))
    halves = [
        jnp.broadcast_to(rows[2 * h] + pltpu.roll(rows[2 * h + 1], 64, 1), tile) for h in range(2)
    ]
    packed = jnp.where(sub % 2 == 0, halves[0], halves[1])
    lines = copies.shape[0]
    for i in range(lines // CP):
        copies[CP * i : CP * (i + 1)] = packed
    writes = [
        pltpu.make_async_copy(copies, msg_hbm.at[pl.ds(lines * i, lines)], sems.at[i])
        for i in range(msg_hbm.shape[0] // lines)
    ]
    for write in writes:
        write.start()
    to_up_ref[0:NVAR] = f1_ref[:, 0]
    to_up_ref[NVAR] = rec[0]
    to_down_ref[0:NVAR] = f1_ref[:, CS - 1]
    to_down_ref[NVAR] = rec[CS - 1]
    for c in range(NVAR):
        to_left_ref[c] = f1_ref[c, :, 0, :]
        to_right_ref[c] = f1_ref[c, :, CP - 1, :]
    to_left_ref[NVAR] = rec[:, 0, :]
    to_right_ref[NVAR] = rec[:, CP - 1, :]
    for write in writes:
        write.wait()


def weight_sum(x):
    moved = [pltpu.roll(x, LANES - 8 * d, 1) for d in range(1, NVAR)]
    return ((x + moved[0]) + (moved[1] + moved[2])) + (moved[3] + moved[4])


def spread(values, first):
    lane = lane_ids(values.shape)
    out = jnp.zeros(values.shape, F32)
    for d in range(NVAR):
        at = first + d
        out = jnp.where(
            lane // 8 == d + WEIGHT_AT // 8,
            jnp.broadcast_to(values[:, at : at + 1], values.shape),
            out,
        )
    return out


def outlet_lanes(row):
    return (1 - row) * (LANES - 1), (1 - row) * (LANES - 2) + row


def settle_kernel(
    bands_ref, f1_ref, src_ref, tau_ref, jac_ref, cell_ref, owner_ref,
    part_ref, pack_ref, ids_ref, seen_ref, node_ref, vs,
):
    row = lax.axis_index("row")
    outlet, inner = outlet_lanes(row)
    ghost = 6 - row
    tile = (CP, LANES)
    zero = jnp.zeros(tile, F32)
    lane = lane_ids(tile)
    fill_stencil(
        vs,
        lambda d, j: f1_ref[d, j],
        lambda d: zero,
        lambda d: zero,
        lambda d, j: zero,
        lambda d, j: zero,
        lambda d, j: zero,
        lambda d, j: zero,
    )
    for n in range(6):
        for j in range(CS):
            pack_ref[n, j] = zero

    def advance(c, carry):
        part_ref[c] = f1_ref[c] + tau_ref[...] * (src_ref[c] - image_of(jac_ref, vs, c))
        for n in range(6):
            point = n if n < 5 else ghost
            extra = 1 - row if n < 5 else 2 - 3 * row
            for j in range(CS):
                pack = pack_ref[n, j]
                for d in range(NVAR):
                    at = WEIGHT_AT + 8 * d + c
                    moved = pltpu.roll(jac_ref[point, c, d, j].astype(F32), at + extra, 1)
                    pack = jnp.where(lane == at, moved, pack)
                pack_ref[n, j] = pack
        return carry

    lax.fori_loop(0, NVAR, advance, 0)
    for j in range(CS):
        steps = [
            jnp.sum(jnp.where(lane == at, tau_ref[j], 0.0), axis=1, keepdims=True)
            for at in (outlet, inner)
        ]
        for n in range(6):
            pack_ref[n, j] = pack_ref[n, j] * steps[n // 5]
    square = (LANES, LANES)
    lines = ids_ref.shape[0] // 2
    line = row_ids((lines, LANES))
    first_cell = CS * (line // CP) + 2 * (line % 2)
    even_cell = (lane_ids((lines, LANES)) == first_cell).astype(F32).astype(BF16)
    for of_row in range(2):
        bands = bands_ref[of_row : of_row + 1].astype(F32)
        pair = jnp.where(
            row_ids(square) < LANES // 2,
            jnp.broadcast_to(bands, square),
            jnp.broadcast_to(pltpu.roll(bands, LANES - 1, 1), square),
        )
        ids_ref[lines * of_row : lines * (of_row + 1)] = lax.dot_general(
            even_cell, pair.astype(BF16), (((1,), (1,)), ((), ())), preferred_element_type=F32
        )
    cells = cell_ref[0, 0]
    for j in range(CS):
        here = row_ids(tile) + CP * j == cells // LANES
        for n, at in enumerate((outlet, inner)):
            seen_ref[n, j] = jnp.where(here & (cells % LANES == at), 1.0, 0.0).astype(F32)
    picked = (row_ids(square) == owner_ref[0, 0] % LANES).astype(F32).astype(BF16)
    for n in range(3):
        node_ref[:, LANES * n : LANES * (n + 1)] = picked


def settle_edges_kernel(
    part_ref, jac_ref, tau_ref, up_ref, down_ref, left_ref, right_ref, cell_ref,
    part2_ref, face_ref, sides,
):
    keep = inner_sides()
    tile = (CP, LANES)
    fill_sides(sides, left_ref, right_ref)

    def body(c, carry):
        lost = edge_terms(jac_ref, sides, up_ref, down_ref, keep, c)
        for j in range(CS):
            part2_ref[c, j] = part_ref[c, j] - tau_ref[j] * lost[j]
        return carry

    lax.fori_loop(0, NVAR, body, 0)
    cells = cell_ref[0, 0]
    square = (LANES, LANES)
    axial_pick = (row_ids(square) == cells % LANES).astype(F32).astype(BF16)
    picked = dot3(part2_ref[...].reshape(NVAR * CS * CP, LANES), axial_pick)
    here = row_ids((CS * CP, LANES)) == cells // LANES
    for c in range(NVAR):
        block = picked[c * CS * CP : (c + 1) * CS * CP]
        face_ref[c : c + 1] = jnp.sum(jnp.where(here, block, 0.0), axis=0, keepdims=True)


def cycle_kernel(
    bands_ref, part_ref, rec_ref, pack_ref, ids_ref, all_ref, up_ref, down_ref, left_ref, right_ref,
    seen_ref, node_ref, face_ref, owner_ref, weight_ref, out_hbm, dense_ref, field, sem,
):
    row = lax.axis_index("row")
    span = lax.axis_index("span")
    outlet, inner = outlet_lanes(row)
    keep = inner_sides()
    tile = (CP, LANES)
    lane, sub = lane_ids(tile), row_ids(tile)
    last_cell = bands_ref.shape[1] - 1
    wanted = [
        bands_ref[row, jnp.clip(span * CS - 1 + t, 0, last_cell)].astype(F32)
        for t in range(CS + 2)
    ]
    half = all_ref.shape[0] // 2
    zero = jnp.zeros(tile, F32)

    def body(i, sums):
        sums = list(sums)
        for n, of_row in enumerate((1 - row, row)):
            at = pl.multiple_of(of_row * half + i * CP, CP)
            ids, values = ids_ref[pl.ds(at, CP), :], all_ref[pl.ds(at, CP), :]
            for t, band in enumerate(wanted):
                k = (CS + 2) * n + t
                sums[k] = sums[k] + jnp.where(ids == band, values, 0.0)
        return tuple(sums)

    sums = lax.fori_loop(0, half // CP, body, (zero,) * (2 * CS + 4), unroll=8)

    def folded(parts):
        rows = [jnp.sum(x, axis=0, keepdims=True) for x in parts]
        whole = jnp.concatenate(rows + [rows[-1]] * (CP - len(rows)), axis=0)
        whole = whole + pltpu.roll(whole, 64, 1)
        return whole, jnp.broadcast_to(whole[:, COUNT_AT : COUNT_AT + 1], tile)

    other, other_count = folded(sums[: CS + 2])
    mine, my_count = folded(sums[CS + 2 :])
    spread0 = spread(other / other_count, 0)
    lost = weight_sum(other * spread(mine / my_count, 0))
    cycle1 = (other - pltpu.roll(lost, LANES - (WEIGHT_AT - FIRST_AT), 1)) / other_count
    spread1 = spread(cycle1, FIRST_AT)

    def shift_of(record, values):
        moved = weight_sum(record * values)
        return moved, spread(moved, WEIGHT_AT)

    own = [shift_of(rec_ref[j], spread0[j + 1 : j + 2]) for j in range(CS)]
    above = shift_of(up_ref[NVAR], spread0[:1])[1] * keep[0]
    below = shift_of(down_ref[NVAR], spread0[CS + 1 : CS + 2])[1] * keep[1]
    left = shift_of(left_ref[NVAR], spread0[1 : 1 + CS])[1]
    right = shift_of(right_ref[NVAR], spread0[1 : 1 + CS])[1]
    changes = []
    for j in range(CS):
        x = own[j][1]
        total = pack_ref[0, j] * x - rec_ref[j] * spread1[j + 1 : j + 2]
        total = total + pack_ref[1, j] * (own[j - 1][1] if j > 0 else above)
        total = total + pack_ref[2, j] * (own[j + 1][1] if j < CS - 1 else below)
        total = total + pack_ref[3, j] * jnp.where(
            sub == 0, jnp.broadcast_to(left[j : j + 1], tile), pltpu.roll(x, 1, 0)
        )
        total = total + pack_ref[4, j] * jnp.where(
            sub == CP - 1, jnp.broadcast_to(right[j : j + 1], tile), pltpu.roll(x, CP - 1, 0)
        )
        changes.append((weight_sum(total) - own[j][0], weight_sum(pack_ref[5, j] * x)))
    wide = [
        [
            [jnp.broadcast_to(x[:, WEIGHT_AT + c : WEIGHT_AT + c + 1], tile) for x in changes[j]]
            for j in range(CS)
        ]
        for c in range(NVAR)
    ]
    for c in range(NVAR):
        for j in range(CS):
            first, second = wide[c][j]
            moved = jnp.where(lane == outlet, first, jnp.where(lane == inner, second, 0.0))
            field[0, c, j] = part_ref[c, j] + moved
    write = pltpu.make_async_copy(field, out_hbm, sem)
    write.start()
    terms = [jnp.zeros((1, LANES), F32)] * 3
    for c in range(NVAR):
        seen = zero
        for j in range(CS):
            first, second = wide[c][j]
            seen = seen + (seen_ref[0, j] * first + seen_ref[1, j] * second)
        value = face_ref[c : c + 1] + jnp.sum(seen, axis=0, keepdims=True)
        for k in range(3):
            at = NVAR * k + c
            terms[k] = terms[k] + weight_ref[0, 0, 0, at : at + 1] * value
    shape = dense_ref.shape
    line = row_ids(shape)
    device = (line * 43691) >> 17
    here = device == owner_ref[0, 0] // LANES
    cycle_rows = (24, LANES)
    coord = row_ids(cycle_rows) % 3
    pieces = []
    for parts in zip(*(split3(x) for x in terms)):
        wide = [jnp.broadcast_to(x.astype(F32), cycle_rows) for x in parts]
        pattern = jnp.where(coord == 0, wide[0], jnp.where(coord == 1, wide[1], wide[2]))
        pattern = jnp.concatenate([pattern] * (shape[0] // 24), axis=0)
        pieces.append(jnp.where(here, pattern, 0.0).astype(BF16))
    dense_ref[...] = lax.dot_general(
        jnp.concatenate(pieces, axis=1),
        node_ref[...],
        (((1,), (1,)), ((), ())),
        preferred_element_type=F32,
    )
    write.wait()


def third_kernel(parts_ref, out_ref):
    folded = jnp.sum(parts_ref[...].reshape(-1, 24, LANES), axis=0)
    coord = row_ids(folded.shape) % 3
    for k in range(3):
        out_ref[k] = jnp.sum(jnp.where(coord == k, folded, 0.0), axis=0, keepdims=True)


VM = pl.BlockSpec(memory_space=pltpu.VMEM)
SM = pl.BlockSpec(memory_space=pltpu.SMEM)
PARAMS = pltpu.CompilerParams(vmem_limit_bytes=32 * 1024 * 1024)


HBM = pl.BlockSpec(memory_space=pltpu.HBM)


def in_hbm(x):
    return pltpu.with_memory_space_constraint(x, pltpu.HBM)


def call(kernel, name, outs, in_specs, scratch=(), cost=None, out_specs=None):
    outs = [out if isinstance(out[0], tuple) else (out, F32) for out in outs]
    return pl.pallas_call(
        kernel,
        out_shape=tuple(jax.ShapeDtypeStruct(shape, dtype) for shape, dtype in outs),
        in_specs=in_specs,
        out_specs=out_specs or (VM,) * len(outs),
        scratch_shapes=list(scratch),
        compiler_params=PARAMS,
        cost_estimate=cost,
        name=name,
    )


def shifted(value, axis, by):
    devices = lax.axis_size(axis)
    return lax.ppermute(value, axis, [(i, (i + by) % devices) for i in range(devices)])


def over_span(to_up, to_down):
    return shifted(to_down, "span", 1), shifted(to_up, "span", -1)


def over_pitch(to_left, to_right):
    return shifted(to_right, "pitch", 1), shifted(to_left, "pitch", -1)


def on_device(
    adjoint, source, pseudo_step, jac_blocks, band_map, face_cell, face_owner, face_weight
):
    rows, spans, pitches = (lax.axis_size(name) for name in ("row", "span", "pitch"))
    devices = rows * spans * pitches
    peers = spans * pitches
    block = (NVAR, CS, CP, LANES)
    edge = (NVAR, CP, LANES)
    side = (NVAR, CS, LANES)
    edges = call(
        edges_kernel,
        "edges",
        [edge, edge, side, side],
        in_specs=[HBM],
        scratch=[pltpu.SemaphoreType.DMA((4,))],
        cost=pl.CostEstimate(flops=2_000_000_000, bytes_accessed=30_000_000, transcendentals=0),
    )(in_hbm(adjoint))
    halo = over_span(*edges[:2]) + over_pitch(*edges[2:])
    jac, src, tau = jac_blocks[0], source[0], pseudo_step[0]
    part, record = call(
        interior_kernel,
        "interior",
        [block, (CS, CP, LANES)],
        in_specs=[VM] * 4,
        scratch=[pltpu.VMEM((7 * NVAR, CS, CP, LANES), F32)],
        cost=pl.CostEstimate(flops=9_000_000, bytes_accessed=3_000_000, transcendentals=0),
    )(adjoint[0], src, tau, jac)
    edge = (NVAR + 1, CP, LANES)
    side = (NVAR + 1, CS, LANES)
    first, message, full_record, *sends = call(
        edge_kernel,
        "edge_update",
        [block, (2 * devices, LANES), (CS, CP, LANES), edge, edge, side, side],
        in_specs=[VM] * 8,
        out_specs=(VM, HBM) + (VM,) * 5,
        scratch=[
            pltpu.VMEM((2 * NVAR, CS, CP, LANES), F32),
            pltpu.VMEM((2 * devices // 8, LANES), F32),
            pltpu.SemaphoreType.DMA((8,)),
        ],
    )(part, record, jac, tau, *halo)
    records = lax.all_to_all(
        message.reshape(devices, 1, 2 * LANES), ("row", "span", "pitch"), 0, 0
    ).reshape(2 * devices, LANES)
    halo = over_span(*sends[:2]) + over_pitch(*sends[2:])
    part, packs, ids, seen, picks = call(
        settle_kernel,
        "settle",
        [
            block, (6, CS, CP, LANES), ((2 * devices, LANES), F32), (2, CS, CP, LANES),
            ((LANES, 3 * LANES), BF16),
        ],
        in_specs=[VM] * 7,
        scratch=[pltpu.VMEM((7 * NVAR, CS, CP, LANES), F32)],
        cost=pl.CostEstimate(flops=9_000_000, bytes_accessed=3_000_000, transcendentals=0),
    )(band_map, first, src, tau, jac, face_cell, face_owner)
    part, faces = call(
        settle_edges_kernel,
        "settle_edges",
        [block, (CP, LANES)],
        in_specs=[VM] * 8,
        scratch=[pltpu.VMEM((2 * NVAR, CS, CP, LANES), F32)],
        cost=pl.CostEstimate(flops=3_000_000, bytes_accessed=2_000_000, transcendentals=0),
    )(part, jac, tau, *halo, face_cell)
    field, dense = call(
        cycle_kernel,
        "cycle_update",
        [(1,) + block, (3 * peers, LANES)],
        in_specs=[SM] + [VM] * 14,
        out_specs=(HBM, VM),
        scratch=[pltpu.VMEM((1,) + block, F32), pltpu.SemaphoreType.DMA],
    )(
        band_map, part, full_record, packs, ids, records, *halo, seen, picks, faces, face_owner,
        face_weight,
    )
    parts = lax.all_to_all(dense.reshape(peers, 1, 3 * LANES), ("span", "pitch"), 0, 0)
    (nodes,) = call(third_kernel, "node_sums", [(3, 1, LANES)], in_specs=[VM])(
        parts.reshape(3 * peers, LANES)
    )
    return field, nodes.transpose(1, 0, 2)


def solution(mesh):
    in_specs = (
        P("row", None, "span", "pitch", None),
        P("row", None, "span", "pitch", None),
        P("row", "span", "pitch", None),
        P("row", None, None, None, "span", "pitch", None),
        P(),
        P("row", "span", "pitch", None),
        P("row", "span", "pitch", None),
        P("row", "span", "pitch", None, None),
    )
    out_specs = (P("row", None, "span", "pitch", None), P("row", None, ("span", "pitch")))
    return jax.shard_map(
        on_device, mesh=mesh, in_specs=in_specs, out_specs=out_specs, check_vma=False
    )
```

```python
import jax
import jax.numpy as jnp
from jax import lax
from jax.experimental import pallas as pl
from jax.experimental.pallas import tpu as pltpu
from jax.sharding import PartitionSpec as P

NVAR = 6
CS = 4
CP = 8
LANES = 128
F32 = jnp.float32
BF16 = jnp.bfloat16
FIRST_AT = 8
WEIGHT_AT = 16
COUNT_AT = 6


def lane_ids(shape):
    return lax.broadcasted_iota(jnp.int32, shape, len(shape) - 1)


def row_ids(shape):
    return lax.broadcasted_iota(jnp.int32, shape, len(shape) - 2)


def split3(x):
    hi = x.astype(BF16)
    rest = x - hi.astype(F32)
    mid = rest.astype(BF16)
    low = (rest - mid.astype(F32)).astype(BF16)
    return hi, mid, low


def dot3(x, onehot, dims):
    parts = [
        lax.dot_general(part, onehot, (dims, ((), ())), preferred_element_type=F32)
        for part in split3(x)
    ]
    return parts[0] + (parts[1] + parts[2])


def fill_stencil(vs, field, up, down, left, right, lower, upper):
    tile = (CP, LANES)
    lane, sub = lane_ids(tile), row_ids(tile)
    for d in range(NVAR):
        for j in range(CS):
            x = field(d, j)
            vs[d, j] = x
            vs[6 + d, j] = field(d, j - 1) if j > 0 else up(d)
            vs[12 + d, j] = field(d, j + 1) if j < CS - 1 else down(d)
            vs[18 + d, j] = jnp.where(
                sub == 0, jnp.broadcast_to(left(d, j), tile), pltpu.roll(x, 1, 0)
            )
            vs[24 + d, j] = jnp.where(
                sub == CP - 1, jnp.broadcast_to(right(d, j), tile), pltpu.roll(x, CP - 1, 0)
            )
            vs[30 + d, j] = jnp.where(lane == 0, lower(d, j), pltpu.roll(x, 1, 1))
            vs[36 + d, j] = jnp.where(lane == LANES - 1, upper(d, j), pltpu.roll(x, LANES - 1, 1))


def image_of(jac_ref, vs, c):
    acc = jnp.zeros((CS, CP, LANES), F32)
    for s in range(7):
        for d in range(NVAR):
            acc = acc + jac_ref[s, c, d].astype(F32) * vs[6 * s + d]
    return acc


def edges_kernel(adj_ref, up_ref, down_ref, left_ref, right_ref, sems):
    adj = adj_ref.at[0]
    copies = [
        pltpu.make_async_copy(adj.at[:, 0], up_ref, sems.at[0]),
        pltpu.make_async_copy(adj.at[:, CS - 1], down_ref, sems.at[1]),
        pltpu.make_async_copy(adj.at[:, :, 0], left_ref, sems.at[2]),
        pltpu.make_async_copy(adj.at[:, :, CP - 1], right_ref, sems.at[3]),
    ]
    for copy in copies:
        copy.start()
    for copy in copies:
        copy.wait()


def interior_kernel(adj_ref, src_ref, tau_ref, jac_ref, part_ref, rec_ref, vs):
    row = lax.axis_index("row")
    outlet = (1 - row) * (LANES - 1)
    ghost = 6 - row
    tile = (CP, LANES)
    zero = jnp.zeros(tile, F32)
    lane = lane_ids(tile)
    fill_stencil(
        vs,
        lambda d, j: adj_ref[d, j],
        lambda d: zero,
        lambda d: zero,
        lambda d, j: zero,
        lambda d, j: zero,
        lambda d, j: zero,
        lambda d, j: zero,
    )

    def advance(c, carry):
        weights, sums = (list(x) for x in carry)
        part_ref[c] = adj_ref[c] + tau_ref[...] * (src_ref[c] - image_of(jac_ref, vs, c))
        for j in range(CS):
            for d in range(NVAR):
                at = WEIGHT_AT + 8 * d + c
                moved = pltpu.roll(jac_ref[ghost, c, d, j].astype(F32), at + 1 - row, 1)
                weights[j] = jnp.where(lane == at, moved, weights[j])
            sums[j] = jnp.where(lane == c, pltpu.roll(adj_ref[c, j], c + 1 - row, 1), sums[j])
        return tuple(weights), tuple(sums)

    ones = jnp.where(lane == COUNT_AT, 1.0, 0.0).astype(F32)
    weights, sums = lax.fori_loop(0, NVAR, advance, ((zero,) * CS, (ones,) * CS))
    for j in range(CS):
        tau_out = jnp.sum(jnp.where(lane == outlet, tau_ref[j], 0.0), axis=1, keepdims=True)
        rec_ref[j] = sums[j] + weights[j] * tau_out


def inner_sides():
    span = lax.axis_index("span")
    return (
        jnp.where(span > 0, 1.0, 0.0).astype(F32),
        jnp.where(span < lax.axis_size("span") - 1, 1.0, 0.0).astype(F32),
    )


def fill_sides(sides, left_ref, right_ref):
    tile = (CP, LANES)
    sub = row_ids(tile)
    for d in range(NVAR):
        for j in range(CS):
            sides[d, j] = jnp.where(
                sub == 0, jnp.broadcast_to(left_ref[d, j : j + 1], tile), 0.0
            )
            sides[NVAR + d, j] = jnp.where(
                sub == CP - 1, jnp.broadcast_to(right_ref[d, j : j + 1], tile), 0.0
            )


def edge_terms(jac_ref, sides, up_ref, down_ref, keep, c):
    acc = jnp.zeros((CS, CP, LANES), F32)
    first = jnp.zeros((CP, LANES), F32)
    last = jnp.zeros((CP, LANES), F32)
    for d in range(NVAR):
        acc = acc + jac_ref[3, c, d].astype(F32) * sides[d]
        acc = acc + jac_ref[4, c, d].astype(F32) * sides[NVAR + d]
        first = first + jac_ref[1, c, d, 0].astype(F32) * up_ref[d]
        last = last + jac_ref[2, c, d, CS - 1].astype(F32) * down_ref[d]
    lost = [acc[j] for j in range(CS)]
    lost[0] = lost[0] + first * keep[0]
    lost[CS - 1] = lost[CS - 1] + last * keep[1]
    return lost


def edge_kernel(
    part_ref, rec_in, jac_ref, tau_ref, up_ref, down_ref, left_ref, right_ref,
    f1_ref, msg_hbm, rec, to_up_ref, to_down_ref, to_left_ref, to_right_ref, sides, copies, sems,
):
    row = lax.axis_index("row")
    keep = inner_sides()
    tile = (CP, LANES)
    lane, sub = lane_ids(tile), row_ids(tile)
    fill_sides(sides, left_ref, right_ref)

    def body(c, sums):
        sums = list(sums)
        lost = edge_terms(jac_ref, sides, up_ref, down_ref, keep, c)
        at = FIRST_AT + c
        for j in range(CS):
            new = part_ref[c, j] - tau_ref[j] * lost[j]
            f1_ref[c, j] = new
            sums[j] = jnp.where(lane == at, pltpu.roll(new, at + 1 - row, 1), sums[j])
        return tuple(sums)

    sums = lax.fori_loop(0, NVAR, body, tuple(rec_in[j] for j in range(CS)), unroll=True)
    rows = []
    for j in range(CS):
        rec[j] = sums[j]
        rows.append(jnp.sum(sums[j], axis=0, keepdims=True))
    halves = [
        jnp.broadcast_to(rows[2 * h] + pltpu.roll(rows[2 * h + 1], 64, 1), tile) for h in range(2)
    ]
    packed = jnp.where(sub % 2 == 0, halves[0], halves[1])
    lines = copies.shape[0]
    for i in range(lines // CP):
        copies[CP * i : CP * (i + 1)] = packed
    writes = [
        pltpu.make_async_copy(copies, msg_hbm.at[pl.ds(lines * i, lines)], sems.at[i])
        for i in range(msg_hbm.shape[0] // lines)
    ]
    for write in writes:
        write.start()
    to_up_ref[0:NVAR] = f1_ref[:, 0]
    to_up_ref[NVAR] = rec[0]
    to_down_ref[0:NVAR] = f1_ref[:, CS - 1]
    to_down_ref[NVAR] = rec[CS - 1]
    for c in range(NVAR):
        to_left_ref[c] = f1_ref[c, :, 0, :]
        to_right_ref[c] = f1_ref[c, :, CP - 1, :]
    to_left_ref[NVAR] = rec[:, 0, :]
    to_right_ref[NVAR] = rec[:, CP - 1, :]
    for write in writes:
        write.wait()


def weight_sum(x):
    moved = [pltpu.roll(x, LANES - 8 * d, 1) for d in range(1, NVAR)]
    return ((x + moved[0]) + (moved[1] + moved[2])) + (moved[3] + moved[4])


def spread(values, first):
    lane = lane_ids(values.shape)
    out = jnp.zeros(values.shape, F32)
    for d in range(NVAR):
        at = first + d
        out = jnp.where(
            lane // 8 == d + WEIGHT_AT // 8,
            jnp.broadcast_to(values[:, at : at + 1], values.shape),
            out,
        )
    return out


def outlet_lanes(row):
    return (1 - row) * (LANES - 1), (1 - row) * (LANES - 2) + row


def settle_kernel(
    bands_ref, f1_ref, src_ref, tau_ref, jac_ref, cell_ref, owner_ref,
    part_ref, pack_ref, ids_ref, seen_ref, node_ref, vs,
):
    row = lax.axis_index("row")
    outlet, inner = outlet_lanes(row)
    ghost = 6 - row
    tile = (CP, LANES)
    zero = jnp.zeros(tile, F32)
    lane = lane_ids(tile)
    fill_stencil(
        vs,
        lambda d, j: f1_ref[d, j],
        lambda d: zero,
        lambda d: zero,
        lambda d, j: zero,
        lambda d, j: zero,
        lambda d, j: zero,
        lambda d, j: zero,
    )
    for n in range(6):
        for j in range(CS):
            pack_ref[n, j] = zero

    def advance(c, carry):
        part_ref[c] = f1_ref[c] + tau_ref[...] * (src_ref[c] - image_of(jac_ref, vs, c))
        for n in range(6):
            point = n if n < 5 else ghost
            extra = 1 - row if n < 5 else 2 - 3 * row
            for j in range(CS):
                pack = pack_ref[n, j]
                for d in range(NVAR):
                    at = WEIGHT_AT + 8 * d + c
                    moved = pltpu.roll(jac_ref[point, c, d, j].astype(F32), at + extra, 1)
                    pack = jnp.where(lane == at, moved, pack)
                pack_ref[n, j] = pack
        return carry

    lax.fori_loop(0, NVAR, advance, 0)
    for j in range(CS):
        steps = [
            jnp.sum(jnp.where(lane == at, tau_ref[j], 0.0), axis=1, keepdims=True)
            for at in (outlet, inner)
        ]
        for n in range(6):
            pack_ref[n, j] = pack_ref[n, j] * steps[n // 5]
    square = (LANES, LANES)
    lines = ids_ref.shape[0] // 2
    line = row_ids((lines, LANES))
    first_cell = CS * (line // CP) + 2 * (line % 2)
    even_cell = (lane_ids((lines, LANES)) == first_cell).astype(F32).astype(BF16)
    for of_row in range(2):
        bands = bands_ref[of_row : of_row + 1].astype(F32)
        pair = jnp.where(
            row_ids(square) < LANES // 2,
            jnp.broadcast_to(bands, square),
            jnp.broadcast_to(pltpu.roll(bands, LANES - 1, 1), square),
        )
        ids_ref[lines * of_row : lines * (of_row + 1)] = lax.dot_general(
            even_cell, pair.astype(BF16), (((1,), (1,)), ((), ())), preferred_element_type=F32
        )
    cells = cell_ref[0, 0]
    for j in range(CS):
        here = row_ids(tile) + CP * j == cells // LANES
        for n, at in enumerate((outlet, inner)):
            seen_ref[n, j] = jnp.where(here & (cells % LANES == at), 1.0, 0.0).astype(F32)
    picked = (row_ids(square) == owner_ref[0, 0] % LANES).astype(F32).astype(BF16)
    for n in range(3):
        node_ref[:, LANES * n : LANES * (n + 1)] = picked


def settle_edges_kernel(
    part_ref, jac_ref, tau_ref, up_ref, down_ref, left_ref, right_ref, cell_ref,
    part2_ref, face_ref, sides,
):
    keep = inner_sides()
    tile = (CP, LANES)
    fill_sides(sides, left_ref, right_ref)

    def body(c, carry):
        lost = edge_terms(jac_ref, sides, up_ref, down_ref, keep, c)
        for j in range(CS):
            part2_ref[c, j] = part_ref[c, j] - tau_ref[j] * lost[j]
        return carry

    lax.fori_loop(0, NVAR, body, 0, unroll=True)
    cells = cell_ref[0, 0]
    square = (LANES, LANES)
    axial_pick = (row_ids(square) == cells % LANES).astype(F32).astype(BF16)
    picked = dot3(part2_ref[...].reshape(NVAR * CS * CP, LANES), axial_pick, ((1,), (0,)))
    here = row_ids((CS * CP, LANES)) == cells // LANES
    for c in range(NVAR):
        block = picked[c * CS * CP : (c + 1) * CS * CP]
        face_ref[c : c + 1] = jnp.sum(jnp.where(here, block, 0.0), axis=0, keepdims=True)


def cycle_kernel(
    bands_ref, part_ref, rec_ref, pack_ref, ids_ref, all_ref, up_ref, down_ref, left_ref, right_ref,
    seen_ref, node_ref, face_ref, owner_ref, weight_ref, out_hbm, dense_ref, field, sem,
):
    row = lax.axis_index("row")
    span = lax.axis_index("span")
    outlet, inner = outlet_lanes(row)
    keep = inner_sides()
    tile = (CP, LANES)
    lane, sub = lane_ids(tile), row_ids(tile)
    last_cell = bands_ref.shape[1] - 1
    wanted = [
        bands_ref[row, jnp.clip(span * CS - 1 + t, 0, last_cell)].astype(F32)
        for t in range(CS + 2)
    ]
    half = all_ref.shape[0] // 2
    zero = jnp.zeros(tile, F32)

    def body(i, sums):
        sums = list(sums)
        for n, of_row in enumerate((1 - row, row)):
            at = pl.multiple_of(of_row * half + i * CP, CP)
            ids, values = ids_ref[pl.ds(at, CP), :], all_ref[pl.ds(at, CP), :]
            for t, band in enumerate(wanted):
                k = (CS + 2) * n + t
                sums[k] = sums[k] + jnp.where(ids == band, values, 0.0)
        return tuple(sums)

    sums = lax.fori_loop(0, half // CP, body, (zero,) * (2 * CS + 4), unroll=8)

    def folded(parts):
        rows = [jnp.sum(x, axis=0, keepdims=True) for x in parts]
        whole = jnp.concatenate(rows + [rows[-1]] * (CP - len(rows)), axis=0)
        whole = whole + pltpu.roll(whole, 64, 1)
        return whole, jnp.broadcast_to(whole[:, COUNT_AT : COUNT_AT + 1], tile)

    other, other_count = folded(sums[: CS + 2])
    mine, my_count = folded(sums[CS + 2 :])
    spread0 = spread(other / other_count, 0)
    lost = weight_sum(other * spread(mine / my_count, 0))
    cycle1 = (other - pltpu.roll(lost, LANES - (WEIGHT_AT - FIRST_AT), 1)) / other_count
    spread1 = spread(cycle1, FIRST_AT)

    def shift_of(record, values):
        moved = weight_sum(record * values)
        return moved, spread(moved, WEIGHT_AT)

    own = [shift_of(rec_ref[j], spread0[j + 1 : j + 2]) for j in range(CS)]
    above = shift_of(up_ref[NVAR], spread0[:1])[1] * keep[0]
    below = shift_of(down_ref[NVAR], spread0[CS + 1 : CS + 2])[1] * keep[1]
    left = shift_of(left_ref[NVAR], spread0[1 : 1 + CS])[1]
    right = shift_of(right_ref[NVAR], spread0[1 : 1 + CS])[1]
    changes = []
    for j in range(CS):
        x = own[j][1]
        total = pack_ref[0, j] * x - rec_ref[j] * spread1[j + 1 : j + 2]
        total = total + pack_ref[1, j] * (own[j - 1][1] if j > 0 else above)
        total = total + pack_ref[2, j] * (own[j + 1][1] if j < CS - 1 else below)
        total = total + pack_ref[3, j] * jnp.where(
            sub == 0, jnp.broadcast_to(left[j : j + 1], tile), pltpu.roll(x, 1, 0)
        )
        total = total + pack_ref[4, j] * jnp.where(
            sub == CP - 1, jnp.broadcast_to(right[j : j + 1], tile), pltpu.roll(x, CP - 1, 0)
        )
        changes.append((weight_sum(total) - own[j][0], weight_sum(pack_ref[5, j] * x)))
    wide = [
        [
            [jnp.broadcast_to(x[:, WEIGHT_AT + c : WEIGHT_AT + c + 1], tile) for x in changes[j]]
            for j in range(CS)
        ]
        for c in range(NVAR)
    ]
    for c in range(NVAR):
        for j in range(CS):
            first, second = wide[c][j]
            moved = jnp.where(lane == outlet, first, jnp.where(lane == inner, second, 0.0))
            field[0, c, j] = part_ref[c, j] + moved
    write = pltpu.make_async_copy(field, out_hbm, sem)
    write.start()
    terms = [jnp.zeros((1, LANES), F32)] * 3
    for c in range(NVAR):
        seen = zero
        for j in range(CS):
            first, second = wide[c][j]
            seen = seen + (seen_ref[0, j] * first + seen_ref[1, j] * second)
        value = face_ref[c : c + 1] + jnp.sum(seen, axis=0, keepdims=True)
        for k in range(3):
            at = NVAR * k + c
            terms[k] = terms[k] + weight_ref[0, 0, 0, at : at + 1] * value
    shape = dense_ref.shape
    line = row_ids(shape)
    device = (line * 43691) >> 17
    here = device == owner_ref[0, 0] // LANES
    cycle_rows = (24, LANES)
    coord = row_ids(cycle_rows) % 3
    pieces = []
    for parts in zip(*(split3(x) for x in terms)):
        wide = [jnp.broadcast_to(x.astype(F32), cycle_rows) for x in parts]
        pattern = jnp.where(coord == 0, wide[0], jnp.where(coord == 1, wide[1], wide[2]))
        pattern = jnp.concatenate([pattern] * (shape[0] // 24), axis=0)
        pieces.append(jnp.where(here, pattern, 0.0).astype(BF16))
    dense_ref[...] = lax.dot_general(
        jnp.concatenate(pieces, axis=1),
        node_ref[...],
        (((1,), (1,)), ((), ())),
        preferred_element_type=F32,
    )
    write.wait()


VM = pl.BlockSpec(memory_space=pltpu.VMEM)
SM = pl.BlockSpec(memory_space=pltpu.SMEM)
PARAMS = pltpu.CompilerParams(vmem_limit_bytes=32 * 1024 * 1024)


HBM = pl.BlockSpec(memory_space=pltpu.HBM)


def in_hbm(x):
    return pltpu.with_memory_space_constraint(x, pltpu.HBM)


def call(kernel, name, outs, in_specs, scratch=(), cost=None, out_specs=None):
    outs = [out if isinstance(out[0], tuple) else (out, F32) for out in outs]
    return pl.pallas_call(
        kernel,
        out_shape=tuple(jax.ShapeDtypeStruct(shape, dtype) for shape, dtype in outs),
        in_specs=in_specs,
        out_specs=out_specs or (VM,) * len(outs),
        scratch_shapes=list(scratch),
        compiler_params=PARAMS,
        cost_estimate=cost,
        name=name,
    )


def shifted(value, axis, by):
    devices = lax.axis_size(axis)
    return lax.ppermute(value, axis, [(i, (i + by) % devices) for i in range(devices)])


def over_span(to_up, to_down):
    return shifted(to_down, "span", 1), shifted(to_up, "span", -1)


def over_pitch(to_left, to_right):
    return shifted(to_right, "pitch", 1), shifted(to_left, "pitch", -1)


def on_device(
    adjoint, source, pseudo_step, jac_blocks, band_map, face_cell, face_owner, face_weight
):
    rows, spans, pitches = (lax.axis_size(name) for name in ("row", "span", "pitch"))
    devices = rows * spans * pitches
    peers = spans * pitches
    block = (NVAR, CS, CP, LANES)
    edge = (NVAR, CP, LANES)
    side = (NVAR, CS, LANES)
    edges = call(
        edges_kernel,
        "edges",
        [edge, edge, side, side],
        in_specs=[HBM],
        scratch=[pltpu.SemaphoreType.DMA((4,))],
        cost=pl.CostEstimate(flops=2_000_000_000, bytes_accessed=30_000_000, transcendentals=0),
    )(in_hbm(adjoint))
    halo = over_span(*edges[:2]) + over_pitch(*edges[2:])
    jac, src, tau = jac_blocks[0], source[0], pseudo_step[0]
    part, record = call(
        interior_kernel,
        "interior",
        [block, (CS, CP, LANES)],
        in_specs=[VM] * 4,
        scratch=[pltpu.VMEM((7 * NVAR, CS, CP, LANES), F32)],
        cost=pl.CostEstimate(flops=9_000_000, bytes_accessed=3_000_000, transcendentals=0),
    )(adjoint[0], src, tau, jac)
    edge = (NVAR + 1, CP, LANES)
    side = (NVAR + 1, CS, LANES)
    first, message, full_record, *sends = call(
        edge_kernel,
        "edge_update",
        [block, (2 * devices, LANES), (CS, CP, LANES), edge, edge, side, side],
        in_specs=[VM] * 8,
        out_specs=(VM, HBM) + (VM,) * 5,
        scratch=[
            pltpu.VMEM((2 * NVAR, CS, CP, LANES), F32),
            pltpu.VMEM((2 * devices // 8, LANES), F32),
            pltpu.SemaphoreType.DMA((8,)),
        ],
    )(part, record, jac, tau, *halo)
    records = lax.all_to_all(
        message.reshape(devices, 1, 2 * LANES), ("row", "span", "pitch"), 0, 0
    ).reshape(2 * devices, LANES)
    halo = over_span(*sends[:2]) + over_pitch(*sends[2:])
    part, packs, ids, seen, picks = call(
        settle_kernel,
        "settle",
        [
            block, (6, CS, CP, LANES), ((2 * devices, LANES), F32), (2, CS, CP, LANES),
            ((LANES, 3 * LANES), BF16),
        ],
        in_specs=[VM] * 7,
        scratch=[pltpu.VMEM((7 * NVAR, CS, CP, LANES), F32)],
        cost=pl.CostEstimate(flops=9_000_000, bytes_accessed=3_000_000, transcendentals=0),
    )(band_map, first, src, tau, jac, face_cell, face_owner)
    part, faces = call(
        settle_edges_kernel,
        "settle_edges",
        [block, (CP, LANES)],
        in_specs=[VM] * 8,
        scratch=[pltpu.VMEM((2 * NVAR, CS, CP, LANES), F32)],
        cost=pl.CostEstimate(flops=3_000_000, bytes_accessed=2_000_000, transcendentals=0),
    )(part, jac, tau, *halo, face_cell)
    field, dense = call(
        cycle_kernel,
        "cycle_update",
        [(1,) + block, (3 * peers, LANES)],
        in_specs=[SM] + [VM] * 14,
        out_specs=(HBM, VM),
        scratch=[pltpu.VMEM((1,) + block, F32), pltpu.SemaphoreType.DMA],
    )(
        band_map, part, full_record, packs, ids, records, *halo, seen, picks, faces, face_owner,
        face_weight,
    )
    parts = lax.all_to_all(dense.reshape(peers, 1, 3 * LANES), ("span", "pitch"), 0, 0)
    nodes = jnp.sum(parts, axis=(0, 1)).reshape(1, 3, LANES)
    return field, nodes


def solution(mesh):
    in_specs = (
        P("row", None, "span", "pitch", None),
        P("row", None, "span", "pitch", None),
        P("row", "span", "pitch", None),
        P("row", None, None, None, "span", "pitch", None),
        P(),
        P("row", "span", "pitch", None),
        P("row", "span", "pitch", None),
        P("row", "span", "pitch", None, None),
    )
    out_specs = (P("row", None, "span", "pitch", None), P("row", None, ("span", "pitch")))
    return jax.shard_map(
        on_device, mesh=mesh, in_specs=in_specs, out_specs=out_specs, check_vma=False
    )
```
